512 devices in a mesh: dom: 64 (over z_lo, y, core), col: 8 (over x, z_hi).
Axes of the slice: x: 4, y: 8, z: 8 (z_hi: 2, z_lo: 4; z = z_hi * 4 + z_lo), core: 2. Of those that a mesh axis runs over, the one named last changes fastest.
Arguments:
- features: bfloat16 [128, 16384], P('col', 'dom'), may hold values from -6 to 6
- cached_embed: bfloat16 [128, 16384], P('col'), may hold values from -6 to 6
- staleness: int32 [64], replicated, may hold values from 0 to 15, as said below
- node_counts: int32 [64], replicated, may hold values from 64 to 256, as said below
- neighbours: int32 [16, 16384], P(None, 'dom'), may hold values from 0 to 16383, as said below
- degrees: int32 [16384], P('dom'), may hold values from 1 to 16
- w_self: bfloat16 [128, 256], P('col'), may hold values from -0.5 to 0.5
- w_nbr: bfloat16 [128, 256], P('col'), may hold values from -0.5 to 0.5
- sage_bias: float32 [256], P('col'), may hold values from -3 to 3
- cotangent: bfloat16 [256, 16384], P('col', 'dom'), may hold values from -6 to 6
Outputs:
- activation: bfloat16 [256, 16384], P('col', 'dom')
- grad_feat: bfloat16 [128, 16384], P('col', 'dom')
- grad_self: float32 [128, 256], P('col')
- grad_nbr: float32 [128, 256], P('col')
- grad_bias: float32 [256], P('col')
The draws below stay inside these ranges and needn't reach their ends.
Inputs may be any that keep to these rules, and one draw needn't show every extreme that they name: Exactly 16 partitions have staleness of 8 or more. `node_counts`: some partition has all 256 node slots live. `neighbours`: every neighbour slot names a live node slot; about half lie in the node's own partition.
All inputs are finite; a program needn't handle non-finite values.
Results may differ from the reference program's by a relative error of at most 0.015.
Values may be sent and summed in bfloat16 or wider, within the bound.
A program may use at most 64 MiB of HBM per device.

```python
import jax
import jax.numpy as jnp

F = 128
H = 256
K = 16
LIMIT = 8
P_DEV = 256
PARTS_SIZE = 64
NODES = 16384
FRESH = 16


def graph_counts(key):
    count_key = jax.random.fold_in(key, 11)
    values = jax.random.randint(jax.random.fold_in(count_key, 1), (PARTS_SIZE,), P_DEV // 4, P_DEV + 1)
    chosen = jax.random.randint(jax.random.fold_in(count_key, 2), (), 0, PARTS_SIZE)
    return values.at[chosen].set(P_DEV).astype(jnp.int32)


def draw_node_counts(key, part):
    return graph_counts(key)


def draw_neighbours(key, part):
    counts = graph_counts(key)
    nbr_key = jax.random.fold_in(key, 23)
    own_part = (jnp.arange(NODES, dtype=jnp.int32) // P_DEV)[:, None] + jnp.zeros((NODES, K), jnp.int32)
    other_part = jax.random.randint(jax.random.fold_in(nbr_key, 1), (NODES, K), 0, PARTS_SIZE)
    picker = jax.random.randint(jax.random.fold_in(nbr_key, 2), (NODES, K), 0, 2)
    source_part = jnp.where(picker == 1, own_part, other_part)
    offset = jax.random.randint(jax.random.fold_in(nbr_key, 3), (NODES, K), 0, 1 << 20) % counts[source_part]
    return (source_part * P_DEV + offset).astype(jnp.int32).T


def draw_degrees(key, part):
    values = jax.random.randint(jax.random.fold_in(key, 37), (NODES,), 1, K + 1)
    return values.at[0].set(K).astype(jnp.int32)


def draw_staleness(key, part):
    order_key = jax.random.fold_in(key, 41)
    shuffled = jax.random.permutation(jax.random.fold_in(order_key, 1), PARTS_SIZE)
    rank_pos = jnp.arange(PARTS_SIZE, dtype=jnp.int32)
    low_vals = jax.random.randint(jax.random.fold_in(order_key, 2), (PARTS_SIZE,), 0, LIMIT)
    values = jnp.where(rank_pos < FRESH, low_vals + LIMIT, low_vals)
    values = jnp.where(rank_pos == 0, 2 * LIMIT - 1, values)
    values = jnp.where(rank_pos == FRESH, 0, values)
    return jnp.zeros((PARTS_SIZE,), jnp.int32).at[shuffled].set(values.astype(jnp.int32))


def block_scale(key, dims, split, smallest, largest):
    def one(position, blocks):
        steps = jax.random.uniform(jax.random.fold_in(jax.random.fold_in(key, 6), position), (blocks,), jnp.float32, smallest / len(split), largest / len(split))
        return jnp.repeat(jnp.exp(steps), dims[position] // blocks).reshape((-1,) + (1,) * (len(dims) - position - 1))

    gain = one(*split[0])
    for cut in split[1:]:
        gain = gain * one(*cut)
    return gain


def noise(stream_key, shape, deviation, most, shards=(), kind=jnp.bfloat16):
    values = jax.random.normal(stream_key, shape, jnp.float32) * deviation
    if len(shards) > 0:
        values = block_scale(stream_key, shape, shards, -0.22, 0.18) * values
    return jnp.clip(values, min=-most, max=most).astype(kind)


def setup_inputs(seed: int = 0) -> dict:
    streams_of = jax.random.split(jax.random.key(seed), 11)
    features = noise(streams_of[0], (F, NODES), 1.0, 6.0, ((0, 8), (1, 64)))
    cached_embed = noise(streams_of[1], (F, NODES), 1.0, 6.0, ((0, 8),))
    staleness = draw_staleness(jax.random.fold_in(streams_of[10], 71), 0)
    node_counts = draw_node_counts(jax.random.fold_in(streams_of[10], 71), 0)
    neighbours = draw_neighbours(jax.random.fold_in(streams_of[10], 71), 0)
    degrees = draw_degrees(jax.random.fold_in(streams_of[10], 71), 0)
    w_self = noise(streams_of[6], (F, H), F ** -0.5, 0.5, ((0, 8),))
    w_nbr = noise(streams_of[7], (F, H), F ** -0.5, 0.5, ((0, 8),))
    sage_bias = noise(streams_of[8], (H,), 0.5, 3.0, ((0, 8),), jnp.float32)
    cotangent = noise(streams_of[9], (H, NODES), 1.0, 6.0, ((0, 8), (1, 64)))
    return dict(features=features, cached_embed=cached_embed, staleness=staleness, node_counts=node_counts, neighbours=neighbours, degrees=degrees, w_self=w_self, w_nbr=w_nbr, sage_bias=sage_bias, cotangent=cotangent)


def reference(features, cached_embed, staleness, node_counts, neighbours, degrees, w_self, w_nbr, sage_bias, cotangent):
    feat_rows = features.T
    cache_rows = cached_embed.T
    nbr_rows = neighbours.T
    cot_rows = cotangent.T
    node_slot = jnp.arange(NODES, dtype=jnp.int32)
    part_of = node_slot // P_DEV
    fresh_flag = (staleness >= LIMIT).astype(jnp.int32)
    fresh_rows = fresh_flag[part_of]
    sources = jnp.where(fresh_rows[:, None] == 1, feat_rows, cache_rows)
    live_rows = (node_slot % P_DEV < node_counts[part_of]).astype(jnp.float32)
    slot_index = jnp.arange(K, dtype=jnp.int32)
    used = (slot_index[None, :] < degrees[:, None]).astype(jnp.float32)
    weights = used * (live_rows / degrees.astype(jnp.float32))[:, None]
    gathered = sources[nbr_rows].astype(jnp.float32)
    aggregated = jnp.einsum("nk,nkc->nc", weights, gathered).astype(jnp.bfloat16)
    pre_act = (jnp.dot(feat_rows, w_self, preferred_element_type=jnp.float32)
               + jnp.dot(aggregated, w_nbr, preferred_element_type=jnp.float32) + sage_bias)
    sigmoid = 1.0 / (1.0 + jnp.exp(-pre_act))
    activation = (live_rows[:, None] * pre_act * sigmoid).astype(jnp.bfloat16)
    grad_pre = (live_rows[:, None] * cot_rows.astype(jnp.float32) * sigmoid * (1.0 + pre_act * (1.0 - sigmoid))).astype(jnp.bfloat16)
    grad_bias = jnp.sum(grad_pre.astype(jnp.float32), axis=0)
    grad_self = jnp.dot(feat_rows.T, grad_pre, preferred_element_type=jnp.float32)
    grad_nbr = jnp.dot(aggregated.T, grad_pre, preferred_element_type=jnp.float32)
    grad_agg = jnp.dot(grad_pre, w_nbr.T, preferred_element_type=jnp.float32).astype(jnp.bfloat16)
    own_term = jnp.dot(grad_pre, w_self.T, preferred_element_type=jnp.float32)
    spread = weights[:, :, None] * grad_agg.astype(jnp.float32)[:, None, :]
    back = jnp.zeros((NODES, F), jnp.float32).at[nbr_rows.reshape(-1)].add(spread.reshape(-1, F))
    grad_feat = (own_term + fresh_rows.astype(jnp.float32)[:, None] * back).astype(jnp.bfloat16)
    return activation.T, grad_feat.T, grad_self, grad_nbr, grad_bias
```

```python
import functools

import jax
import jax.numpy as jnp
from jax import lax
from jax.experimental import pallas as pl
from jax.experimental.pallas import tpu as pltpu
from jax.sharding import PartitionSpec as P

LIMIT = 8
MESH = pl.DeviceIdType.MESH


def left_product(weight, data):
    return lax.dot_general(
        weight, data, (((0,), (0,)), ((), ())), preferred_element_type=jnp.float32
    )


def right_product(data, grads):
    return lax.dot_general(
        data, grads, (((1,), (1,)), ((), ())), preferred_element_type=jnp.float32
    )


def exchange_kernel(axis, size, stride, bcast, reduce, x_ref, y_ref, buf, send_sem, recv_sem):
    me = lax.axis_index(axis)
    pos = lax.rem(me // stride, size)

    def member(j):
        return me + (j - pos) * stride

    barrier = pltpu.get_barrier_semaphore()

    def greet(k, carry):
        j = lax.rem(pos + k, size)
        pl.semaphore_signal(barrier, 1, device_id={axis: member(j)}, device_id_type=MESH)
        return carry

    lax.fori_loop(1, size, greet, 0)
    pl.semaphore_wait(barrier, size - 1)

    def desc(j, slot):
        src = x_ref if bcast else x_ref.at[j]
        return pltpu.make_async_remote_copy(
            src_ref=src,
            dst_ref=buf.at[slot],
            send_sem=send_sem.at[j],
            recv_sem=recv_sem.at[slot],
            device_id={axis: member(j)},
            device_id_type=MESH,
        )

    def send(k, carry):
        j = lax.rem(pos + k, size)
        desc(j, pos).start()
        return carry

    lax.fori_loop(1, size, send, 0)
    if bcast:
        buf[pos] = x_ref[...]
    else:
        buf[pos] = x_ref[pos]

    def finish(k, carry):
        j = lax.rem(pos + k, size)
        desc(j, pos).wait_send()
        desc(j, j).wait_recv()
        return carry

    lax.fori_loop(1, size, finish, 0)
    if reduce:
        y_ref[...] = jnp.sum(buf[...].astype(jnp.float32), axis=0)
    else:
        y_ref[...] = buf[...]


def exchange(x, ident, axis, size, stride=1, bcast=False, reduce=False):
    block = x.shape if bcast else x.shape[1:]
    out_shape = block if reduce else (size,) + block
    out_dtype = jnp.float32 if reduce else x.dtype
    return pl.pallas_call(
        functools.partial(exchange_kernel, axis, size, stride, bcast, reduce),
        out_shape=jax.ShapeDtypeStruct(out_shape, out_dtype),
        in_specs=[pl.BlockSpec(memory_space=pltpu.VMEM)],
        out_specs=pl.BlockSpec(memory_space=pltpu.VMEM),
        scratch_shapes=[
            pltpu.VMEM((size,) + block, x.dtype),
            pltpu.SemaphoreType.DMA((size,)),
            pltpu.SemaphoreType.DMA((size,)),
        ],
        compiler_params=pltpu.CompilerParams(collective_id=ident, has_side_effects=True),
    )(x)


def per_device(
    features,
    cached_embed,
    staleness,
    node_counts,
    neighbours,
    degrees,
    w_self,
    w_nbr,
    sage_bias,
    cotangent,
):
    n_dom = lax.axis_size("dom")
    n_col = lax.axis_size("col")
    col_width = features.shape[0]
    part_rows = features.shape[1]
    slot_count = neighbours.shape[0]
    hidden = w_self.shape[1]
    my_index = lax.axis_index("dom")
    fresh_flag = (staleness >= LIMIT).astype(jnp.int32)
    my_fresh = fresh_flag[my_index]
    own_cache = lax.dynamic_slice_in_dim(cached_embed, my_index * part_rows, part_rows, 1)
    own_source = jnp.where(my_fresh == 1, features, own_cache)
    blocks = exchange(own_source, 0, "dom", n_dom, bcast=True)
    sources = blocks.transpose(1, 0, 2).reshape(col_width, n_dom * part_rows)
    local_slot = jnp.arange(part_rows, dtype=jnp.int32)
    live_rows = (local_slot < node_counts[my_index]).astype(jnp.float32)
    slot_index = jnp.arange(slot_count, dtype=jnp.int32)
    used = (slot_index[:, None] < degrees[None, :]).astype(jnp.float32)
    weights = used * (live_rows / degrees.astype(jnp.float32))[None, :]
    gathered = sources[:, neighbours].astype(jnp.float32)
    aggregated = jnp.sum(weights[None, :, :] * gathered, axis=1).astype(jnp.bfloat16)
    partial_pre = left_product(w_self, features) + left_product(w_nbr, aggregated)
    pre_act = (
        exchange(partial_pre.reshape(n_col, hidden // n_col, part_rows), 1, "col", n_col, reduce=True)
        + sage_bias[:, None]
    )
    sigmoid = 1.0 / (1.0 + jnp.exp(-pre_act))
    activation = (live_rows[None, :] * pre_act * sigmoid).astype(jnp.bfloat16)
    grad_pre = (
        live_rows[None, :]
        * cotangent.astype(jnp.float32)
        * sigmoid
        * (1.0 + pre_act * (1.0 - sigmoid))
    ).astype(jnp.bfloat16)
    grad_full = exchange(grad_pre, 2, "col", n_col, bcast=True).reshape(hidden, part_rows)
    self_part = right_product(features, grad_full)
    nbr_part = right_product(aggregated, grad_full)
    bias_part = jnp.sum(grad_pre.astype(jnp.float32), axis=1)
    bias_rows = jnp.zeros((8, hidden), jnp.float32).at[0, : bias_part.shape[0]].set(bias_part)
    packed = jnp.concatenate([self_part, nbr_part, bias_rows], axis=0)
    group = 8 if n_dom % 8 == 0 else n_dom
    summed = exchange(packed, 3, "dom", group, bcast=True, reduce=True)
    if group < n_dom:
        summed = exchange(summed, 4, "dom", n_dom // group, stride=group, bcast=True, reduce=True)
    grad_self = summed[:col_width]
    grad_nbr = summed[col_width : 2 * col_width]
    grad_bias = summed[2 * col_width, : bias_part.shape[0]]
    grad_agg = jnp.dot(w_nbr, grad_full, preferred_element_type=jnp.float32).astype(jnp.bfloat16)
    own_term = jnp.dot(w_self, grad_full, preferred_element_type=jnp.float32)
    spread = weights[None, :, :] * grad_agg.astype(jnp.float32)[:, None, :]
    total_rows = cached_embed.shape[1]
    contrib = (
        jnp.zeros((col_width, total_rows), jnp.float32)
        .at[:, neighbours.reshape(-1)]
        .add(spread.reshape(col_width, -1))
    )
    contrib_blocks = contrib.reshape(col_width, n_dom, part_rows).transpose(1, 0, 2)
    back = exchange(contrib_blocks, 5, "dom", n_dom, reduce=True)
    grad_feat = (own_term + my_fresh.astype(jnp.float32) * back).astype(jnp.bfloat16)
    return (activation, grad_feat, grad_self, grad_nbr, grad_bias)


def solution(mesh):
    placed = (
        P("col", "dom"),
        P("col", None),
        P(),
        P(),
        P(None, "dom"),
        P("dom"),
        P("col", None),
        P("col", None),
        P("col"),
        P("col", "dom"),
    )
    return jax.shard_map(
        per_device,
        mesh=mesh,
        in_specs=placed,
        out_specs=(P("col", "dom"), P("col", "dom"), P("col", None), P("col", None), P("col")),
        check_vma=False,
    )
```

```python
import functools

import jax
import jax.numpy as jnp
from jax import lax
from jax.experimental import pallas as pl
from jax.experimental.pallas import tpu as pltpu
from jax.sharding import PartitionSpec as P

LIMIT = 8
MESH = pl.DeviceIdType.MESH


def left_product(weight, data):
    return lax.dot_general(
        weight, data, (((0,), (0,)), ((), ())), preferred_element_type=jnp.float32
    )


def right_product(data, grads):
    return lax.dot_general(
        data, grads, (((1,), (1,)), ((), ())), preferred_element_type=jnp.float32
    )


def exchange_kernel(axis, size, stride, bcast, reduce, lanes, x_ref, y_ref, buf, send_sem, recv_sem):
    me = lax.axis_index(axis)
    pos = lax.rem(me // stride, size)

    def member(j):
        return me + (j - pos) * stride

    barrier = pltpu.get_barrier_semaphore()

    def greet(k, carry):
        j = lax.rem(pos + k, size)
        pl.semaphore_signal(barrier, 1, device_id={axis: member(j)}, device_id_type=MESH)
        return carry

    lax.fori_loop(1, size, greet, 0)
    pl.semaphore_wait(barrier, size - 1)

    def chunk(j):
        if bcast:
            return x_ref
        if lanes:
            return x_ref.at[:, pl.ds(pl.multiple_of(j * lanes, lanes), lanes)]
        return x_ref.at[j]

    def desc(j, slot):
        src = chunk(j)
        return pltpu.make_async_remote_copy(
            src_ref=src,
            dst_ref=buf.at[slot],
            send_sem=send_sem.at[j],
            recv_sem=recv_sem.at[slot],
            device_id={axis: member(j)},
            device_id_type=MESH,
        )

    def send(k, carry):
        j = lax.rem(pos + k, size)
        desc(j, pos).start()
        return carry

    lax.fori_loop(1, size, send, 0)
    buf[pos] = chunk(pos)[...]

    def finish(k, carry):
        j = lax.rem(pos + k, size)
        desc(j, pos).wait_send()
        desc(j, j).wait_recv()
        return carry

    lax.fori_loop(1, size, finish, 0)
    if reduce:
        y_ref[...] = jnp.sum(buf[...].astype(jnp.float32), axis=0)
    else:
        y_ref[...] = buf[...]


def exchange(x, ident, axis, size, stride=1, bcast=False, reduce=False, lanes=0):
    if bcast:
        block = x.shape
    elif lanes:
        block = (x.shape[0], lanes)
    else:
        block = x.shape[1:]
    out_shape = block if reduce else (size,) + block
    out_dtype = jnp.float32 if reduce else x.dtype
    return pl.pallas_call(
        functools.partial(exchange_kernel, axis, size, stride, bcast, reduce, lanes),
        out_shape=jax.ShapeDtypeStruct(out_shape, out_dtype),
        in_specs=[pl.BlockSpec(memory_space=pltpu.VMEM)],
        out_specs=pl.BlockSpec(memory_space=pltpu.VMEM),
        scratch_shapes=[
            pltpu.VMEM((size,) + block, x.dtype),
            pltpu.SemaphoreType.DMA((size,)),
            pltpu.SemaphoreType.DMA((size,)),
        ],
        compiler_params=pltpu.CompilerParams(collective_id=ident, has_side_effects=True),
    )(x)


def per_device(
    features,
    cached_embed,
    staleness,
    node_counts,
    neighbours,
    degrees,
    w_self,
    w_nbr,
    sage_bias,
    cotangent,
):
    n_dom = lax.axis_size("dom")
    n_col = lax.axis_size("col")
    col_width = features.shape[0]
    part_rows = features.shape[1]
    slot_count = neighbours.shape[0]
    hidden = w_self.shape[1]
    my_index = lax.axis_index("dom")
    fresh_flag = (staleness >= LIMIT).astype(jnp.int32)
    my_fresh = fresh_flag[my_index]
    own_cache = lax.dynamic_slice_in_dim(cached_embed, my_index * part_rows, part_rows, 1)
    own_source = jnp.where(my_fresh == 1, features, own_cache)
    blocks = exchange(own_source, 0, "dom", n_dom, bcast=True)
    sources = blocks.transpose(1, 0, 2).reshape(col_width, n_dom * part_rows)
    local_slot = jnp.arange(part_rows, dtype=jnp.int32)
    live_rows = (local_slot < node_counts[my_index]).astype(jnp.float32)
    slot_index = jnp.arange(slot_count, dtype=jnp.int32)
    used = (slot_index[:, None] < degrees[None, :]).astype(jnp.float32)
    weights = used * (live_rows / degrees.astype(jnp.float32))[None, :]
    gathered = sources[:, neighbours].astype(jnp.float32)
    aggregated = jnp.sum(weights[None, :, :] * gathered, axis=1).astype(jnp.bfloat16)
    partial_pre = left_product(w_self, features) + left_product(w_nbr, aggregated)
    pre_act = (
        exchange(partial_pre.reshape(n_col, hidden // n_col, part_rows), 1, "col", n_col, reduce=True)
        + sage_bias[:, None]
    )
    sigmoid = 1.0 / (1.0 + jnp.exp(-pre_act))
    activation = (live_rows[None, :] * pre_act * sigmoid).astype(jnp.bfloat16)
    grad_pre = (
        live_rows[None, :]
        * cotangent.astype(jnp.float32)
        * sigmoid
        * (1.0 + pre_act * (1.0 - sigmoid))
    ).astype(jnp.bfloat16)
    grad_full = exchange(grad_pre, 2, "col", n_col, bcast=True).reshape(hidden, part_rows)
    self_part = right_product(features, grad_full)
    nbr_part = right_product(aggregated, grad_full)
    bias_part = jnp.sum(grad_pre.astype(jnp.float32), axis=1)
    bias_rows = jnp.zeros((8, hidden), jnp.float32).at[0, : bias_part.shape[0]].set(bias_part)
    packed = jnp.concatenate([self_part, nbr_part, bias_rows], axis=0)
    group = 8 if n_dom % 8 == 0 else n_dom
    summed = exchange(packed, 3, "dom", group, bcast=True, reduce=True)
    if group < n_dom:
        summed = exchange(summed, 4, "dom", n_dom // group, stride=group, bcast=True, reduce=True)
    grad_self = summed[:col_width]
    grad_nbr = summed[col_width : 2 * col_width]
    grad_bias = summed[2 * col_width, : bias_part.shape[0]]
    grad_agg = jnp.dot(w_nbr, grad_full, preferred_element_type=jnp.float32).astype(jnp.bfloat16)
    own_term = jnp.dot(w_self, grad_full, preferred_element_type=jnp.float32)
    spread = weights[None, :, :] * grad_agg.astype(jnp.float32)[:, None, :]
    total_rows = cached_embed.shape[1]
    contrib = (
        jnp.zeros((col_width, total_rows), jnp.float32)
        .at[:, neighbours.reshape(-1)]
        .add(spread.reshape(col_width, -1))
    )
    back = exchange(contrib.astype(jnp.bfloat16), 5, "dom", n_dom, reduce=True, lanes=part_rows)
    grad_feat = (own_term + my_fresh.astype(jnp.float32) * back).astype(jnp.bfloat16)
    return (activation, grad_feat, grad_self, grad_nbr, grad_bias)


def solution(mesh):
    placed = (
        P("col", "dom"),
        P("col", None),
        P(),
        P(),
        P(None, "dom"),
        P("dom"),
        P("col", None),
        P("col", None),
        P("col"),
        P("col", "dom"),
    )
    return jax.shard_map(
        per_device,
        mesh=mesh,
        in_specs=placed,
        out_specs=(P("col", "dom"), P("col", "dom"), P("col", None), P("col", None), P("col")),
        check_vma=False,
    )
```

```python
import functools

import jax
import jax.numpy as jnp
from jax import lax
from jax.experimental import pallas as pl
from jax.experimental.pallas import tpu as pltpu
from jax.sharding import PartitionSpec as P

LIMIT = 8
MESH = pl.DeviceIdType.MESH


def left_product(weight, data):
    return lax.dot_general(
        weight, data, (((0,), (0,)), ((), ())), preferred_element_type=jnp.float32
    )


def right_product(data, grads):
    return lax.dot_general(
        data, grads, (((1,), (1,)), ((), ())), preferred_element_type=jnp.float32
    )


def exchange_kernel(specs, *refs):
    count = len(specs)
    xs, ys = refs[:count], refs[count : 2 * count]
    scratch = refs[2 * count :]
    barrier = pltpu.get_barrier_semaphore()
    plans = []
    for e, (axis, size, stride, bcast, reduce, lanes) in enumerate(specs):
        x_ref, y_ref = xs[e], ys[e]
        buf, send_sem, recv_sem = scratch[3 * e : 3 * e + 3]
        me = lax.axis_index(axis)
        pos = lax.rem(me // stride, size)
        plans.append((axis, size, stride, bcast, reduce, lanes, x_ref, y_ref, buf, send_sem, recv_sem, me, pos))

    def member(plan, j):
        stride, me, pos = plan[2], plan[11], plan[12]
        return me + (j - pos) * stride

    def chunk(plan, j):
        bcast, lanes, x_ref = plan[3], plan[5], plan[6]
        if bcast:
            return x_ref
        if lanes:
            return x_ref.at[:, pl.ds(pl.multiple_of(j * lanes, lanes), lanes)]
        return x_ref.at[j]

    def desc(plan, j, slot):
        axis, buf, send_sem, recv_sem = plan[0], plan[8], plan[9], plan[10]
        return pltpu.make_async_remote_copy(
            src_ref=chunk(plan, j),
            dst_ref=buf.at[slot],
            send_sem=send_sem.at[j],
            recv_sem=recv_sem.at[slot],
            device_id={axis: member(plan, j)},
            device_id_type=MESH,
        )

    def each_peer(plan, body):
        size, pos = plan[1], plan[12]

        def step(k, carry):
            body(lax.rem(pos + k, size))
            return carry

        lax.fori_loop(1, size, step, 0)

    greetings = 0
    for plan in plans:
        each_peer(
            plan,
            lambda j, plan=plan: pl.semaphore_signal(
                barrier, 1, device_id={plan[0]: member(plan, j)}, device_id_type=MESH
            ),
        )
        greetings += plan[1] - 1
    pl.semaphore_wait(barrier, greetings)
    for plan in plans:
        each_peer(plan, lambda j, plan=plan: desc(plan, j, plan[12]).start())
    for plan in plans:
        buf, pos = plan[8], plan[12]
        buf[pos] = chunk(plan, pos)[...]
    for plan in plans:

        def finish(j, plan=plan):
            desc(plan, j, plan[12]).wait_send()
            desc(plan, j, j).wait_recv()

        each_peer(plan, finish)
    for plan in plans:
        reduce, y_ref, buf = plan[4], plan[7], plan[8]
        if reduce:
            y_ref[...] = jnp.sum(buf[...].astype(jnp.float32), axis=0)
        else:
            y_ref[...] = buf[...]


def exchange_many(ident, jobs):
    specs, out_shapes, scratch = [], [], []
    for x, axis, size, stride, bcast, reduce, lanes in jobs:
        if bcast:
            block = x.shape
        elif lanes:
            block = (x.shape[0], lanes)
        else:
            block = x.shape[1:]
        specs.append((axis, size, stride, bcast, reduce, lanes))
        out_shapes.append(
            jax.ShapeDtypeStruct(block if reduce else (size,) + block, jnp.float32 if reduce else x.dtype)
        )
        scratch += [
            pltpu.VMEM((size,) + block, x.dtype),
            pltpu.SemaphoreType.DMA((size,)),
            pltpu.SemaphoreType.DMA((size,)),
        ]
    return pl.pallas_call(
        functools.partial(exchange_kernel, tuple(specs)),
        out_shape=tuple(out_shapes),
        in_specs=[pl.BlockSpec(memory_space=pltpu.VMEM)] * len(jobs),
        out_specs=tuple(pl.BlockSpec(memory_space=pltpu.VMEM) for _ in jobs),
        scratch_shapes=scratch,
        compiler_params=pltpu.CompilerParams(collective_id=ident, has_side_effects=True),
    )(*[job[0] for job in jobs])


def exchange(x, ident, axis, size, stride=1, bcast=False, reduce=False, lanes=0):
    return exchange_many(ident, [(x, axis, size, stride, bcast, reduce, lanes)])[0]


def per_device(
    features,
    cached_embed,
    staleness,
    node_counts,
    neighbours,
    degrees,
    w_self,
    w_nbr,
    sage_bias,
    cotangent,
):
    n_dom = lax.axis_size("dom")
    n_col = lax.axis_size("col")
    col_width = features.shape[0]
    part_rows = features.shape[1]
    slot_count = neighbours.shape[0]
    hidden = w_self.shape[1]
    my_index = lax.axis_index("dom")
    fresh_flag = (staleness >= LIMIT).astype(jnp.int32)
    my_fresh = fresh_flag[my_index]
    own_cache = lax.dynamic_slice_in_dim(cached_embed, my_index * part_rows, part_rows, 1)
    own_source = jnp.where(my_fresh == 1, features, own_cache)
    col_inputs = jnp.concatenate([features, w_self, w_nbr, cotangent], axis=0)
    bias_block = jnp.zeros((8, 128), jnp.float32).at[0, : sage_bias.shape[0]].set(sage_bias)
    blocks, col_blocks, bias_blocks = exchange_many(
        0,
        [
            (own_source, "dom", n_dom, 1, True, False, 0),
            (col_inputs, "col", n_col, 1, True, False, 0),
            (bias_block, "col", n_col, 1, True, False, 0),
        ],
    )
    sources = blocks.transpose(1, 0, 2).reshape(col_width, n_dom * part_rows)
    feat_full = col_blocks[:, :col_width].reshape(n_col * col_width, part_rows)
    w_self_full = col_blocks[:, col_width : 2 * col_width].reshape(n_col * col_width, hidden)
    w_nbr_full = col_blocks[:, 2 * col_width : 3 * col_width].reshape(n_col * col_width, hidden)
    cot_full = col_blocks[:, 3 * col_width :].reshape(hidden, part_rows)
    bias_full = bias_blocks[:, 0, : sage_bias.shape[0]].reshape(hidden)
    local_slot = jnp.arange(part_rows, dtype=jnp.int32)
    live_rows = (local_slot < node_counts[my_index]).astype(jnp.float32)
    slot_index = jnp.arange(slot_count, dtype=jnp.int32)
    used = (slot_index[:, None] < degrees[None, :]).astype(jnp.float32)
    weights = used * (live_rows / degrees.astype(jnp.float32))[None, :]
    gathered = sources[:, neighbours].astype(jnp.float32)
    aggregated = jnp.sum(weights[None, :, :] * gathered, axis=1).astype(jnp.bfloat16)
    agg_full = exchange(aggregated, 1, "col", n_col, bcast=True).reshape(n_col * col_width, part_rows)
    pre_full = (
        left_product(w_self_full, feat_full)
        + left_product(w_nbr_full, agg_full)
        + bias_full[:, None]
    )
    sig_full = 1.0 / (1.0 + jnp.exp(-pre_full))
    my_col = lax.axis_index("col")
    block_rows = hidden // n_col
    pre_act = lax.dynamic_slice_in_dim(pre_full, my_col * block_rows, block_rows, 0)
    sigmoid = lax.dynamic_slice_in_dim(sig_full, my_col * block_rows, block_rows, 0)
    activation = (live_rows[None, :] * pre_act * sigmoid).astype(jnp.bfloat16)
    grad_full = (
        live_rows[None, :]
        * cot_full.astype(jnp.float32)
        * sig_full
        * (1.0 + pre_full * (1.0 - sig_full))
    ).astype(jnp.bfloat16)
    grad_pre = lax.dynamic_slice_in_dim(grad_full, my_col * block_rows, block_rows, 0)
    self_part = right_product(features, grad_full)
    nbr_part = right_product(aggregated, grad_full)
    bias_part = jnp.sum(grad_pre.astype(jnp.float32), axis=1)
    bias_rows = jnp.zeros((8, hidden), jnp.float32).at[0, : bias_part.shape[0]].set(bias_part)
    packed = jnp.concatenate([self_part, nbr_part, bias_rows], axis=0)
    group = 8 if n_dom % 8 == 0 else n_dom
    summed = exchange(packed, 3, "dom", group, bcast=True, reduce=True)
    if group < n_dom:
        summed = exchange(summed, 4, "dom", n_dom // group, stride=group, bcast=True, reduce=True)
    grad_self = summed[:col_width]
    grad_nbr = summed[col_width : 2 * col_width]
    grad_bias = summed[2 * col_width, : bias_part.shape[0]]
    grad_agg = jnp.dot(w_nbr, grad_full, preferred_element_type=jnp.float32).astype(jnp.bfloat16)
    own_term = jnp.dot(w_self, grad_full, preferred_element_type=jnp.float32)
    spread = weights[None, :, :] * grad_agg.astype(jnp.float32)[:, None, :]
    total_rows = cached_embed.shape[1]
    contrib = (
        jnp.zeros((col_width, total_rows), jnp.float32)
        .at[:, neighbours.reshape(-1)]
        .add(spread.reshape(col_width, -1))
    )
    back = exchange(contrib.astype(jnp.bfloat16), 5, "dom", n_dom, reduce=True, lanes=part_rows)
    grad_feat = (own_term + my_fresh.astype(jnp.float32) * back).astype(jnp.bfloat16)
    return (activation, grad_feat, grad_self, grad_nbr, grad_bias)


def solution(mesh):
    placed = (
        P("col", "dom"),
        P("col", None),
        P(),
        P(),
        P(None, "dom"),
        P("dom"),
        P("col", None),
        P("col", None),
        P("col"),
        P("col", "dom"),
    )
    return jax.shard_map(
        per_device,
        mesh=mesh,
        in_specs=placed,
        out_specs=(P("col", "dom"), P("col", "dom"), P("col", None), P("col", None), P("col")),
        check_vma=False,
    )
```

```python
import functools

import jax
import jax.numpy as jnp
from jax import lax
from jax.experimental import pallas as pl
from jax.experimental.pallas import tpu as pltpu
from jax.sharding import PartitionSpec as P

LIMIT = 8
MESH = pl.DeviceIdType.MESH


def left_product(weight, data):
    return lax.dot_general(
        weight, data, (((0,), (0,)), ((), ())), preferred_element_type=jnp.float32
    )


def right_product(data, grads):
    return lax.dot_general(
        data, grads, (((1,), (1,)), ((), ())), preferred_element_type=jnp.float32
    )


def exchange_kernel(specs, *refs):
    count = len(specs)
    xs, ys = refs[:count], refs[count : 2 * count]
    scratch = refs[2 * count :]
    barrier = pltpu.get_barrier_semaphore()
    plans = []
    for e, (axis, size, stride, bcast, reduce, lanes) in enumerate(specs):
        x_ref, y_ref = xs[e], ys[e]
        buf, send_sem, recv_sem = scratch[3 * e : 3 * e + 3]
        me = lax.axis_index(axis)
        pos = lax.rem(me // stride, size)
        plans.append((axis, size, stride, bcast, reduce, lanes, x_ref, y_ref, buf, send_sem, recv_sem, me, pos))

    def member(plan, j):
        stride, me, pos = plan[2], plan[11], plan[12]
        return me + (j - pos) * stride

    def chunk(plan, j):
        bcast, lanes, x_ref = plan[3], plan[5], plan[6]
        if bcast:
            return x_ref
        if lanes:
            return x_ref.at[:, pl.ds(pl.multiple_of(j * lanes, lanes), lanes)]
        return x_ref.at[j]

    def desc(plan, j, slot):
        axis, buf, send_sem, recv_sem = plan[0], plan[8], plan[9], plan[10]
        return pltpu.make_async_remote_copy(
            src_ref=chunk(plan, j),
            dst_ref=buf.at[slot],
            send_sem=send_sem.at[j],
            recv_sem=recv_sem.at[slot],
            device_id={axis: member(plan, j)},
            device_id_type=MESH,
        )

    def each_peer(plan, body):
        size, pos = plan[1], plan[12]

        def step(k, carry):
            body(lax.rem(pos + k, size))
            return carry

        lax.fori_loop(1, size, step, 0)

    greetings = 0
    for plan in plans:
        each_peer(
            plan,
            lambda j, plan=plan: pl.semaphore_signal(
                barrier, 1, device_id={plan[0]: member(plan, j)}, device_id_type=MESH
            ),
        )
        greetings += plan[1] - 1
    pl.semaphore_wait(barrier, greetings)
    for plan in plans:
        each_peer(plan, lambda j, plan=plan: desc(plan, j, plan[12]).start())
    for plan in plans:
        buf, pos = plan[8], plan[12]
        buf[pos] = chunk(plan, pos)[...]
    for plan in plans:

        def finish(j, plan=plan):
            desc(plan, j, plan[12]).wait_send()
            desc(plan, j, j).wait_recv()

        each_peer(plan, finish)
    for plan in plans:
        reduce, y_ref, buf = plan[4], plan[7], plan[8]
        if reduce:
            y_ref[...] = jnp.sum(buf[...].astype(jnp.float32), axis=0)
        else:
            y_ref[...] = buf[...]


def exchange_many(ident, jobs):
    specs, out_shapes, scratch = [], [], []
    for x, axis, size, stride, bcast, reduce, lanes in jobs:
        if bcast:
            block = x.shape
        elif lanes:
            block = (x.shape[0], lanes)
        else:
            block = x.shape[1:]
        specs.append((axis, size, stride, bcast, reduce, lanes))
        out_shapes.append(
            jax.ShapeDtypeStruct(block if reduce else (size,) + block, jnp.float32 if reduce else x.dtype)
        )
        scratch += [
            pltpu.VMEM((size,) + block, x.dtype),
            pltpu.SemaphoreType.DMA((size,)),
            pltpu.SemaphoreType.DMA((size,)),
        ]
    return pl.pallas_call(
        functools.partial(exchange_kernel, tuple(specs)),
        out_shape=tuple(out_shapes),
        in_specs=[pl.BlockSpec(memory_space=pltpu.VMEM)] * len(jobs),
        out_specs=tuple(pl.BlockSpec(memory_space=pltpu.VMEM) for _ in jobs),
        scratch_shapes=scratch,
        compiler_params=pltpu.CompilerParams(collective_id=ident, has_side_effects=True),
    )(*[job[0] for job in jobs])


def exchange(x, ident, axis, size, stride=1, bcast=False, reduce=False, lanes=0):
    return exchange_many(ident, [(x, axis, size, stride, bcast, reduce, lanes)])[0]


def per_device(
    features,
    cached_embed,
    staleness,
    node_counts,
    neighbours,
    degrees,
    w_self,
    w_nbr,
    sage_bias,
    cotangent,
):
    n_dom = lax.axis_size("dom")
    n_col = lax.axis_size("col")
    col_width = features.shape[0]
    part_rows = features.shape[1]
    slot_count = neighbours.shape[0]
    hidden = w_self.shape[1]
    my_index = lax.axis_index("dom")
    fresh_flag = (staleness >= LIMIT).astype(jnp.int32)
    my_fresh = fresh_flag[my_index]
    own_cache = lax.dynamic_slice_in_dim(cached_embed, my_index * part_rows, part_rows, 1)
    own_source = jnp.where(my_fresh == 1, features, own_cache)
    col_inputs = jnp.concatenate([features, w_self, w_nbr, cotangent], axis=0)
    bias_block = jnp.zeros((8, 128), jnp.float32).at[0, : sage_bias.shape[0]].set(sage_bias)
    blocks = exchange(own_source, 0, "dom", n_dom, bcast=True)
    sources = blocks.transpose(1, 0, 2).reshape(col_width, n_dom * part_rows)
    local_slot = jnp.arange(part_rows, dtype=jnp.int32)
    live_rows = (local_slot < node_counts[my_index]).astype(jnp.float32)
    slot_index = jnp.arange(slot_count, dtype=jnp.int32)
    used = (slot_index[:, None] < degrees[None, :]).astype(jnp.float32)
    weights = used * (live_rows / degrees.astype(jnp.float32))[None, :]
    gathered = sources[:, neighbours].astype(jnp.float32)
    aggregated = jnp.sum(weights[None, :, :] * gathered, axis=1).astype(jnp.bfloat16)
    col_blocks, bias_blocks = exchange_many(
        1,
        [
            (jnp.concatenate([aggregated, col_inputs], axis=0), "col", n_col, 1, True, False, 0),
            (bias_block, "col", n_col, 1, True, False, 0),
        ],
    )
    agg_full = col_blocks[:, :col_width].reshape(n_col * col_width, part_rows)
    col_blocks = col_blocks[:, col_width:]
    feat_full = col_blocks[:, :col_width].reshape(n_col * col_width, part_rows)
    w_self_full = col_blocks[:, col_width : 2 * col_width].reshape(n_col * col_width, hidden)
    w_nbr_full = col_blocks[:, 2 * col_width : 3 * col_width].reshape(n_col * col_width, hidden)
    cot_full = col_blocks[:, 3 * col_width :].reshape(hidden, part_rows)
    bias_full = bias_blocks[:, 0, : sage_bias.shape[0]].reshape(hidden)
    pre_full = (
        left_product(w_self_full, feat_full)
        + left_product(w_nbr_full, agg_full)
        + bias_full[:, None]
    )
    sig_full = 1.0 / (1.0 + jnp.exp(-pre_full))
    my_col = lax.axis_index("col")
    block_rows = hidden // n_col
    pre_act = lax.dynamic_slice_in_dim(pre_full, my_col * block_rows, block_rows, 0)
    sigmoid = lax.dynamic_slice_in_dim(sig_full, my_col * block_rows, block_rows, 0)
    activation = (live_rows[None, :] * pre_act * sigmoid).astype(jnp.bfloat16)
    grad_full = (
        live_rows[None, :]
        * cot_full.astype(jnp.float32)
        * sig_full
        * (1.0 + pre_full * (1.0 - sig_full))
    ).astype(jnp.bfloat16)
    grad_pre = lax.dynamic_slice_in_dim(grad_full, my_col * block_rows, block_rows, 0)
    self_part = right_product(features, grad_full)
    nbr_part = right_product(aggregated, grad_full)
    bias_part = jnp.sum(grad_pre.astype(jnp.float32), axis=1)
    bias_rows = jnp.zeros((8, hidden), jnp.float32).at[0, : bias_part.shape[0]].set(bias_part)
    packed = jnp.concatenate([self_part, nbr_part, bias_rows], axis=0)
    grad_agg = jnp.dot(w_nbr, grad_full, preferred_element_type=jnp.float32).astype(jnp.bfloat16)
    own_term = jnp.dot(w_self, grad_full, preferred_element_type=jnp.float32)
    spread = weights[None, :, :] * grad_agg.astype(jnp.float32)[:, None, :]
    total_rows = cached_embed.shape[1]
    contrib = (
        jnp.zeros((col_width, total_rows), jnp.float32)
        .at[:, neighbours.reshape(-1)]
        .add(spread.reshape(col_width, -1))
    )
    group = 8 if n_dom % 8 == 0 else n_dom
    back, summed = exchange_many(
        5,
        [
            (contrib.astype(jnp.bfloat16), "dom", n_dom, 1, False, True, part_rows),
            (packed, "dom", group, 1, True, True, 0),
        ],
    )
    if group < n_dom:
        summed = exchange(summed, 4, "dom", n_dom // group, stride=group, bcast=True, reduce=True)
    grad_self = summed[:col_width]
    grad_nbr = summed[col_width : 2 * col_width]
    grad_bias = summed[2 * col_width, : bias_part.shape[0]]
    grad_feat = (own_term + my_fresh.astype(jnp.float32) * back).astype(jnp.bfloat16)
    return (activation, grad_feat, grad_self, grad_nbr, grad_bias)


def solution(mesh):
    placed = (
        P("col", "dom"),
        P("col", None),
        P(),
        P(),
        P(None, "dom"),
        P("dom"),
        P("col", None),
        P("col", None),
        P("col"),
        P("col", "dom"),
    )
    return jax.shard_map(
        per_device,
        mesh=mesh,
        in_specs=placed,
        out_specs=(P("col", "dom"), P("col", "dom"), P("col", None), P("col", None), P("col")),
        check_vma=False,
    )
```

```python
import functools

import jax
import jax.numpy as jnp
from jax import lax
from jax.experimental import pallas as pl
from jax.experimental.pallas import tpu as pltpu
from jax.sharding import PartitionSpec as P

LIMIT = 8
MESH = pl.DeviceIdType.MESH


def left_product(weight, data):
    return lax.dot_general(
        weight, data, (((0,), (0,)), ((), ())), preferred_element_type=jnp.float32
    )


def right_product(data, grads):
    return lax.dot_general(
        data, grads, (((1,), (1,)), ((), ())), preferred_element_type=jnp.float32
    )


def exchange_kernel(specs, *refs):
    count = len(specs)
    xs, ys = refs[:count], refs[count : 2 * count]
    scratch = refs[2 * count :]
    barrier = pltpu.get_barrier_semaphore()
    plans = []
    for e, (axis, size, stride, bcast, reduce, lanes) in enumerate(specs):
        x_ref, y_ref = xs[e], ys[e]
        buf, send_sem, recv_sem = scratch[3 * e : 3 * e + 3]
        me = lax.axis_index(axis)
        pos = lax.rem(me // stride, size)
        plans.append((axis, size, stride, bcast, reduce, lanes, x_ref, y_ref, buf, send_sem, recv_sem, me, pos))

    def member(plan, j):
        stride, me, pos = plan[2], plan[11], plan[12]
        return me + (j - pos) * stride

    def chunk(plan, j):
        bcast, lanes, x_ref = plan[3], plan[5], plan[6]
        if bcast:
            return x_ref
        if lanes:
            return x_ref.at[:, pl.ds(pl.multiple_of(j * lanes, lanes), lanes)]
        return x_ref.at[j]

    def desc(plan, j, slot):
        axis, buf, send_sem, recv_sem = plan[0], plan[8], plan[9], plan[10]
        return pltpu.make_async_remote_copy(
            src_ref=chunk(plan, j),
            dst_ref=buf.at[slot],
            send_sem=send_sem.at[j],
            recv_sem=recv_sem.at[slot],
            device_id={axis: member(plan, j)},
            device_id_type=MESH,
        )

    def each_peer(plan, body):
        size, pos = plan[1], plan[12]

        def step(k, carry):
            body(lax.rem(pos + k, size))
            return carry

        lax.fori_loop(1, size, step, 0)

    greetings = 0
    for plan in plans:
        each_peer(
            plan,
            lambda j, plan=plan: pl.semaphore_signal(
                barrier, 1, device_id={plan[0]: member(plan, j)}, device_id_type=MESH
            ),
        )
        greetings += plan[1] - 1
    pl.semaphore_wait(barrier, greetings)
    for plan in plans:
        each_peer(plan, lambda j, plan=plan: desc(plan, j, plan[12]).start())
    for plan in plans:
        buf, pos = plan[8], plan[12]
        buf[pos] = chunk(plan, pos)[...]
    for plan in plans:

        def finish(j, plan=plan):
            desc(plan, j, plan[12]).wait_send()
            desc(plan, j, j).wait_recv()

        each_peer(plan, finish)
    for plan in plans:
        reduce, y_ref, buf = plan[4], plan[7], plan[8]
        if reduce:
            y_ref[...] = jnp.sum(buf[...].astype(jnp.float32), axis=0)
        else:
            y_ref[...] = buf[...]


def exchange_many(ident, jobs):
    specs, out_shapes, scratch = [], [], []
    for x, axis, size, stride, bcast, reduce, lanes in jobs:
        if bcast:
            block = x.shape
        elif lanes:
            block = (x.shape[0], lanes)
        else:
            block = x.shape[1:]
        specs.append((axis, size, stride, bcast, reduce, lanes))
        out_shapes.append(
            jax.ShapeDtypeStruct(block if reduce else (size,) + block, jnp.float32 if reduce else x.dtype)
        )
        scratch += [
            pltpu.VMEM((size,) + block, x.dtype),
            pltpu.SemaphoreType.DMA((size,)),
            pltpu.SemaphoreType.DMA((size,)),
        ]
    return pl.pallas_call(
        functools.partial(exchange_kernel, tuple(specs)),
        out_shape=tuple(out_shapes),
        in_specs=[pl.BlockSpec(memory_space=pltpu.VMEM)] * len(jobs),
        out_specs=tuple(pl.BlockSpec(memory_space=pltpu.VMEM) for _ in jobs),
        scratch_shapes=scratch,
        compiler_params=pltpu.CompilerParams(collective_id=ident, has_side_effects=True),
    )(*[job[0] for job in jobs])


def exchange(x, ident, axis, size, stride=1, bcast=False, reduce=False, lanes=0):
    return exchange_many(ident, [(x, axis, size, stride, bcast, reduce, lanes)])[0]


def group_sum(x, axis, n, size, stride):
    total = x
    for k in range(1, size):
        pairs = []
        for d in range(n):
            pos = (d // stride) % size
            pairs.append((d, d + ((pos + k) % size - pos) * stride))
        total = total + lax.ppermute(x, axis, pairs)
    return total


def per_device(
    features,
    cached_embed,
    staleness,
    node_counts,
    neighbours,
    degrees,
    w_self,
    w_nbr,
    sage_bias,
    cotangent,
):
    n_dom = lax.axis_size("dom")
    n_col = lax.axis_size("col")
    col_width = features.shape[0]
    part_rows = features.shape[1]
    slot_count = neighbours.shape[0]
    hidden = w_self.shape[1]
    my_index = lax.axis_index("dom")
    fresh_flag = (staleness >= LIMIT).astype(jnp.int32)
    my_fresh = fresh_flag[my_index]
    own_cache = lax.dynamic_slice_in_dim(cached_embed, my_index * part_rows, part_rows, 1)
    own_source = jnp.where(my_fresh == 1, features, own_cache)
    col_inputs = jnp.concatenate([features, w_self, w_nbr, cotangent], axis=0)
    bias_block = jnp.zeros((8, 128), jnp.float32).at[0, : sage_bias.shape[0]].set(sage_bias)
    blocks = exchange(own_source, 0, "dom", n_dom, bcast=True)
    sources = blocks.transpose(1, 0, 2).reshape(col_width, n_dom * part_rows)
    local_slot = jnp.arange(part_rows, dtype=jnp.int32)
    live_rows = (local_slot < node_counts[my_index]).astype(jnp.float32)
    slot_index = jnp.arange(slot_count, dtype=jnp.int32)
    used = (slot_index[:, None] < degrees[None, :]).astype(jnp.float32)
    weights = used * (live_rows / degrees.astype(jnp.float32))[None, :]
    gathered = sources[:, neighbours].astype(jnp.float32)
    aggregated = jnp.sum(weights[None, :, :] * gathered, axis=1).astype(jnp.bfloat16)
    col_blocks, bias_blocks = exchange_many(
        1,
        [
            (jnp.concatenate([aggregated, col_inputs], axis=0), "col", n_col, 1, True, False, 0),
            (bias_block, "col", n_col, 1, True, False, 0),
        ],
    )
    agg_full = col_blocks[:, :col_width].reshape(n_col * col_width, part_rows)
    col_blocks = col_blocks[:, col_width:]
    feat_full = col_blocks[:, :col_width].reshape(n_col * col_width, part_rows)
    w_self_full = col_blocks[:, col_width : 2 * col_width].reshape(n_col * col_width, hidden)
    w_nbr_full = col_blocks[:, 2 * col_width : 3 * col_width].reshape(n_col * col_width, hidden)
    cot_full = col_blocks[:, 3 * col_width :].reshape(hidden, part_rows)
    bias_full = bias_blocks[:, 0, : sage_bias.shape[0]].reshape(hidden)
    pre_full = (
        left_product(w_self_full, feat_full)
        + left_product(w_nbr_full, agg_full)
        + bias_full[:, None]
    )
    sig_full = 1.0 / (1.0 + jnp.exp(-pre_full))
    my_col = lax.axis_index("col")
    block_rows = hidden // n_col
    pre_act = lax.dynamic_slice_in_dim(pre_full, my_col * block_rows, block_rows, 0)
    sigmoid = lax.dynamic_slice_in_dim(sig_full, my_col * block_rows, block_rows, 0)
    activation = (live_rows[None, :] * pre_act * sigmoid).astype(jnp.bfloat16)
    grad_full = (
        live_rows[None, :]
        * cot_full.astype(jnp.float32)
        * sig_full
        * (1.0 + pre_full * (1.0 - sig_full))
    ).astype(jnp.bfloat16)
    grad_pre = lax.dynamic_slice_in_dim(grad_full, my_col * block_rows, block_rows, 0)
    self_part = right_product(features, grad_full)
    nbr_part = right_product(aggregated, grad_full)
    bias_part = jnp.sum(grad_pre.astype(jnp.float32), axis=1)
    bias_rows = jnp.zeros((8, hidden), jnp.float32).at[0, : bias_part.shape[0]].set(bias_part)
    packed = jnp.concatenate([self_part, nbr_part, bias_rows], axis=0)
    grad_agg = jnp.dot(w_nbr, grad_full, preferred_element_type=jnp.float32).astype(jnp.bfloat16)
    own_term = jnp.dot(w_self, grad_full, preferred_element_type=jnp.float32)
    spread = weights[None, :, :] * grad_agg.astype(jnp.float32)[:, None, :]
    total_rows = cached_embed.shape[1]
    contrib = (
        jnp.zeros((col_width, total_rows), jnp.float32)
        .at[:, neighbours.reshape(-1)]
        .add(spread.reshape(col_width, -1))
    )
    group = 8 if n_dom % 8 == 0 else n_dom
    summed = group_sum(packed, "dom", n_dom, group, 1)
    contrib_low, summed = lax.optimization_barrier((contrib.astype(jnp.bfloat16), summed))
    back = exchange(contrib_low, 5, "dom", n_dom, reduce=True, lanes=part_rows)
    if group < n_dom:
        summed = group_sum(summed, "dom", n_dom, n_dom // group, group)
    grad_self = summed[:col_width]
    grad_nbr = summed[col_width : 2 * col_width]
    grad_bias = summed[2 * col_width, : bias_part.shape[0]]
    grad_feat = (own_term + my_fresh.astype(jnp.float32) * back).astype(jnp.bfloat16)
    return (activation, grad_feat, grad_self, grad_nbr, grad_bias)


def solution(mesh):
    placed = (
        P("col", "dom"),
        P("col", None),
        P(),
        P(),
        P(None, "dom"),
        P("dom"),
        P("col", None),
        P("col", None),
        P("col"),
        P("col", "dom"),
    )
    return jax.shard_map(
        per_device,
        mesh=mesh,
        in_specs=placed,
        out_specs=(P("col", "dom"), P("col", "dom"), P("col", None), P("col", None), P("col")),
        check_vma=False,
    )
```

```python
import functools

import jax
import jax.numpy as jnp
from jax import lax
from jax.experimental import pallas as pl
from jax.experimental.pallas import tpu as pltpu
from jax.sharding import PartitionSpec as P

LIMIT = 8
MESH = pl.DeviceIdType.MESH


def left_product(weight, data):
    return lax.dot_general(
        weight, data, (((0,), (0,)), ((), ())), preferred_element_type=jnp.float32
    )


def right_product(data, grads):
    return lax.dot_general(
        data, grads, (((1,), (1,)), ((), ())), preferred_element_type=jnp.float32
    )


def exchange_kernel(specs, *refs):
    count = len(specs)
    xs, ys = refs[:count], refs[count : 2 * count]
    scratch = refs[2 * count :]
    barrier = pltpu.get_barrier_semaphore()
    plans = []
    extra = scratch[3 * count :]
    for e, (axis, size, stride, bcast, reduce, lanes, _, _) in enumerate(specs):
        x_ref, y_ref = xs[e], ys[e]
        buf, send_sem, recv_sem = scratch[3 * e : 3 * e + 3]
        me = lax.axis_index(axis)
        pos = lax.rem(me // stride, size)
        plans.append((axis, size, stride, bcast, reduce, lanes, x_ref, y_ref, buf, send_sem, recv_sem, me, pos))

    def member(plan, j):
        stride, me, pos = plan[2], plan[11], plan[12]
        return me + (j - pos) * stride

    def chunk(plan, j):
        bcast, lanes, x_ref = plan[3], plan[5], plan[6]
        if bcast:
            return x_ref
        if lanes:
            return x_ref.at[:, pl.ds(pl.multiple_of(j * lanes, lanes), lanes)]
        return x_ref.at[j]

    def desc(plan, j, slot):
        axis, buf, send_sem, recv_sem = plan[0], plan[8], plan[9], plan[10]
        return pltpu.make_async_remote_copy(
            src_ref=chunk(plan, j),
            dst_ref=buf.at[slot],
            send_sem=send_sem.at[j],
            recv_sem=recv_sem.at[slot],
            device_id={axis: member(plan, j)},
            device_id_type=MESH,
        )

    def each_peer(plan, body):
        size, pos = plan[1], plan[12]

        def step(k, carry):
            body(lax.rem(pos + k, size))
            return carry

        lax.fori_loop(1, size, step, 0)

    seconds = []
    for e, spec in enumerate(specs):
        if spec[6] > 1:
            stage, buf2, send2, recv2 = extra[4 * len(seconds) : 4 * len(seconds) + 4]
            me = plans[e][11]
            second = (spec[0], spec[6], spec[7], True, True, 0, stage, None, buf2, send2, recv2, me,
                      lax.rem(me // spec[7], spec[6]))
            seconds.append((e, second))
    greetings = 0
    for plan in plans + [second for _, second in seconds]:
        each_peer(
            plan,
            lambda j, plan=plan: pl.semaphore_signal(
                barrier, 1, device_id={plan[0]: member(plan, j)}, device_id_type=MESH
            ),
        )
        greetings += plan[1] - 1
    pl.semaphore_wait(barrier, greetings)
    for plan in plans:
        each_peer(plan, lambda j, plan=plan: desc(plan, j, plan[12]).start())
    for plan in plans:
        buf, pos = plan[8], plan[12]
        buf[pos] = chunk(plan, pos)[...]
    for e, second in seconds:
        plan = plans[e]

        def finish_first(j, plan=plan):
            desc(plan, j, plan[12]).wait_send()
            desc(plan, j, j).wait_recv()

        each_peer(plan, finish_first)
        second[6][...] = jnp.sum(plan[8][...].astype(jnp.float32), axis=0)
    for e, plan in enumerate(plans):
        if specs[e][6] > 1:
            continue
        for k in range(1, min(plan[1], 9)):
            desc(plan, lax.rem(plan[12] + k, plan[1]), plan[12]).wait_send()
    for _, second in seconds:
        each_peer(second, lambda j, second=second: desc(second, j, second[12]).start())
        second[8][second[12]] = second[6][...]
    for e, plan in enumerate(plans):
        if specs[e][6] > 1:
            continue

        def finish(k, carry, plan=plan):
            j = lax.rem(plan[12] + k, plan[1])
            desc(plan, j, plan[12]).wait_send()
            return carry

        lax.fori_loop(min(plan[1], 9), plan[1], finish, 0)

        def arrive(j, plan=plan):
            desc(plan, j, j).wait_recv()

        each_peer(plan, arrive)
    for _, second in seconds:

        def finish_second(j, second=second):
            desc(second, j, second[12]).wait_send()
            desc(second, j, j).wait_recv()

        each_peer(second, finish_second)
    for e, plan in enumerate(plans):
        reduce, y_ref, buf = plan[4], plan[7], plan[8]
        if specs[e][6] > 1:
            buf = dict(seconds)[e][8]
        if reduce:
            y_ref[...] = jnp.sum(buf[...].astype(jnp.float32), axis=0)
        else:
            y_ref[...] = buf[...]


def exchange_many(ident, jobs):
    specs, out_shapes, scratch, extra = [], [], [], []
    for job in jobs:
        x, axis, size, stride, bcast, reduce, lanes = job[:7]
        size2, stride2 = job[7:] if len(job) > 7 else (1, 1)
        if bcast:
            block = x.shape
        elif lanes:
            block = (x.shape[0], lanes)
        else:
            block = x.shape[1:]
        specs.append((axis, size, stride, bcast, reduce, lanes, size2, stride2))
        if size2 > 1:
            extra += [
                pltpu.VMEM(block, jnp.float32),
                pltpu.VMEM((size2,) + block, jnp.float32),
                pltpu.SemaphoreType.DMA((size2,)),
                pltpu.SemaphoreType.DMA((size2,)),
            ]
        out_shapes.append(
            jax.ShapeDtypeStruct(block if reduce else (size,) + block, jnp.float32 if reduce else x.dtype)
        )
        scratch += [
            pltpu.VMEM((size,) + block, x.dtype),
            pltpu.SemaphoreType.DMA((size,)),
            pltpu.SemaphoreType.DMA((size,)),
        ]
    return pl.pallas_call(
        functools.partial(exchange_kernel, tuple(specs)),
        out_shape=tuple(out_shapes),
        in_specs=[pl.BlockSpec(memory_space=pltpu.VMEM)] * len(jobs),
        out_specs=tuple(pl.BlockSpec(memory_space=pltpu.VMEM) for _ in jobs),
        scratch_shapes=scratch + extra,
        compiler_params=pltpu.CompilerParams(collective_id=ident, has_side_effects=True),
    )(*[job[0] for job in jobs])


def exchange(x, ident, axis, size, stride=1, bcast=False, reduce=False, lanes=0):
    return exchange_many(ident, [(x, axis, size, stride, bcast, reduce, lanes)])[0]


def per_device(
    features,
    cached_embed,
    staleness,
    node_counts,
    neighbours,
    degrees,
    w_self,
    w_nbr,
    sage_bias,
    cotangent,
):
    n_dom = lax.axis_size("dom")
    n_col = lax.axis_size("col")
    col_width = features.shape[0]
    part_rows = features.shape[1]
    slot_count = neighbours.shape[0]
    hidden = w_self.shape[1]
    my_index = lax.axis_index("dom")
    fresh_flag = (staleness >= LIMIT).astype(jnp.int32)
    my_fresh = fresh_flag[my_index]
    own_cache = lax.dynamic_slice_in_dim(cached_embed, my_index * part_rows, part_rows, 1)
    own_source = jnp.where(my_fresh == 1, features, own_cache)
    col_inputs = jnp.concatenate([features, w_self, w_nbr, cotangent], axis=0)
    bias_block = jnp.zeros((8, 128), jnp.float32).at[0, : sage_bias.shape[0]].set(sage_bias)
    blocks = exchange(own_source, 0, "dom", n_dom, bcast=True)
    sources = blocks.transpose(1, 0, 2).reshape(col_width, n_dom * part_rows)
    local_slot = jnp.arange(part_rows, dtype=jnp.int32)
    live_rows = (local_slot < node_counts[my_index]).astype(jnp.float32)
    slot_index = jnp.arange(slot_count, dtype=jnp.int32)
    used = (slot_index[:, None] < degrees[None, :]).astype(jnp.float32)
    weights = used * (live_rows / degrees.astype(jnp.float32))[None, :]
    gathered = sources[:, neighbours].astype(jnp.float32)
    aggregated = jnp.sum(weights[None, :, :] * gathered, axis=1).astype(jnp.bfloat16)
    col_blocks, bias_blocks = exchange_many(
        1,
        [
            (jnp.concatenate([aggregated, col_inputs], axis=0), "col", n_col, 1, True, False, 0),
            (bias_block, "col", n_col, 1, True, False, 0),
        ],
    )
    agg_full = col_blocks[:, :col_width].reshape(n_col * col_width, part_rows)
    col_blocks = col_blocks[:, col_width:]
    feat_full = col_blocks[:, :col_width].reshape(n_col * col_width, part_rows)
    w_self_full = col_blocks[:, col_width : 2 * col_width].reshape(n_col * col_width, hidden)
    w_nbr_full = col_blocks[:, 2 * col_width : 3 * col_width].reshape(n_col * col_width, hidden)
    cot_full = col_blocks[:, 3 * col_width :].reshape(hidden, part_rows)
    bias_full = bias_blocks[:, 0, : sage_bias.shape[0]].reshape(hidden)
    pre_full = (
        left_product(w_self_full, feat_full)
        + left_product(w_nbr_full, agg_full)
        + bias_full[:, None]
    )
    sig_full = 1.0 / (1.0 + jnp.exp(-pre_full))
    my_col = lax.axis_index("col")
    block_rows = hidden // n_col
    pre_act = lax.dynamic_slice_in_dim(pre_full, my_col * block_rows, block_rows, 0)
    sigmoid = lax.dynamic_slice_in_dim(sig_full, my_col * block_rows, block_rows, 0)
    activation = (live_rows[None, :] * pre_act * sigmoid).astype(jnp.bfloat16)
    grad_full = (
        live_rows[None, :]
        * cot_full.astype(jnp.float32)
        * sig_full
        * (1.0 + pre_full * (1.0 - sig_full))
    ).astype(jnp.bfloat16)
    grad_pre = lax.dynamic_slice_in_dim(grad_full, my_col * block_rows, block_rows, 0)
    self_part = right_product(features, grad_full)
    nbr_part = right_product(aggregated, grad_full)
    bias_part = jnp.sum(grad_pre.astype(jnp.float32), axis=1)
    bias_rows = jnp.zeros((8, hidden), jnp.float32).at[0, : bias_part.shape[0]].set(bias_part)
    packed = jnp.concatenate([self_part, nbr_part, bias_rows], axis=0)
    grad_agg = jnp.dot(w_nbr, grad_full, preferred_element_type=jnp.float32).astype(jnp.bfloat16)
    own_term = jnp.dot(w_self, grad_full, preferred_element_type=jnp.float32)
    spread = weights[None, :, :] * grad_agg.astype(jnp.float32)[:, None, :]
    total_rows = cached_embed.shape[1]
    contrib = (
        jnp.zeros((col_width, total_rows), jnp.float32)
        .at[:, neighbours.reshape(-1)]
        .add(spread.reshape(col_width, -1))
    )
    group = 8 if n_dom % 8 == 0 else n_dom
    back, summed = exchange_many(
        5,
        [
            (contrib.astype(jnp.bfloat16), "dom", n_dom, 1, False, True, part_rows),
            (packed, "dom", group, 1, True, True, 0, n_dom // group, group),
        ],
    )
    grad_self = summed[:col_width]
    grad_nbr = summed[col_width : 2 * col_width]
    grad_bias = summed[2 * col_width, : bias_part.shape[0]]
    grad_feat = (own_term + my_fresh.astype(jnp.float32) * back).astype(jnp.bfloat16)
    return (activation, grad_feat, grad_self, grad_nbr, grad_bias)


def solution(mesh):
    placed = (
        P("col", "dom"),
        P("col", None),
        P(),
        P(),
        P(None, "dom"),
        P("dom"),
        P("col", None),
        P("col", None),
        P("col"),
        P("col", "dom"),
    )
    return jax.shard_map(
        per_device,
        mesh=mesh,
        in_specs=placed,
        out_specs=(P("col", "dom"), P("col", "dom"), P("col", None), P("col", None), P("col")),
        check_vma=False,
    )
```

```python
import functools

import jax
import jax.numpy as jnp
from jax import lax
from jax.experimental import pallas as pl
from jax.experimental.pallas import tpu as pltpu
from jax.sharding import PartitionSpec as P

LIMIT = 8
MESH = pl.DeviceIdType.MESH


def left_product(weight, data):
    return lax.dot_general(
        weight, data, (((0,), (0,)), ((), ())), preferred_element_type=jnp.float32
    )


def right_product(data, grads):
    return lax.dot_general(
        data, grads, (((1,), (1,)), ((), ())), preferred_element_type=jnp.float32
    )


def group_pos(me, digits):
    pos, scale = 0, 1
    for radix, stride in digits:
        pos = pos + lax.rem(me // stride, radix) * scale
        scale *= radix
    return pos


def group_member(me, pos, j, digits):
    for radix, stride in digits:
        me = me + (lax.rem(j, radix) - lax.rem(pos, radix)) * stride
        j, pos = j // radix, pos // radix
    return me


def exchange_kernel(specs, *refs):
    count = len(specs)
    xs, ys = refs[:count], refs[count : 2 * count]
    scratch = refs[2 * count :]
    barrier = pltpu.get_barrier_semaphore()
    plans = []
    extra = scratch[3 * count :]
    for e, (axis, size, stride, bcast, reduce, lanes, _, _) in enumerate(specs):
        x_ref, y_ref = xs[e], ys[e]
        buf, send_sem, recv_sem = scratch[3 * e : 3 * e + 3]
        me = lax.axis_index(axis)
        pos = group_pos(me, stride)
        plans.append((axis, size, stride, bcast, reduce, lanes, x_ref, y_ref, buf, send_sem, recv_sem, me, pos))

    def member(plan, j):
        stride, me, pos = plan[2], plan[11], plan[12]
        return group_member(me, pos, j, stride)

    def chunk(plan, j):
        bcast, lanes, x_ref = plan[3], plan[5], plan[6]
        if bcast:
            return x_ref
        if lanes:
            return x_ref.at[:, pl.ds(pl.multiple_of(j * lanes, lanes), lanes)]
        return x_ref.at[j]

    def desc(plan, j, slot):
        axis, buf, send_sem, recv_sem = plan[0], plan[8], plan[9], plan[10]
        return pltpu.make_async_remote_copy(
            src_ref=chunk(plan, j),
            dst_ref=buf.at[slot],
            send_sem=send_sem.at[j],
            recv_sem=recv_sem.at[slot],
            device_id={axis: member(plan, j)},
            device_id_type=MESH,
        )

    def each_peer(plan, body):
        size, pos = plan[1], plan[12]

        def step(k, carry):
            body(lax.rem(pos + k, size))
            return carry

        lax.fori_loop(1, size, step, 0)

    seconds = []
    for e, spec in enumerate(specs):
        if spec[6] > 1:
            stage, buf2, send2, recv2 = extra[4 * len(seconds) : 4 * len(seconds) + 4]
            me = plans[e][11]
            second = (spec[0], spec[6], spec[7], True, True, 0, stage, None, buf2, send2, recv2, me,
                      group_pos(me, spec[7]))
            seconds.append((e, second))
    greetings = 0
    for plan in plans + [second for _, second in seconds]:
        each_peer(
            plan,
            lambda j, plan=plan: pl.semaphore_signal(
                barrier, 1, device_id={plan[0]: member(plan, j)}, device_id_type=MESH
            ),
        )
        greetings += plan[1] - 1
    pl.semaphore_wait(barrier, greetings)
    for plan in plans:
        each_peer(plan, lambda j, plan=plan: desc(plan, j, plan[12]).start())
    for plan in plans:
        buf, pos = plan[8], plan[12]
        buf[pos] = chunk(plan, pos)[...]
    for e, second in seconds:
        plan = plans[e]

        def finish_first(j, plan=plan):
            desc(plan, j, plan[12]).wait_send()
            desc(plan, j, j).wait_recv()

        each_peer(plan, finish_first)
        second[6][...] = jnp.sum(plan[8][...].astype(jnp.float32), axis=0)
    for e, plan in enumerate(plans):
        if specs[e][6] > 1:
            continue
        for k in range(1, min(plan[1], 9)):
            desc(plan, lax.rem(plan[12] + k, plan[1]), plan[12]).wait_send()
    for _, second in seconds:
        each_peer(second, lambda j, second=second: desc(second, j, second[12]).start())
        second[8][second[12]] = second[6][...]
    for e, plan in enumerate(plans):
        if specs[e][6] > 1:
            continue

        def finish(k, carry, plan=plan):
            j = lax.rem(plan[12] + k, plan[1])
            desc(plan, j, plan[12]).wait_send()
            return carry

        lax.fori_loop(min(plan[1], 9), plan[1], finish, 0)

        def arrive(j, plan=plan):
            desc(plan, j, j).wait_recv()

        each_peer(plan, arrive)
    for _, second in seconds:

        def finish_second(j, second=second):
            desc(second, j, second[12]).wait_send()
            desc(second, j, j).wait_recv()

        each_peer(second, finish_second)
    for e, plan in enumerate(plans):
        reduce, y_ref, buf = plan[4], plan[7], plan[8]
        if specs[e][6] > 1:
            buf = dict(seconds)[e][8]
        if reduce:
            y_ref[...] = jnp.sum(buf[...].astype(jnp.float32), axis=0)
        else:
            y_ref[...] = buf[...]


def exchange_many(ident, jobs):
    specs, out_shapes, scratch, extra = [], [], [], []
    for job in jobs:
        x, axis, size, stride, bcast, reduce, lanes = job[:7]
        size2, stride2 = job[7:] if len(job) > 7 else (1, ((1, 1),))
        if bcast:
            block = x.shape
        elif lanes:
            block = (x.shape[0], lanes)
        else:
            block = x.shape[1:]
        specs.append((axis, size, stride, bcast, reduce, lanes, size2, stride2))
        if size2 > 1:
            extra += [
                pltpu.VMEM(block, jnp.float32),
                pltpu.VMEM((size2,) + block, jnp.float32),
                pltpu.SemaphoreType.DMA((size2,)),
                pltpu.SemaphoreType.DMA((size2,)),
            ]
        out_shapes.append(
            jax.ShapeDtypeStruct(block if reduce else (size,) + block, jnp.float32 if reduce else x.dtype)
        )
        scratch += [
            pltpu.VMEM((size,) + block, x.dtype),
            pltpu.SemaphoreType.DMA((size,)),
            pltpu.SemaphoreType.DMA((size,)),
        ]
    return pl.pallas_call(
        functools.partial(exchange_kernel, tuple(specs)),
        out_shape=tuple(out_shapes),
        in_specs=[pl.BlockSpec(memory_space=pltpu.VMEM)] * len(jobs),
        out_specs=tuple(pl.BlockSpec(memory_space=pltpu.VMEM) for _ in jobs),
        scratch_shapes=scratch + extra,
        compiler_params=pltpu.CompilerParams(collective_id=ident, has_side_effects=True),
    )(*[job[0] for job in jobs])


def exchange(x, ident, axis, size, stride=None, bcast=False, reduce=False, lanes=0):
    stride = ((size, 1),) if stride is None else stride
    return exchange_many(ident, [(x, axis, size, stride, bcast, reduce, lanes)])[0]


def per_device(
    features,
    cached_embed,
    staleness,
    node_counts,
    neighbours,
    degrees,
    w_self,
    w_nbr,
    sage_bias,
    cotangent,
):
    n_dom = lax.axis_size("dom")
    n_col = lax.axis_size("col")
    col_width = features.shape[0]
    part_rows = features.shape[1]
    slot_count = neighbours.shape[0]
    hidden = w_self.shape[1]
    my_index = lax.axis_index("dom")
    fresh_flag = (staleness >= LIMIT).astype(jnp.int32)
    my_fresh = fresh_flag[my_index]
    own_cache = lax.dynamic_slice_in_dim(cached_embed, my_index * part_rows, part_rows, 1)
    own_source = jnp.where(my_fresh == 1, features, own_cache)
    col_inputs = jnp.concatenate([features, w_self, w_nbr, cotangent], axis=0)
    bias_block = jnp.zeros((8, 128), jnp.float32).at[0, : sage_bias.shape[0]].set(sage_bias)
    blocks = exchange(own_source, 0, "dom", n_dom, bcast=True)
    sources = blocks.transpose(1, 0, 2).reshape(col_width, n_dom * part_rows)
    local_slot = jnp.arange(part_rows, dtype=jnp.int32)
    live_rows = (local_slot < node_counts[my_index]).astype(jnp.float32)
    slot_index = jnp.arange(slot_count, dtype=jnp.int32)
    used = (slot_index[:, None] < degrees[None, :]).astype(jnp.float32)
    weights = used * (live_rows / degrees.astype(jnp.float32))[None, :]
    gathered = sources[:, neighbours].astype(jnp.float32)
    aggregated = jnp.sum(weights[None, :, :] * gathered, axis=1).astype(jnp.bfloat16)
    col_blocks, bias_blocks = exchange_many(
        1,
        [
            (jnp.concatenate([aggregated, col_inputs], axis=0), "col", n_col, ((n_col, 1),), True, False, 0),
            (bias_block, "col", n_col, ((n_col, 1),), True, False, 0),
        ],
    )
    agg_full = col_blocks[:, :col_width].reshape(n_col * col_width, part_rows)
    col_blocks = col_blocks[:, col_width:]
    feat_full = col_blocks[:, :col_width].reshape(n_col * col_width, part_rows)
    w_self_full = col_blocks[:, col_width : 2 * col_width].reshape(n_col * col_width, hidden)
    w_nbr_full = col_blocks[:, 2 * col_width : 3 * col_width].reshape(n_col * col_width, hidden)
    cot_full = col_blocks[:, 3 * col_width :].reshape(hidden, part_rows)
    bias_full = bias_blocks[:, 0, : sage_bias.shape[0]].reshape(hidden)
    pre_full = (
        left_product(w_self_full, feat_full)
        + left_product(w_nbr_full, agg_full)
        + bias_full[:, None]
    )
    sig_full = 1.0 / (1.0 + jnp.exp(-pre_full))
    my_col = lax.axis_index("col")
    block_rows = hidden // n_col
    pre_act = lax.dynamic_slice_in_dim(pre_full, my_col * block_rows, block_rows, 0)
    sigmoid = lax.dynamic_slice_in_dim(sig_full, my_col * block_rows, block_rows, 0)
    activation = (live_rows[None, :] * pre_act * sigmoid).astype(jnp.bfloat16)
    grad_full = (
        live_rows[None, :]
        * cot_full.astype(jnp.float32)
        * sig_full
        * (1.0 + pre_full * (1.0 - sig_full))
    ).astype(jnp.bfloat16)
    grad_pre = lax.dynamic_slice_in_dim(grad_full, my_col * block_rows, block_rows, 0)
    self_part = right_product(features, grad_full)
    nbr_part = right_product(aggregated, grad_full)
    bias_part = jnp.sum(grad_pre.astype(jnp.float32), axis=1)
    bias_rows = jnp.zeros((8, hidden), jnp.float32).at[0, : bias_part.shape[0]].set(bias_part)
    packed = jnp.concatenate([self_part, nbr_part, bias_rows], axis=0)
    grad_agg = jnp.dot(w_nbr, grad_full, preferred_element_type=jnp.float32).astype(jnp.bfloat16)
    own_term = jnp.dot(w_self, grad_full, preferred_element_type=jnp.float32)
    spread = weights[None, :, :] * grad_agg.astype(jnp.float32)[:, None, :]
    total_rows = cached_embed.shape[1]
    contrib = (
        jnp.zeros((col_width, total_rows), jnp.float32)
        .at[:, neighbours.reshape(-1)]
        .add(spread.reshape(col_width, -1))
    )
    ys = 8 if n_dom % 16 == 0 else 1
    first = ((2, 1), (n_dom // (2 * ys), 2 * ys))
    back, summed = exchange_many(
        5,
        [
            (contrib.astype(jnp.bfloat16), "dom", n_dom, ((n_dom, 1),), False, True, part_rows),
            (packed, "dom", n_dom // ys, first, True, True, 0, ys, ((ys, 2),)),
        ],
    )
    grad_self = summed[:col_width]
    grad_nbr = summed[col_width : 2 * col_width]
    grad_bias = summed[2 * col_width, : bias_part.shape[0]]
    grad_feat = (own_term + my_fresh.astype(jnp.float32) * back).astype(jnp.bfloat16)
    return (activation, grad_feat, grad_self, grad_nbr, grad_bias)


def solution(mesh):
    placed = (
        P("col", "dom"),
        P("col", None),
        P(),
        P(),
        P(None, "dom"),
        P("dom"),
        P("col", None),
        P("col", None),
        P("col"),
        P("col", "dom"),
    )
    return jax.shard_map(
        per_device,
        mesh=mesh,
        in_specs=placed,
        out_specs=(P("col", "dom"), P("col", "dom"), P("col", None), P("col", None), P("col")),
        check_vma=False,
    )
```

```python
import functools

import jax
import jax.numpy as jnp
from jax import lax
from jax.experimental import pallas as pl
from jax.experimental.pallas import tpu as pltpu
from jax.sharding import PartitionSpec as P

LIMIT = 8
MESH = pl.DeviceIdType.MESH


def left_product(weight, data):
    return lax.dot_general(
        weight, data, (((0,), (0,)), ((), ())), preferred_element_type=jnp.float32
    )


def right_product(data, grads):
    return lax.dot_general(
        data, grads, (((1,), (1,)), ((), ())), preferred_element_type=jnp.float32
    )


def group_pos(me, digits):
    pos, scale = 0, 1
    for radix, stride in digits:
        pos = pos + lax.rem(me // stride, radix) * scale
        scale *= radix
    return pos


def group_member(me, pos, j, digits):
    for radix, stride in digits:
        me = me + (lax.rem(j, radix) - lax.rem(pos, radix)) * stride
        j, pos = j // radix, pos // radix
    return me


def exchange_kernel(specs, *refs):
    count = len(specs)
    xs, ys = refs[:count], refs[count : 2 * count]
    scratch = refs[2 * count :]
    barrier = pltpu.get_barrier_semaphore()
    plans = []
    extra = scratch[3 * count :]
    for e, (axis, size, stride, bcast, reduce, lanes, _, _) in enumerate(specs):
        x_ref, y_ref = xs[e], ys[e]
        buf, send_sem, recv_sem = scratch[3 * e : 3 * e + 3]
        me = lax.axis_index(axis)
        pos = group_pos(me, stride)
        plans.append((axis, size, stride, bcast, reduce, lanes, x_ref, y_ref, buf, send_sem, recv_sem, me, pos))

    def member(plan, j):
        stride, me, pos = plan[2], plan[11], plan[12]
        return group_member(me, pos, j, stride)

    def chunk(plan, j):
        bcast, lanes, x_ref = plan[3], plan[5], plan[6]
        if bcast:
            return x_ref
        if lanes:
            return x_ref.at[:, pl.ds(pl.multiple_of(j * lanes, lanes), lanes)]
        return x_ref.at[j]

    def desc(plan, j, slot):
        axis, buf, send_sem, recv_sem = plan[0], plan[8], plan[9], plan[10]
        return pltpu.make_async_remote_copy(
            src_ref=chunk(plan, j),
            dst_ref=buf.at[slot],
            send_sem=send_sem.at[j],
            recv_sem=recv_sem.at[slot],
            device_id={axis: member(plan, j)},
            device_id_type=MESH,
        )

    def each_peer(plan, body):
        size, pos = plan[1], plan[12]

        def step(k, carry):
            body(lax.rem(pos + k, size))
            return carry

        lax.fori_loop(1, size, step, 0)

    seconds = []
    for e, spec in enumerate(specs):
        if spec[6] > 1:
            stage, buf2, send2, recv2 = extra[4 * len(seconds) : 4 * len(seconds) + 4]
            me = plans[e][11]
            second = (spec[0], spec[6], spec[7], True, True, 0, stage, None, buf2, send2, recv2, me,
                      group_pos(me, spec[7]))
            seconds.append((e, second))
    greetings = 0
    for plan in plans + [second for _, second in seconds]:
        each_peer(
            plan,
            lambda j, plan=plan: pl.semaphore_signal(
                barrier, 1, device_id={plan[0]: member(plan, j)}, device_id_type=MESH
            ),
        )
        greetings += plan[1] - 1
    pl.semaphore_wait(barrier, greetings)
    for plan in plans:
        each_peer(plan, lambda j, plan=plan: desc(plan, j, plan[12]).start())
    for plan in plans:
        buf, pos = plan[8], plan[12]
        buf[pos] = chunk(plan, pos)[...]
    for e, second in seconds:
        plan = plans[e]

        def finish_first(j, plan=plan):
            desc(plan, j, plan[12]).wait_send()
            desc(plan, j, j).wait_recv()

        each_peer(plan, finish_first)
        second[6][...] = jnp.sum(plan[8][...].astype(jnp.float32), axis=0).astype(second[6].dtype)
    for e, plan in enumerate(plans):
        if specs[e][6] > 1:
            continue
        for k in range(1, min(plan[1], 9)):
            desc(plan, lax.rem(plan[12] + k, plan[1]), plan[12]).wait_send()
    for _, second in seconds:
        each_peer(second, lambda j, second=second: desc(second, j, second[12]).start())
        second[8][second[12]] = second[6][...]
    for e, plan in enumerate(plans):
        if specs[e][6] > 1:
            continue

        def finish(k, carry, plan=plan):
            j = lax.rem(plan[12] + k, plan[1])
            desc(plan, j, plan[12]).wait_send()
            return carry

        lax.fori_loop(min(plan[1], 9), plan[1], finish, 0)

        def arrive(j, plan=plan):
            desc(plan, j, j).wait_recv()

        each_peer(plan, arrive)
    for _, second in seconds:

        def finish_second(j, second=second):
            desc(second, j, second[12]).wait_send()
            desc(second, j, j).wait_recv()

        each_peer(second, finish_second)
    for e, plan in enumerate(plans):
        reduce, y_ref, buf = plan[4], plan[7], plan[8]
        if specs[e][6] > 1:
            buf = dict(seconds)[e][8]
        if reduce:
            y_ref[...] = jnp.sum(buf[...].astype(jnp.float32), axis=0)
        else:
            y_ref[...] = buf[...]


def exchange_many(ident, jobs):
    specs, out_shapes, scratch, extra = [], [], [], []
    for job in jobs:
        x, axis, size, stride, bcast, reduce, lanes = job[:7]
        size2, stride2 = job[7:] if len(job) > 7 else (1, ((1, 1),))
        if bcast:
            block = x.shape
        elif lanes:
            block = (x.shape[0], lanes)
        else:
            block = x.shape[1:]
        specs.append((axis, size, stride, bcast, reduce, lanes, size2, stride2))
        if size2 > 1:
            extra += [
                pltpu.VMEM(block, x.dtype),
                pltpu.VMEM((size2,) + block, x.dtype),
                pltpu.SemaphoreType.DMA((size2,)),
                pltpu.SemaphoreType.DMA((size2,)),
            ]
        out_shapes.append(
            jax.ShapeDtypeStruct(block if reduce else (size,) + block, jnp.float32 if reduce else x.dtype)
        )
        scratch += [
            pltpu.VMEM((size,) + block, x.dtype),
            pltpu.SemaphoreType.DMA((size,)),
            pltpu.SemaphoreType.DMA((size,)),
        ]
    return pl.pallas_call(
        functools.partial(exchange_kernel, tuple(specs)),
        out_shape=tuple(out_shapes),
        in_specs=[pl.BlockSpec(memory_space=pltpu.VMEM)] * len(jobs),
        out_specs=tuple(pl.BlockSpec(memory_space=pltpu.VMEM) for _ in jobs),
        scratch_shapes=scratch + extra,
        compiler_params=pltpu.CompilerParams(collective_id=ident, has_side_effects=True),
    )(*[job[0] for job in jobs])


def exchange(x, ident, axis, size, stride=None, bcast=False, reduce=False, lanes=0):
    stride = ((size, 1),) if stride is None else stride
    return exchange_many(ident, [(x, axis, size, stride, bcast, reduce, lanes)])[0]


def per_device(
    features,
    cached_embed,
    staleness,
    node_counts,
    neighbours,
    degrees,
    w_self,
    w_nbr,
    sage_bias,
    cotangent,
):
    n_dom = lax.axis_size("dom")
    n_col = lax.axis_size("col")
    col_width = features.shape[0]
    part_rows = features.shape[1]
    slot_count = neighbours.shape[0]
    hidden = w_self.shape[1]
    my_index = lax.axis_index("dom")
    fresh_flag = (staleness >= LIMIT).astype(jnp.int32)
    my_fresh = fresh_flag[my_index]
    own_cache = lax.dynamic_slice_in_dim(cached_embed, my_index * part_rows, part_rows, 1)
    own_source = jnp.where(my_fresh == 1, features, own_cache)
    col_inputs = jnp.concatenate([features, w_self, w_nbr, cotangent], axis=0)
    bias_block = jnp.zeros((8, 128), jnp.float32).at[0, : sage_bias.shape[0]].set(sage_bias)
    blocks = exchange(own_source, 0, "dom", n_dom, bcast=True)
    sources = blocks.transpose(1, 0, 2).reshape(col_width, n_dom * part_rows)
    local_slot = jnp.arange(part_rows, dtype=jnp.int32)
    live_rows = (local_slot < node_counts[my_index]).astype(jnp.float32)
    slot_index = jnp.arange(slot_count, dtype=jnp.int32)
    used = (slot_index[:, None] < degrees[None, :]).astype(jnp.float32)
    weights = used * (live_rows / degrees.astype(jnp.float32))[None, :]
    gathered = sources[:, neighbours].astype(jnp.float32)
    aggregated = jnp.sum(weights[None, :, :] * gathered, axis=1).astype(jnp.bfloat16)
    col_blocks, bias_blocks = exchange_many(
        1,
        [
            (jnp.concatenate([aggregated, col_inputs], axis=0), "col", n_col, ((n_col, 1),), True, False, 0),
            (bias_block, "col", n_col, ((n_col, 1),), True, False, 0),
        ],
    )
    agg_full = col_blocks[:, :col_width].reshape(n_col * col_width, part_rows)
    col_blocks = col_blocks[:, col_width:]
    feat_full = col_blocks[:, :col_width].reshape(n_col * col_width, part_rows)
    w_self_full = col_blocks[:, col_width : 2 * col_width].reshape(n_col * col_width, hidden)
    w_nbr_full = col_blocks[:, 2 * col_width : 3 * col_width].reshape(n_col * col_width, hidden)
    cot_full = col_blocks[:, 3 * col_width :].reshape(hidden, part_rows)
    bias_full = bias_blocks[:, 0, : sage_bias.shape[0]].reshape(hidden)
    pre_full = (
        left_product(w_self_full, feat_full)
        + left_product(w_nbr_full, agg_full)
        + bias_full[:, None]
    )
    sig_full = 1.0 / (1.0 + jnp.exp(-pre_full))
    my_col = lax.axis_index("col")
    block_rows = hidden // n_col
    pre_act = lax.dynamic_slice_in_dim(pre_full, my_col * block_rows, block_rows, 0)
    sigmoid = lax.dynamic_slice_in_dim(sig_full, my_col * block_rows, block_rows, 0)
    activation = (live_rows[None, :] * pre_act * sigmoid).astype(jnp.bfloat16)
    grad_full = (
        live_rows[None, :]
        * cot_full.astype(jnp.float32)
        * sig_full
        * (1.0 + pre_full * (1.0 - sig_full))
    ).astype(jnp.bfloat16)
    grad_pre = lax.dynamic_slice_in_dim(grad_full, my_col * block_rows, block_rows, 0)
    self_part = right_product(features, grad_full)
    nbr_part = right_product(aggregated, grad_full)
    bias_part = jnp.sum(grad_pre.astype(jnp.float32), axis=1)
    bias_rows = jnp.zeros((8, hidden), jnp.float32).at[0, : bias_part.shape[0]].set(bias_part)
    packed = jnp.concatenate([self_part, nbr_part, bias_rows], axis=0)
    grad_agg = jnp.dot(w_nbr, grad_full, preferred_element_type=jnp.float32).astype(jnp.bfloat16)
    own_term = jnp.dot(w_self, grad_full, preferred_element_type=jnp.float32)
    spread = weights[None, :, :] * grad_agg.astype(jnp.float32)[:, None, :]
    total_rows = cached_embed.shape[1]
    contrib = (
        jnp.zeros((col_width, total_rows), jnp.float32)
        .at[:, neighbours.reshape(-1)]
        .add(spread.reshape(col_width, -1))
    )
    ys = 8 if n_dom % 16 == 0 else 1
    first = ((2, 1), (n_dom // (2 * ys), 2 * ys))
    back, summed = exchange_many(
        5,
        [
            (contrib.astype(jnp.bfloat16), "dom", n_dom, ((n_dom, 1),), False, True, part_rows),
            (packed.astype(jnp.bfloat16), "dom", n_dom // ys, first, True, True, 0, ys, ((ys, 2),)),
        ],
    )
    grad_self = summed[:col_width]
    grad_nbr = summed[col_width : 2 * col_width]
    grad_bias = summed[2 * col_width, : bias_part.shape[0]]
    grad_feat = (own_term + my_fresh.astype(jnp.float32) * back).astype(jnp.bfloat16)
    return (activation, grad_feat, grad_self, grad_nbr, grad_bias)


def solution(mesh):
    placed = (
        P("col", "dom"),
        P("col", None),
        P(),
        P(),
        P(None, "dom"),
        P("dom"),
        P("col", None),
        P("col", None),
        P("col"),
        P("col", "dom"),
    )
    return jax.shard_map(
        per_device,
        mesh=mesh,
        in_specs=placed,
        out_specs=(P("col", "dom"), P("col", "dom"), P("col", None), P("col", None), P("col")),
        check_vma=False,
    )
```

```python
import functools

import jax
import jax.numpy as jnp
from jax import lax
from jax.experimental import pallas as pl
from jax.experimental.pallas import tpu as pltpu
from jax.sharding import PartitionSpec as P

LIMIT = 8
FRESH = 16
MESH = pl.DeviceIdType.MESH


def left_product(weight, data):
    return lax.dot_general(
        weight, data, (((0,), (0,)), ((), ())), preferred_element_type=jnp.float32
    )


def right_product(data, grads):
    return lax.dot_general(
        data, grads, (((1,), (1,)), ((), ())), preferred_element_type=jnp.float32
    )


def group_pos(me, digits):
    pos, scale = 0, 1
    for radix, stride in digits:
        pos = pos + lax.rem(me // stride, radix) * scale
        scale *= radix
    return pos


def group_member(me, pos, j, digits):
    for radix, stride in digits:
        me = me + (lax.rem(j, radix) - lax.rem(pos, radix)) * stride
        j, pos = j // radix, pos // radix
    return me


def exchange_kernel(specs, *refs):
    count = len(specs)
    xs, ys = refs[:count], refs[count : 2 * count]
    scratch = refs[2 * count :]
    barrier = pltpu.get_barrier_semaphore()
    plans = []
    extra = scratch[3 * count :]
    for e, (axis, size, stride, bcast, reduce, lanes, _, _) in enumerate(specs):
        x_ref, y_ref = xs[e], ys[e]
        buf, send_sem, recv_sem = scratch[3 * e : 3 * e + 3]
        me = lax.axis_index(axis)
        pos = group_pos(me, stride)
        plans.append((axis, size, stride, bcast, reduce, lanes, x_ref, y_ref, buf, send_sem, recv_sem, me, pos))

    def member(plan, j):
        stride, me, pos = plan[2], plan[11], plan[12]
        return group_member(me, pos, j, stride)

    def chunk(plan, j):
        bcast, lanes, x_ref = plan[3], plan[5], plan[6]
        if bcast:
            return x_ref
        if lanes:
            return x_ref.at[:, pl.ds(pl.multiple_of(j * lanes, lanes), lanes)]
        return x_ref.at[j]

    def desc(plan, j, slot):
        axis, buf, send_sem, recv_sem = plan[0], plan[8], plan[9], plan[10]
        return pltpu.make_async_remote_copy(
            src_ref=chunk(plan, j),
            dst_ref=buf.at[slot],
            send_sem=send_sem.at[j],
            recv_sem=recv_sem.at[slot],
            device_id={axis: member(plan, j)},
            device_id_type=MESH,
        )

    def each_peer(plan, body):
        size, pos = plan[1], plan[12]

        def step(k, carry):
            body(lax.rem(pos + k, size))
            return carry

        lax.fori_loop(1, size, step, 0)

    seconds = []
    for e, spec in enumerate(specs):
        if spec[6] > 1:
            stage, buf2, send2, recv2 = extra[4 * len(seconds) : 4 * len(seconds) + 4]
            me = plans[e][11]
            second = (spec[0], spec[6], spec[7], True, True, 0, stage, None, buf2, send2, recv2, me,
                      group_pos(me, spec[7]))
            seconds.append((e, second))
    greetings = 0
    for plan in plans + [second for _, second in seconds]:
        each_peer(
            plan,
            lambda j, plan=plan: pl.semaphore_signal(
                barrier, 1, device_id={plan[0]: member(plan, j)}, device_id_type=MESH
            ),
        )
        greetings += plan[1] - 1
    pl.semaphore_wait(barrier, greetings)
    for plan in plans:
        each_peer(plan, lambda j, plan=plan: desc(plan, j, plan[12]).start())
    for plan in plans:
        buf, pos = plan[8], plan[12]
        buf[pos] = chunk(plan, pos)[...]
    for e, second in seconds:
        plan = plans[e]

        def finish_first(j, plan=plan):
            desc(plan, j, plan[12]).wait_send()
            desc(plan, j, j).wait_recv()

        each_peer(plan, finish_first)
        second[6][...] = jnp.sum(plan[8][...].astype(jnp.float32), axis=0).astype(second[6].dtype)
    for e, plan in enumerate(plans):
        if specs[e][6] > 1:
            continue
        for k in range(1, min(plan[1], 9)):
            desc(plan, lax.rem(plan[12] + k, plan[1]), plan[12]).wait_send()
    for _, second in seconds:
        each_peer(second, lambda j, second=second: desc(second, j, second[12]).start())
        second[8][second[12]] = second[6][...]
    for e, plan in enumerate(plans):
        if specs[e][6] > 1:
            continue

        def finish(k, carry, plan=plan):
            j = lax.rem(plan[12] + k, plan[1])
            desc(plan, j, plan[12]).wait_send()
            return carry

        lax.fori_loop(min(plan[1], 9), plan[1], finish, 0)

        def arrive(j, plan=plan):
            desc(plan, j, j).wait_recv()

        each_peer(plan, arrive)
    for _, second in seconds:

        def finish_second(j, second=second):
            desc(second, j, second[12]).wait_send()
            desc(second, j, j).wait_recv()

        each_peer(second, finish_second)
    for e, plan in enumerate(plans):
        reduce, y_ref, buf = plan[4], plan[7], plan[8]
        if specs[e][6] > 1:
            buf = dict(seconds)[e][8]
        if reduce:
            y_ref[...] = jnp.sum(buf[...].astype(jnp.float32), axis=0)
        else:
            y_ref[...] = buf[...]


def exchange_many(ident, jobs):
    specs, out_shapes, scratch, extra = [], [], [], []
    for job in jobs:
        x, axis, size, stride, bcast, reduce, lanes = job[:7]
        size2, stride2 = job[7:] if len(job) > 7 else (1, ((1, 1),))
        if bcast:
            block = x.shape
        elif lanes:
            block = (x.shape[0], lanes)
        else:
            block = x.shape[1:]
        specs.append((axis, size, stride, bcast, reduce, lanes, size2, stride2))
        if size2 > 1:
            extra += [
                pltpu.VMEM(block, x.dtype),
                pltpu.VMEM((size2,) + block, x.dtype),
                pltpu.SemaphoreType.DMA((size2,)),
                pltpu.SemaphoreType.DMA((size2,)),
            ]
        out_shapes.append(
            jax.ShapeDtypeStruct(block if reduce else (size,) + block, jnp.float32 if reduce else x.dtype)
        )
        scratch += [
            pltpu.VMEM((size,) + block, x.dtype),
            pltpu.SemaphoreType.DMA((size,)),
            pltpu.SemaphoreType.DMA((size,)),
        ]
    return pl.pallas_call(
        functools.partial(exchange_kernel, tuple(specs)),
        out_shape=tuple(out_shapes),
        in_specs=[pl.BlockSpec(memory_space=pltpu.VMEM)] * len(jobs),
        out_specs=tuple(pl.BlockSpec(memory_space=pltpu.VMEM) for _ in jobs),
        scratch_shapes=scratch + extra,
        compiler_params=pltpu.CompilerParams(collective_id=ident, has_side_effects=True),
    )(*[job[0] for job in jobs])


def exchange(x, ident, axis, size, stride=None, bcast=False, reduce=False, lanes=0):
    stride = ((size, 1),) if stride is None else stride
    return exchange_many(ident, [(x, axis, size, stride, bcast, reduce, lanes)])[0]


def per_device(
    features,
    cached_embed,
    staleness,
    node_counts,
    neighbours,
    degrees,
    w_self,
    w_nbr,
    sage_bias,
    cotangent,
):
    n_dom = lax.axis_size("dom")
    n_col = lax.axis_size("col")
    col_width = features.shape[0]
    part_rows = features.shape[1]
    slot_count = neighbours.shape[0]
    hidden = w_self.shape[1]
    my_index = lax.axis_index("dom")
    fresh_flag = (staleness >= LIMIT).astype(jnp.int32)
    my_fresh = fresh_flag[my_index]
    own_cache = lax.dynamic_slice_in_dim(cached_embed, my_index * part_rows, part_rows, 1)
    own_source = jnp.where(my_fresh == 1, features, own_cache)
    col_inputs = jnp.concatenate([features, w_self, w_nbr, cotangent], axis=0)
    bias_block = jnp.zeros((8, 128), jnp.float32).at[0, : sage_bias.shape[0]].set(sage_bias)
    blocks = exchange(own_source, 0, "dom", n_dom, bcast=True)
    sources = blocks.transpose(1, 0, 2).reshape(col_width, n_dom * part_rows)
    local_slot = jnp.arange(part_rows, dtype=jnp.int32)
    live_rows = (local_slot < node_counts[my_index]).astype(jnp.float32)
    slot_index = jnp.arange(slot_count, dtype=jnp.int32)
    used = (slot_index[:, None] < degrees[None, :]).astype(jnp.float32)
    weights = used * (live_rows / degrees.astype(jnp.float32))[None, :]
    gathered = sources[:, neighbours].astype(jnp.float32)
    aggregated = jnp.sum(weights[None, :, :] * gathered, axis=1).astype(jnp.bfloat16)
    col_blocks, bias_blocks = exchange_many(
        1,
        [
            (jnp.concatenate([aggregated, col_inputs], axis=0), "col", n_col, ((n_col, 1),), True, False, 0),
            (bias_block, "col", n_col, ((n_col, 1),), True, False, 0),
        ],
    )
    agg_full = col_blocks[:, :col_width].reshape(n_col * col_width, part_rows)
    col_blocks = col_blocks[:, col_width:]
    feat_full = col_blocks[:, :col_width].reshape(n_col * col_width, part_rows)
    w_self_full = col_blocks[:, col_width : 2 * col_width].reshape(n_col * col_width, hidden)
    w_nbr_full = col_blocks[:, 2 * col_width : 3 * col_width].reshape(n_col * col_width, hidden)
    cot_full = col_blocks[:, 3 * col_width :].reshape(hidden, part_rows)
    bias_full = bias_blocks[:, 0, : sage_bias.shape[0]].reshape(hidden)
    pre_full = (
        left_product(w_self_full, feat_full)
        + left_product(w_nbr_full, agg_full)
        + bias_full[:, None]
    )
    sig_full = 1.0 / (1.0 + jnp.exp(-pre_full))
    my_col = lax.axis_index("col")
    block_rows = hidden // n_col
    pre_act = lax.dynamic_slice_in_dim(pre_full, my_col * block_rows, block_rows, 0)
    sigmoid = lax.dynamic_slice_in_dim(sig_full, my_col * block_rows, block_rows, 0)
    activation = (live_rows[None, :] * pre_act * sigmoid).astype(jnp.bfloat16)
    grad_full = (
        live_rows[None, :]
        * cot_full.astype(jnp.float32)
        * sig_full
        * (1.0 + pre_full * (1.0 - sig_full))
    ).astype(jnp.bfloat16)
    grad_pre = lax.dynamic_slice_in_dim(grad_full, my_col * block_rows, block_rows, 0)
    self_part = right_product(features, grad_full)
    nbr_part = right_product(aggregated, grad_full)
    bias_part = jnp.sum(grad_pre.astype(jnp.float32), axis=1)
    bias_rows = jnp.zeros((8, hidden), jnp.float32).at[0, : bias_part.shape[0]].set(bias_part)
    packed = jnp.concatenate([self_part, nbr_part, bias_rows], axis=0)
    grad_agg = jnp.dot(w_nbr, grad_full, preferred_element_type=jnp.float32).astype(jnp.bfloat16)
    own_term = jnp.dot(w_self, grad_full, preferred_element_type=jnp.float32)
    spread = weights[None, :, :] * grad_agg.astype(jnp.float32)[:, None, :]
    fresh_rank = jnp.cumsum(fresh_flag) - 1
    nbr_part = neighbours // part_rows
    compact = jnp.where(
        fresh_flag[nbr_part] == 1,
        fresh_rank[nbr_part] * part_rows + neighbours % part_rows,
        FRESH * part_rows,
    )
    contrib = (
        jnp.zeros((col_width, FRESH * part_rows), jnp.float32)
        .at[:, compact.reshape(-1)]
        .add(spread.reshape(col_width, -1), mode="drop")
    )
    padded = jnp.concatenate(
        [contrib.astype(jnp.bfloat16), jnp.zeros((col_width, part_rows), jnp.bfloat16)], axis=1
    ).reshape(col_width, FRESH + 1, part_rows)
    block_of = jnp.where(fresh_flag == 1, fresh_rank, FRESH)
    contrib = jnp.take(padded, block_of, axis=1).reshape(col_width, n_dom * part_rows)
    ys = 8 if n_dom % 16 == 0 else 1
    first = ((2, 1), (n_dom // (2 * ys), 2 * ys))
    back, summed = exchange_many(
        5,
        [
            (contrib, "dom", n_dom, ((n_dom, 1),), False, True, part_rows),
            (packed.astype(jnp.bfloat16), "dom", n_dom // ys, first, True, True, 0, ys, ((ys, 2),)),
        ],
    )
    grad_self = summed[:col_width]
    grad_nbr = summed[col_width : 2 * col_width]
    grad_bias = summed[2 * col_width, : bias_part.shape[0]]
    grad_feat = (own_term + my_fresh.astype(jnp.float32) * back).astype(jnp.bfloat16)
    return (activation, grad_feat, grad_self, grad_nbr, grad_bias)


def solution(mesh):
    placed = (
        P("col", "dom"),
        P("col", None),
        P(),
        P(),
        P(None, "dom"),
        P("dom"),
        P("col", None),
        P("col", None),
        P("col"),
        P("col", "dom"),
    )
    return jax.shard_map(
        per_device,
        mesh=mesh,
        in_specs=placed,
        out_specs=(P("col", "dom"), P("col", "dom"), P("col", None), P("col", None), P("col")),
        check_vma=False,
    )
```

```python
import functools

import jax
import jax.numpy as jnp
from jax import lax
from jax.experimental import pallas as pl
from jax.experimental.pallas import tpu as pltpu
from jax.sharding import PartitionSpec as P

LIMIT = 8
FRESH = 16
MESH = pl.DeviceIdType.MESH


def left_product(weight, data):
    return lax.dot_general(
        weight, data, (((0,), (0,)), ((), ())), preferred_element_type=jnp.float32
    )


def right_product(data, grads):
    return lax.dot_general(
        data, grads, (((1,), (1,)), ((), ())), preferred_element_type=jnp.float32
    )


def group_pos(me, digits):
    pos, scale = 0, 1
    for radix, stride in digits:
        pos = pos + lax.rem(me // stride, radix) * scale
        scale *= radix
    return pos


def group_member(me, pos, j, digits):
    for radix, stride in digits:
        me = me + (lax.rem(j, radix) - lax.rem(pos, radix)) * stride
        j, pos = j // radix, pos // radix
    return me


def exchange_kernel(specs, *refs):
    count = len(specs)
    xs, ys = refs[:count], refs[count : 2 * count]
    scratch = refs[2 * count :]
    barrier = pltpu.get_barrier_semaphore()
    plans = []
    extra = scratch[3 * count :]
    for e, (axis, size, stride, bcast, reduce, lanes, _, _) in enumerate(specs):
        x_ref, y_ref = xs[e], ys[e]
        buf, send_sem, recv_sem = scratch[3 * e : 3 * e + 3]
        me = lax.axis_index(axis)
        pos = group_pos(me, stride)
        plans.append((axis, size, stride, bcast, reduce, lanes, x_ref, y_ref, buf, send_sem, recv_sem, me, pos))

    def member(plan, j):
        stride, me, pos = plan[2], plan[11], plan[12]
        return group_member(me, pos, j, stride)

    def chunk(plan, j):
        bcast, lanes, x_ref = plan[3], plan[5], plan[6]
        if bcast:
            return x_ref
        if lanes:
            return x_ref.at[:, pl.ds(pl.multiple_of(j * lanes, lanes), lanes)]
        return x_ref.at[j]

    def desc(plan, j, slot):
        axis, buf, send_sem, recv_sem = plan[0], plan[8], plan[9], plan[10]
        return pltpu.make_async_remote_copy(
            src_ref=chunk(plan, j),
            dst_ref=buf.at[slot],
            send_sem=send_sem.at[j],
            recv_sem=recv_sem.at[slot],
            device_id={axis: member(plan, j)},
            device_id_type=MESH,
        )

    def each_peer(plan, body):
        size, pos = plan[1], plan[12]

        def step(k, carry):
            body(lax.rem(pos + k, size))
            return carry

        lax.fori_loop(1, size, step, 0)

    seconds = []
    for e, spec in enumerate(specs):
        if spec[6] > 1:
            stage, buf2, send2, recv2 = extra[4 * len(seconds) : 4 * len(seconds) + 4]
            me = plans[e][11]
            second = (spec[0], spec[6], spec[7], True, True, 0, stage, None, buf2, send2, recv2, me,
                      group_pos(me, spec[7]))
            seconds.append((e, second))
    greetings = 0
    for plan in plans + [second for _, second in seconds]:
        each_peer(
            plan,
            lambda j, plan=plan: pl.semaphore_signal(
                barrier, 1, device_id={plan[0]: member(plan, j)}, device_id_type=MESH
            ),
        )
        greetings += plan[1] - 1
    pl.semaphore_wait(barrier, greetings)
    for plan in plans:
        each_peer(plan, lambda j, plan=plan: desc(plan, j, plan[12]).start())
    for plan in plans:
        buf, pos = plan[8], plan[12]
        buf[pos] = chunk(plan, pos)[...]
    for e, second in seconds:
        plan = plans[e]

        def finish_first(j, plan=plan):
            desc(plan, j, plan[12]).wait_send()
            desc(plan, j, j).wait_recv()

        each_peer(plan, finish_first)
        second[6][...] = jnp.sum(plan[8][...].astype(jnp.float32), axis=0).astype(second[6].dtype)
    for e, plan in enumerate(plans):
        if specs[e][6] > 1:
            continue
        for k in range(1, min(plan[1], 9)):
            desc(plan, lax.rem(plan[12] + k, plan[1]), plan[12]).wait_send()
    for _, second in seconds:
        each_peer(second, lambda j, second=second: desc(second, j, second[12]).start())
        second[8][second[12]] = second[6][...]
    for e, plan in enumerate(plans):
        if specs[e][6] > 1:
            continue

        def finish(k, carry, plan=plan):
            j = lax.rem(plan[12] + k, plan[1])
            desc(plan, j, plan[12]).wait_send()
            return carry

        lax.fori_loop(min(plan[1], 9), plan[1], finish, 0)

        def arrive(j, plan=plan):
            desc(plan, j, j).wait_recv()

        each_peer(plan, arrive)
    for _, second in seconds:

        def finish_second(j, second=second):
            desc(second, j, second[12]).wait_send()
            desc(second, j, j).wait_recv()

        each_peer(second, finish_second)
    for e, plan in enumerate(plans):
        reduce, y_ref, buf = plan[4], plan[7], plan[8]
        if specs[e][6] > 1:
            buf = dict(seconds)[e][8]
        if reduce:
            y_ref[...] = jnp.sum(buf[...].astype(jnp.float32), axis=0)
        else:
            y_ref[...] = buf[...]


def exchange_many(ident, jobs):
    specs, out_shapes, scratch, extra = [], [], [], []
    for job in jobs:
        x, axis, size, stride, bcast, reduce, lanes = job[:7]
        size2, stride2 = job[7:] if len(job) > 7 else (1, ((1, 1),))
        if bcast:
            block = x.shape
        elif lanes:
            block = (x.shape[0], lanes)
        else:
            block = x.shape[1:]
        specs.append((axis, size, stride, bcast, reduce, lanes, size2, stride2))
        if size2 > 1:
            extra += [
                pltpu.VMEM(block, x.dtype),
                pltpu.VMEM((size2,) + block, x.dtype),
                pltpu.SemaphoreType.DMA((size2,)),
                pltpu.SemaphoreType.DMA((size2,)),
            ]
        out_shapes.append(
            jax.ShapeDtypeStruct(block if reduce else (size,) + block, jnp.float32 if reduce else x.dtype)
        )
        scratch += [
            pltpu.VMEM((size,) + block, x.dtype),
            pltpu.SemaphoreType.DMA((size,)),
            pltpu.SemaphoreType.DMA((size,)),
        ]
    return pl.pallas_call(
        functools.partial(exchange_kernel, tuple(specs)),
        out_shape=tuple(out_shapes),
        in_specs=[pl.BlockSpec(memory_space=pltpu.VMEM)] * len(jobs),
        out_specs=tuple(pl.BlockSpec(memory_space=pltpu.VMEM) for _ in jobs),
        scratch_shapes=scratch + extra,
        compiler_params=pltpu.CompilerParams(collective_id=ident, has_side_effects=True),
    )(*[job[0] for job in jobs])


def exchange(x, ident, axis, size, stride=None, bcast=False, reduce=False, lanes=0):
    stride = ((size, 1),) if stride is None else stride
    return exchange_many(ident, [(x, axis, size, stride, bcast, reduce, lanes)])[0]


def per_device(
    features,
    cached_embed,
    staleness,
    node_counts,
    neighbours,
    degrees,
    w_self,
    w_nbr,
    sage_bias,
    cotangent,
):
    n_dom = lax.axis_size("dom")
    n_col = lax.axis_size("col")
    col_width = features.shape[0]
    part_rows = features.shape[1]
    slot_count = neighbours.shape[0]
    hidden = w_self.shape[1]
    my_index = lax.axis_index("dom")
    fresh_flag = (staleness >= LIMIT).astype(jnp.int32)
    my_fresh = fresh_flag[my_index]
    own_cache = lax.dynamic_slice_in_dim(cached_embed, my_index * part_rows, part_rows, 1)
    own_source = jnp.where(my_fresh == 1, features, own_cache)
    col_inputs = jnp.concatenate([features, w_self, w_nbr, cotangent], axis=0)
    bias_block = jnp.zeros((8, 128), jnp.float32).at[0, : sage_bias.shape[0]].set(sage_bias)
    blocks = exchange(own_source, 0, "dom", n_dom, bcast=True)
    sources = blocks.transpose(1, 0, 2).reshape(col_width, n_dom * part_rows)
    local_slot = jnp.arange(part_rows, dtype=jnp.int32)
    live_rows = (local_slot < node_counts[my_index]).astype(jnp.float32)
    slot_index = jnp.arange(slot_count, dtype=jnp.int32)
    used = (slot_index[:, None] < degrees[None, :]).astype(jnp.float32)
    weights = used * (live_rows / degrees.astype(jnp.float32))[None, :]
    gathered = sources[:, neighbours].astype(jnp.float32)
    aggregated = jnp.sum(weights[None, :, :] * gathered, axis=1).astype(jnp.bfloat16)
    col_blocks, bias_blocks = exchange_many(
        1,
        [
            (jnp.concatenate([aggregated, col_inputs], axis=0), "col", n_col, ((n_col, 1),), True, False, 0),
            (bias_block, "col", n_col, ((n_col, 1),), True, False, 0),
        ],
    )
    agg_full = col_blocks[:, :col_width].reshape(n_col * col_width, part_rows)
    col_blocks = col_blocks[:, col_width:]
    feat_full = col_blocks[:, :col_width].reshape(n_col * col_width, part_rows)
    w_self_full = col_blocks[:, col_width : 2 * col_width].reshape(n_col * col_width, hidden)
    w_nbr_full = col_blocks[:, 2 * col_width : 3 * col_width].reshape(n_col * col_width, hidden)
    cot_full = col_blocks[:, 3 * col_width :].reshape(hidden, part_rows)
    bias_full = bias_blocks[:, 0, : sage_bias.shape[0]].reshape(hidden)
    pre_full = (
        left_product(w_self_full, feat_full)
        + left_product(w_nbr_full, agg_full)
        + bias_full[:, None]
    )
    sig_full = 1.0 / (1.0 + jnp.exp(-pre_full))
    my_col = lax.axis_index("col")
    block_rows = hidden // n_col
    pre_act = lax.dynamic_slice_in_dim(pre_full, my_col * block_rows, block_rows, 0)
    sigmoid = lax.dynamic_slice_in_dim(sig_full, my_col * block_rows, block_rows, 0)
    activation = (live_rows[None, :] * pre_act * sigmoid).astype(jnp.bfloat16)
    grad_full = (
        live_rows[None, :]
        * cot_full.astype(jnp.float32)
        * sig_full
        * (1.0 + pre_full * (1.0 - sig_full))
    ).astype(jnp.bfloat16)
    grad_pre = lax.dynamic_slice_in_dim(grad_full, my_col * block_rows, block_rows, 0)
    self_part = right_product(features, grad_full)
    nbr_part = right_product(aggregated, grad_full)
    bias_part = jnp.sum(grad_pre.astype(jnp.float32), axis=1)
    bias_rows = jnp.zeros((8, hidden), jnp.float32).at[0, : bias_part.shape[0]].set(bias_part)
    packed = jnp.concatenate([self_part, nbr_part, bias_rows], axis=0)
    grad_agg = jnp.dot(w_nbr, grad_full, preferred_element_type=jnp.float32).astype(jnp.bfloat16)
    own_term = jnp.dot(w_self, grad_full, preferred_element_type=jnp.float32)
    spread = weights[None, :, :] * grad_agg.astype(jnp.float32)[:, None, :]
    fresh_rank = jnp.cumsum(fresh_flag) - 1
    nbr_part = neighbours // part_rows
    owner = nbr_part[:, :, None] == jnp.arange(n_dom, dtype=jnp.int32)
    nbr_fresh = jnp.sum(jnp.where(owner, fresh_flag, 0), axis=2)
    nbr_rank = jnp.sum(jnp.where(owner, fresh_rank, 0), axis=2)
    compact = jnp.where(
        nbr_fresh == 1,
        nbr_rank * part_rows + neighbours % part_rows,
        FRESH * part_rows,
    )
    contrib = (
        jnp.zeros((col_width, FRESH * part_rows), jnp.float32)
        .at[:, compact.reshape(-1)]
        .add(spread.reshape(col_width, -1), mode="drop")
    )
    padded = jnp.concatenate(
        [contrib.astype(jnp.bfloat16), jnp.zeros((col_width, part_rows), jnp.bfloat16)], axis=1
    ).reshape(col_width, FRESH + 1, part_rows)
    block_of = jnp.where(fresh_flag == 1, fresh_rank, FRESH)
    contrib = jnp.take(padded, block_of, axis=1).reshape(col_width, n_dom * part_rows)
    ys = 8 if n_dom % 16 == 0 else 1
    first = ((2, 1), (n_dom // (2 * ys), 2 * ys))
    back, summed = exchange_many(
        5,
        [
            (contrib, "dom", n_dom, ((n_dom, 1),), False, True, part_rows),
            (packed.astype(jnp.bfloat16), "dom", n_dom // ys, first, True, True, 0, ys, ((ys, 2),)),
        ],
    )
    grad_self = summed[:col_width]
    grad_nbr = summed[col_width : 2 * col_width]
    grad_bias = summed[2 * col_width, : bias_part.shape[0]]
    grad_feat = (own_term + my_fresh.astype(jnp.float32) * back).astype(jnp.bfloat16)
    return (activation, grad_feat, grad_self, grad_nbr, grad_bias)


def solution(mesh):
    placed = (
        P("col", "dom"),
        P("col", None),
        P(),
        P(),
        P(None, "dom"),
        P("dom"),
        P("col", None),
        P("col", None),
        P("col"),
        P("col", "dom"),
    )
    return jax.shard_map(
        per_device,
        mesh=mesh,
        in_specs=placed,
        out_specs=(P("col", "dom"), P("col", "dom"), P("col", None), P("col", None), P("col")),
        check_vma=False,
    )
```

```python
import functools

import jax
import jax.numpy as jnp
from jax import lax
from jax.experimental import pallas as pl
from jax.experimental.pallas import tpu as pltpu
from jax.sharding import PartitionSpec as P

LIMIT = 8
FRESH = 16
MESH = pl.DeviceIdType.MESH


def left_product(weight, data):
    return lax.dot_general(
        weight, data, (((0,), (0,)), ((), ())), preferred_element_type=jnp.float32
    )


def right_product(data, grads):
    return lax.dot_general(
        data, grads, (((1,), (1,)), ((), ())), preferred_element_type=jnp.float32
    )


def group_pos(me, digits):
    pos, scale = 0, 1
    for radix, stride in digits:
        pos = pos + lax.rem(me // stride, radix) * scale
        scale *= radix
    return pos


def group_member(me, pos, j, digits):
    for radix, stride in digits:
        me = me + (lax.rem(j, radix) - lax.rem(pos, radix)) * stride
        j, pos = j // radix, pos // radix
    return me


def exchange_kernel(specs, *refs):
    count = len(specs)
    xs, ys = refs[:count], refs[count : 2 * count]
    scratch = refs[2 * count :]
    barrier = pltpu.get_barrier_semaphore()
    plans = []
    extra = scratch[3 * count :]
    for e, (axis, size, stride, bcast, reduce, lanes, _, _) in enumerate(specs):
        x_ref, y_ref = xs[e], ys[e]
        buf, send_sem, recv_sem = scratch[3 * e : 3 * e + 3]
        me = lax.axis_index(axis)
        pos = group_pos(me, stride)
        plans.append((axis, size, stride, bcast, reduce, lanes, x_ref, y_ref, buf, send_sem, recv_sem, me, pos))

    def member(plan, j):
        stride, me, pos = plan[2], plan[11], plan[12]
        return group_member(me, pos, j, stride)

    def chunk(plan, j):
        bcast, lanes, x_ref = plan[3], plan[5], plan[6]
        if bcast:
            return x_ref
        if lanes:
            return x_ref.at[:, pl.ds(pl.multiple_of(j * lanes, lanes), lanes)]
        return x_ref.at[j]

    def desc(plan, j, slot):
        axis, buf, send_sem, recv_sem = plan[0], plan[8], plan[9], plan[10]
        return pltpu.make_async_remote_copy(
            src_ref=chunk(plan, j),
            dst_ref=buf.at[slot],
            send_sem=send_sem.at[j],
            recv_sem=recv_sem.at[slot],
            device_id={axis: member(plan, j)},
            device_id_type=MESH,
        )

    def each_peer(plan, body):
        size, pos = plan[1], plan[12]

        def step(k, carry):
            body(lax.rem(pos + k, size))
            return carry

        lax.fori_loop(1, size, step, 0)

    seconds = []
    for e, spec in enumerate(specs):
        if spec[6] > 1:
            stage, buf2, send2, recv2 = extra[4 * len(seconds) : 4 * len(seconds) + 4]
            me = plans[e][11]
            second = (spec[0], spec[6], spec[7], True, True, 0, stage, None, buf2, send2, recv2, me,
                      group_pos(me, spec[7]))
            seconds.append((e, second))
    greetings = 0
    for plan in plans + [second for _, second in seconds]:
        each_peer(
            plan,
            lambda j, plan=plan: pl.semaphore_signal(
                barrier, 1, device_id={plan[0]: member(plan, j)}, device_id_type=MESH
            ),
        )
        greetings += plan[1] - 1
    pl.semaphore_wait(barrier, greetings)
    for plan in plans:
        each_peer(plan, lambda j, plan=plan: desc(plan, j, plan[12]).start())
    for plan in plans:
        buf, pos = plan[8], plan[12]
        buf[pos] = chunk(plan, pos)[...]
    for e, second in seconds:
        plan = plans[e]

        def finish_first(j, plan=plan):
            desc(plan, j, plan[12]).wait_send()
            desc(plan, j, j).wait_recv()

        each_peer(plan, finish_first)
        second[6][...] = jnp.sum(plan[8][...].astype(jnp.float32), axis=0).astype(second[6].dtype)
    for e, plan in enumerate(plans):
        if specs[e][6] > 1:
            continue
        for k in range(1, min(plan[1], 9)):
            desc(plan, lax.rem(plan[12] + k, plan[1]), plan[12]).wait_send()
    for _, second in seconds:
        each_peer(second, lambda j, second=second: desc(second, j, second[12]).start())
        second[8][second[12]] = second[6][...]
    for e, plan in enumerate(plans):
        if specs[e][6] > 1:
            continue

        def finish(k, carry, plan=plan):
            j = lax.rem(plan[12] + k, plan[1])
            desc(plan, j, plan[12]).wait_send()
            return carry

        lax.fori_loop(min(plan[1], 9), plan[1], finish, 0)

        def arrive(j, plan=plan):
            desc(plan, j, j).wait_recv()

        each_peer(plan, arrive)
    for _, second in seconds:

        def finish_second(j, second=second):
            desc(second, j, second[12]).wait_send()
            desc(second, j, j).wait_recv()

        each_peer(second, finish_second)
    for e, plan in enumerate(plans):
        reduce, y_ref, buf = plan[4], plan[7], plan[8]
        if specs[e][6] > 1:
            buf = dict(seconds)[e][8]
        if reduce:
            y_ref[...] = jnp.sum(buf[...].astype(jnp.float32), axis=0)
        else:
            y_ref[...] = buf[...]


def exchange_many(ident, jobs):
    specs, out_shapes, scratch, extra = [], [], [], []
    for job in jobs:
        x, axis, size, stride, bcast, reduce, lanes = job[:7]
        size2, stride2 = job[7:] if len(job) > 7 else (1, ((1, 1),))
        if bcast:
            block = x.shape
        elif lanes:
            block = (x.shape[0], lanes)
        else:
            block = x.shape[1:]
        specs.append((axis, size, stride, bcast, reduce, lanes, size2, stride2))
        if size2 > 1:
            extra += [
                pltpu.VMEM(block, x.dtype),
                pltpu.VMEM((size2,) + block, x.dtype),
                pltpu.SemaphoreType.DMA((size2,)),
                pltpu.SemaphoreType.DMA((size2,)),
            ]
        out_shapes.append(
            jax.ShapeDtypeStruct(block if reduce else (size,) + block, jnp.float32 if reduce else x.dtype)
        )
        scratch += [
            pltpu.VMEM((size,) + block, x.dtype),
            pltpu.SemaphoreType.DMA((size,)),
            pltpu.SemaphoreType.DMA((size,)),
        ]
    return pl.pallas_call(
        functools.partial(exchange_kernel, tuple(specs)),
        out_shape=tuple(out_shapes),
        in_specs=[pl.BlockSpec(memory_space=pltpu.VMEM)] * len(jobs),
        out_specs=tuple(pl.BlockSpec(memory_space=pltpu.VMEM) for _ in jobs),
        scratch_shapes=scratch + extra,
        compiler_params=pltpu.CompilerParams(collective_id=ident, has_side_effects=True),
    )(*[job[0] for job in jobs])


def exchange(x, ident, axis, size, stride=None, bcast=False, reduce=False, lanes=0):
    stride = ((size, 1),) if stride is None else stride
    return exchange_many(ident, [(x, axis, size, stride, bcast, reduce, lanes)])[0]


def per_device(
    features,
    cached_embed,
    staleness,
    node_counts,
    neighbours,
    degrees,
    w_self,
    w_nbr,
    sage_bias,
    cotangent,
):
    n_dom = lax.axis_size("dom")
    n_col = lax.axis_size("col")
    col_width = features.shape[0]
    part_rows = features.shape[1]
    slot_count = neighbours.shape[0]
    hidden = w_self.shape[1]
    my_index = lax.axis_index("dom")
    fresh_flag = (staleness >= LIMIT).astype(jnp.int32)
    my_fresh = fresh_flag[my_index]
    own_cache = lax.dynamic_slice_in_dim(cached_embed, my_index * part_rows, part_rows, 1)
    own_source = jnp.where(my_fresh == 1, features, own_cache)
    col_inputs = jnp.concatenate([features, w_self, w_nbr, cotangent], axis=0)
    bias_block = jnp.zeros((8, 128), jnp.float32).at[0, : sage_bias.shape[0]].set(sage_bias)
    blocks = exchange(own_source, 0, "dom", n_dom, bcast=True)
    sources = blocks.transpose(1, 0, 2).reshape(col_width, n_dom * part_rows)
    local_slot = jnp.arange(part_rows, dtype=jnp.int32)
    live_rows = (local_slot < node_counts[my_index]).astype(jnp.float32)
    slot_index = jnp.arange(slot_count, dtype=jnp.int32)
    used = (slot_index[:, None] < degrees[None, :]).astype(jnp.float32)
    weights = used * (live_rows / degrees.astype(jnp.float32))[None, :]
    gathered = sources[:, neighbours].astype(jnp.float32)
    aggregated = jnp.sum(weights[None, :, :] * gathered, axis=1).astype(jnp.bfloat16)
    col_blocks, bias_blocks = exchange_many(
        1,
        [
            (jnp.concatenate([aggregated, col_inputs], axis=0), "col", n_col, ((n_col, 1),), True, False, 0),
            (bias_block, "col", n_col, ((n_col, 1),), True, False, 0),
        ],
    )
    agg_full = col_blocks[:, :col_width].reshape(n_col * col_width, part_rows)
    col_blocks = col_blocks[:, col_width:]
    feat_full = col_blocks[:, :col_width].reshape(n_col * col_width, part_rows)
    w_self_full = col_blocks[:, col_width : 2 * col_width].reshape(n_col * col_width, hidden)
    w_nbr_full = col_blocks[:, 2 * col_width : 3 * col_width].reshape(n_col * col_width, hidden)
    cot_full = col_blocks[:, 3 * col_width :].reshape(hidden, part_rows)
    bias_full = bias_blocks[:, 0, : sage_bias.shape[0]].reshape(hidden)
    pre_full = (
        left_product(w_self_full, feat_full)
        + left_product(w_nbr_full, agg_full)
        + bias_full[:, None]
    )
    sig_full = 1.0 / (1.0 + jnp.exp(-pre_full))
    my_col = lax.axis_index("col")
    block_rows = hidden // n_col
    pre_act = lax.dynamic_slice_in_dim(pre_full, my_col * block_rows, block_rows, 0)
    sigmoid = lax.dynamic_slice_in_dim(sig_full, my_col * block_rows, block_rows, 0)
    activation = (live_rows[None, :] * pre_act * sigmoid).astype(jnp.bfloat16)
    grad_full = (
        live_rows[None, :]
        * cot_full.astype(jnp.float32)
        * sig_full
        * (1.0 + pre_full * (1.0 - sig_full))
    ).astype(jnp.bfloat16)
    grad_pre = lax.dynamic_slice_in_dim(grad_full, my_col * block_rows, block_rows, 0)
    self_part = right_product(features, grad_full)
    nbr_part = right_product(aggregated, grad_full)
    bias_part = jnp.sum(grad_pre.astype(jnp.float32), axis=1)
    bias_rows = jnp.zeros((8, hidden), jnp.float32).at[0, : bias_part.shape[0]].set(bias_part)
    packed = jnp.concatenate([self_part, nbr_part, bias_rows], axis=0)
    grad_agg = jnp.dot(w_nbr, grad_full, preferred_element_type=jnp.float32).astype(jnp.bfloat16)
    own_term = jnp.dot(w_self, grad_full, preferred_element_type=jnp.float32)
    spread = weights[None, :, :] * grad_agg.astype(jnp.float32)[:, None, :]
    fresh_rank = jnp.cumsum(fresh_flag) - 1
    nbr_part = neighbours // part_rows
    owner = nbr_part[:, :, None] == jnp.arange(n_dom, dtype=jnp.int32)
    nbr_fresh = jnp.sum(jnp.where(owner, fresh_flag, 0), axis=2)
    nbr_rank = jnp.sum(jnp.where(owner, fresh_rank, 0), axis=2)
    compact = jnp.where(
        nbr_fresh == 1,
        nbr_rank * part_rows + neighbours % part_rows,
        FRESH * part_rows,
    )
    contrib = (
        jnp.zeros((col_width, FRESH * part_rows), jnp.float32)
        .at[:, compact.reshape(-1)]
        .add(spread.reshape(col_width, -1), mode="drop")
    )
    padded = jnp.concatenate(
        [contrib.astype(jnp.bfloat16), jnp.zeros((col_width, part_rows), jnp.bfloat16)], axis=1
    ).reshape(col_width, FRESH + 1, part_rows)
    block_of = jnp.where(fresh_flag == 1, fresh_rank, FRESH)
    contrib = jnp.take(padded, block_of, axis=1).reshape(col_width, n_dom * part_rows)
    ys = 8 if n_dom % 16 == 0 else 1
    first = ((2, 1), (n_dom // (2 * ys), 2 * ys))
    summed, back = exchange_many(
        5,
        [
            (packed.astype(jnp.bfloat16), "dom", n_dom // ys, first, True, True, 0, ys, ((ys, 2),)),
            (contrib, "dom", n_dom, ((n_dom, 1),), False, True, part_rows),
        ],
    )
    grad_self = summed[:col_width]
    grad_nbr = summed[col_width : 2 * col_width]
    grad_bias = summed[2 * col_width, : bias_part.shape[0]]
    grad_feat = (own_term + my_fresh.astype(jnp.float32) * back).astype(jnp.bfloat16)
    return (activation, grad_feat, grad_self, grad_nbr, grad_bias)


def solution(mesh):
    placed = (
        P("col", "dom"),
        P("col", None),
        P(),
        P(),
        P(None, "dom"),
        P("dom"),
        P("col", None),
        P("col", None),
        P("col"),
        P("col", "dom"),
    )
    return jax.shard_map(
        per_device,
        mesh=mesh,
        in_specs=placed,
        out_specs=(P("col", "dom"), P("col", "dom"), P("col", None), P("col", None), P("col")),
        check_vma=False,
    )
```

```python
import functools

import jax
import jax.numpy as jnp
from jax import lax
from jax.experimental import pallas as pl
from jax.experimental.pallas import tpu as pltpu
from jax.sharding import PartitionSpec as P

LIMIT = 8
FRESH = 16
MESH = pl.DeviceIdType.MESH


def left_product(weight, data):
    return lax.dot_general(
        weight, data, (((0,), (0,)), ((), ())), preferred_element_type=jnp.float32
    )


def right_product(data, grads):
    return lax.dot_general(
        data, grads, (((1,), (1,)), ((), ())), preferred_element_type=jnp.float32
    )


def group_pos(me, digits):
    pos, scale = 0, 1
    for radix, stride in digits:
        pos = pos + lax.rem(me // stride, radix) * scale
        scale *= radix
    return pos


def group_member(me, pos, j, digits):
    for radix, stride in digits:
        me = me + (lax.rem(j, radix) - lax.rem(pos, radix)) * stride
        j, pos = j // radix, pos // radix
    return me


def exchange_kernel(specs, *refs):
    count = len(specs)
    xs, ys = refs[:count], refs[count : 2 * count]
    scratch = refs[2 * count :]
    barrier = pltpu.get_barrier_semaphore()
    plans = []
    extra = scratch[3 * count :]
    for e, (axis, size, stride, bcast, reduce, lanes, _, _) in enumerate(specs):
        x_ref, y_ref = xs[e], ys[e]
        buf, send_sem, recv_sem = scratch[3 * e : 3 * e + 3]
        me = lax.axis_index(axis)
        pos = group_pos(me, stride)
        plans.append((axis, size, stride, bcast, reduce, lanes, x_ref, y_ref, buf, send_sem, recv_sem, me, pos))

    def member(plan, j):
        stride, me, pos = plan[2], plan[11], plan[12]
        return group_member(me, pos, j, stride)

    def chunk(plan, j):
        bcast, lanes, x_ref = plan[3], plan[5], plan[6]
        if bcast:
            return x_ref
        if lanes:
            return x_ref.at[:, pl.ds(pl.multiple_of(j * lanes, lanes), lanes)]
        return x_ref.at[j]

    def desc(plan, j, slot):
        axis, buf, send_sem, recv_sem = plan[0], plan[8], plan[9], plan[10]
        return pltpu.make_async_remote_copy(
            src_ref=chunk(plan, j),
            dst_ref=buf.at[slot],
            send_sem=send_sem.at[j],
            recv_sem=recv_sem.at[slot],
            device_id={axis: member(plan, j)},
            device_id_type=MESH,
        )

    def each_peer(plan, body):
        size, pos = plan[1], plan[12]

        def step(k, carry):
            body(lax.rem(pos + k, size))
            return carry

        lax.fori_loop(1, size, step, 0)

    seconds = []
    for e, spec in enumerate(specs):
        if spec[6] > 1:
            stage, buf2, send2, recv2 = extra[4 * len(seconds) : 4 * len(seconds) + 4]
            me = plans[e][11]
            second = (spec[0], spec[6], spec[7], True, True, 0, stage, None, buf2, send2, recv2, me,
                      group_pos(me, spec[7]))
            seconds.append((e, second))
    greetings = 0
    for plan in plans + [second for _, second in seconds]:
        each_peer(
            plan,
            lambda j, plan=plan: pl.semaphore_signal(
                barrier, 1, device_id={plan[0]: member(plan, j)}, device_id_type=MESH
            ),
        )
        greetings += plan[1] - 1
    pl.semaphore_wait(barrier, greetings)
    for plan in plans:
        each_peer(plan, lambda j, plan=plan: desc(plan, j, plan[12]).start())
    for plan in plans:
        buf, pos = plan[8], plan[12]
        buf[pos] = chunk(plan, pos)[...]
    for e, second in seconds:
        plan = plans[e]

        def finish_first(j, plan=plan):
            desc(plan, j, plan[12]).wait_send()
            desc(plan, j, j).wait_recv()

        each_peer(plan, finish_first)
        second[6][...] = jnp.sum(plan[8][...].astype(jnp.float32), axis=0).astype(second[6].dtype)
    for e, plan in enumerate(plans):
        if specs[e][6] > 1:
            continue
        for k in range(1, min(plan[1], 3)):
            desc(plan, lax.rem(plan[12] + k, plan[1]), plan[12]).wait_send()
    for _, second in seconds:
        each_peer(second, lambda j, second=second: desc(second, j, second[12]).start())
        second[8][second[12]] = second[6][...]
    for e, plan in enumerate(plans):
        if specs[e][6] > 1:
            continue

        def finish(k, carry, plan=plan):
            j = lax.rem(plan[12] + k, plan[1])
            desc(plan, j, plan[12]).wait_send()
            return carry

        lax.fori_loop(min(plan[1], 3), plan[1], finish, 0)

        def arrive(j, plan=plan):
            desc(plan, j, j).wait_recv()

        each_peer(plan, arrive)
    for _, second in seconds:

        def finish_second(j, second=second):
            desc(second, j, second[12]).wait_send()
            desc(second, j, j).wait_recv()

        each_peer(second, finish_second)
    for e, plan in enumerate(plans):
        reduce, y_ref, buf = plan[4], plan[7], plan[8]
        if specs[e][6] > 1:
            buf = dict(seconds)[e][8]
        if reduce:
            y_ref[...] = jnp.sum(buf[...].astype(jnp.float32), axis=0)
        else:
            y_ref[...] = buf[...]


def exchange_many(ident, jobs):
    specs, out_shapes, scratch, extra = [], [], [], []
    for job in jobs:
        x, axis, size, stride, bcast, reduce, lanes = job[:7]
        size2, stride2 = job[7:] if len(job) > 7 else (1, ((1, 1),))
        if bcast:
            block = x.shape
        elif lanes:
            block = (x.shape[0], lanes)
        else:
            block = x.shape[1:]
        specs.append((axis, size, stride, bcast, reduce, lanes, size2, stride2))
        if size2 > 1:
            extra += [
                pltpu.VMEM(block, x.dtype),
                pltpu.VMEM((size2,) + block, x.dtype),
                pltpu.SemaphoreType.DMA((size2,)),
                pltpu.SemaphoreType.DMA((size2,)),
            ]
        out_shapes.append(
            jax.ShapeDtypeStruct(block if reduce else (size,) + block, jnp.float32 if reduce else x.dtype)
        )
        scratch += [
            pltpu.VMEM((size,) + block, x.dtype),
            pltpu.SemaphoreType.DMA((size,)),
            pltpu.SemaphoreType.DMA((size,)),
        ]
    return pl.pallas_call(
        functools.partial(exchange_kernel, tuple(specs)),
        out_shape=tuple(out_shapes),
        in_specs=[pl.BlockSpec(memory_space=pltpu.VMEM)] * len(jobs),
        out_specs=tuple(pl.BlockSpec(memory_space=pltpu.VMEM) for _ in jobs),
        scratch_shapes=scratch + extra,
        compiler_params=pltpu.CompilerParams(collective_id=ident, has_side_effects=True),
    )(*[job[0] for job in jobs])


def exchange(x, ident, axis, size, stride=None, bcast=False, reduce=False, lanes=0):
    stride = ((size, 1),) if stride is None else stride
    return exchange_many(ident, [(x, axis, size, stride, bcast, reduce, lanes)])[0]


def per_device(
    features,
    cached_embed,
    staleness,
    node_counts,
    neighbours,
    degrees,
    w_self,
    w_nbr,
    sage_bias,
    cotangent,
):
    n_dom = lax.axis_size("dom")
    n_col = lax.axis_size("col")
    col_width = features.shape[0]
    part_rows = features.shape[1]
    slot_count = neighbours.shape[0]
    hidden = w_self.shape[1]
    my_index = lax.axis_index("dom")
    fresh_flag = (staleness >= LIMIT).astype(jnp.int32)
    my_fresh = fresh_flag[my_index]
    own_cache = lax.dynamic_slice_in_dim(cached_embed, my_index * part_rows, part_rows, 1)
    own_source = jnp.where(my_fresh == 1, features, own_cache)
    col_inputs = jnp.concatenate([features, w_self, w_nbr, cotangent], axis=0)
    bias_block = jnp.zeros((8, 128), jnp.float32).at[0, : sage_bias.shape[0]].set(sage_bias)
    blocks = exchange(own_source, 0, "dom", n_dom, bcast=True)
    sources = blocks.transpose(1, 0, 2).reshape(col_width, n_dom * part_rows)
    local_slot = jnp.arange(part_rows, dtype=jnp.int32)
    live_rows = (local_slot < node_counts[my_index]).astype(jnp.float32)
    slot_index = jnp.arange(slot_count, dtype=jnp.int32)
    used = (slot_index[:, None] < degrees[None, :]).astype(jnp.float32)
    weights = used * (live_rows / degrees.astype(jnp.float32))[None, :]
    gathered = sources[:, neighbours].astype(jnp.float32)
    aggregated = jnp.sum(weights[None, :, :] * gathered, axis=1).astype(jnp.bfloat16)
    col_blocks, bias_blocks = exchange_many(
        1,
        [
            (jnp.concatenate([aggregated, col_inputs], axis=0), "col", n_col, ((n_col, 1),), True, False, 0),
            (bias_block, "col", n_col, ((n_col, 1),), True, False, 0),
        ],
    )
    agg_full = col_blocks[:, :col_width].reshape(n_col * col_width, part_rows)
    col_blocks = col_blocks[:, col_width:]
    feat_full = col_blocks[:, :col_width].reshape(n_col * col_width, part_rows)
    w_self_full = col_blocks[:, col_width : 2 * col_width].reshape(n_col * col_width, hidden)
    w_nbr_full = col_blocks[:, 2 * col_width : 3 * col_width].reshape(n_col * col_width, hidden)
    cot_full = col_blocks[:, 3 * col_width :].reshape(hidden, part_rows)
    bias_full = bias_blocks[:, 0, : sage_bias.shape[0]].reshape(hidden)
    pre_full = (
        left_product(w_self_full, feat_full)
        + left_product(w_nbr_full, agg_full)
        + bias_full[:, None]
    )
    sig_full = 1.0 / (1.0 + jnp.exp(-pre_full))
    my_col = lax.axis_index("col")
    block_rows = hidden // n_col
    pre_act = lax.dynamic_slice_in_dim(pre_full, my_col * block_rows, block_rows, 0)
    sigmoid = lax.dynamic_slice_in_dim(sig_full, my_col * block_rows, block_rows, 0)
    activation = (live_rows[None, :] * pre_act * sigmoid).astype(jnp.bfloat16)
    grad_full = (
        live_rows[None, :]
        * cot_full.astype(jnp.float32)
        * sig_full
        * (1.0 + pre_full * (1.0 - sig_full))
    ).astype(jnp.bfloat16)
    grad_pre = lax.dynamic_slice_in_dim(grad_full, my_col * block_rows, block_rows, 0)
    self_part = right_product(features, grad_full)
    nbr_part = right_product(aggregated, grad_full)
    bias_part = jnp.sum(grad_pre.astype(jnp.float32), axis=1)
    bias_rows = jnp.zeros((8, hidden), jnp.float32).at[0, : bias_part.shape[0]].set(bias_part)
    packed = jnp.concatenate([self_part, nbr_part, bias_rows], axis=0)
    grad_agg = jnp.dot(w_nbr, grad_full, preferred_element_type=jnp.float32).astype(jnp.bfloat16)
    own_term = jnp.dot(w_self, grad_full, preferred_element_type=jnp.float32)
    spread = weights[None, :, :] * grad_agg.astype(jnp.float32)[:, None, :]
    fresh_rank = jnp.cumsum(fresh_flag) - 1
    nbr_part = neighbours // part_rows
    owner = nbr_part[:, :, None] == jnp.arange(n_dom, dtype=jnp.int32)
    nbr_fresh = jnp.sum(jnp.where(owner, fresh_flag, 0), axis=2)
    nbr_rank = jnp.sum(jnp.where(owner, fresh_rank, 0), axis=2)
    compact = jnp.where(
        nbr_fresh == 1,
        nbr_rank * part_rows + neighbours % part_rows,
        FRESH * part_rows,
    )
    contrib = (
        jnp.zeros((col_width, FRESH * part_rows), jnp.float32)
        .at[:, compact.reshape(-1)]
        .add(spread.reshape(col_width, -1), mode="drop")
    )
    padded = jnp.concatenate(
        [contrib.astype(jnp.bfloat16), jnp.zeros((col_width, part_rows), jnp.bfloat16)], axis=1
    ).reshape(col_width, FRESH + 1, part_rows)
    block_of = jnp.where(fresh_flag == 1, fresh_rank, FRESH)
    contrib = jnp.take(padded, block_of, axis=1).reshape(col_width, n_dom * part_rows)
    ys = 8 if n_dom % 16 == 0 else 1
    first = ((2, 1), (n_dom // (2 * ys), 2 * ys))
    summed, back = exchange_many(
        5,
        [
            (packed.astype(jnp.bfloat16), "dom", n_dom // ys, first, True, True, 0, ys, ((ys, 2),)),
            (contrib, "dom", n_dom, ((n_dom, 1),), False, True, part_rows),
        ],
    )
    grad_self = summed[:col_width]
    grad_nbr = summed[col_width : 2 * col_width]
    grad_bias = summed[2 * col_width, : bias_part.shape[0]]
    grad_feat = (own_term + my_fresh.astype(jnp.float32) * back).astype(jnp.bfloat16)
    return (activation, grad_feat, grad_self, grad_nbr, grad_bias)


def solution(mesh):
    placed = (
        P("col", "dom"),
        P("col", None),
        P(),
        P(),
        P(None, "dom"),
        P("dom"),
        P("col", None),
        P("col", None),
        P("col"),
        P("col", "dom"),
    )
    return jax.shard_map(
        per_device,
        mesh=mesh,
        in_specs=placed,
        out_specs=(P("col", "dom"), P("col", "dom"), P("col", None), P("col", None), P("col")),
        check_vma=False,
    )
```

```python
import functools

import jax
import jax.numpy as jnp
from jax import lax
from jax.experimental import pallas as pl
from jax.experimental.pallas import tpu as pltpu
from jax.sharding import PartitionSpec as P

LIMIT = 8
FRESH = 16
MESH = pl.DeviceIdType.MESH


def left_product(weight, data):
    return lax.dot_general(
        weight, data, (((0,), (0,)), ((), ())), preferred_element_type=jnp.float32
    )


def right_product(data, grads):
    return lax.dot_general(
        data, grads, (((1,), (1,)), ((), ())), preferred_element_type=jnp.float32
    )


def group_pos(me, digits):
    pos, scale = 0, 1
    for radix, stride in digits:
        pos = pos + lax.rem(me // stride, radix) * scale
        scale *= radix
    return pos


def group_member(me, pos, j, digits):
    for radix, stride in digits:
        me = me + (lax.rem(j, radix) - lax.rem(pos, radix)) * stride
        j, pos = j // radix, pos // radix
    return me


def exchange_kernel(specs, *refs):
    count = len(specs)
    xs, ys = refs[:count], refs[count : 2 * count]
    scratch = refs[2 * count :]
    barrier = pltpu.get_barrier_semaphore()
    plans = []
    extra = scratch[3 * count :]
    for e, (axis, size, stride, bcast, reduce, lanes, _, _) in enumerate(specs):
        x_ref, y_ref = xs[e], ys[e]
        buf, send_sem, recv_sem = scratch[3 * e : 3 * e + 3]
        me = lax.axis_index(axis)
        pos = group_pos(me, stride)
        plans.append((axis, size, stride, bcast, reduce, lanes, x_ref, y_ref, buf, send_sem, recv_sem, me, pos))

    def member(plan, j):
        stride, me, pos = plan[2], plan[11], plan[12]
        return group_member(me, pos, j, stride)

    def chunk(plan, j):
        bcast, lanes, x_ref = plan[3], plan[5], plan[6]
        if bcast:
            return x_ref
        if lanes:
            return x_ref.at[:, pl.ds(pl.multiple_of(j * lanes, lanes), lanes)]
        return x_ref.at[j]

    def desc(plan, j, slot):
        axis, buf, send_sem, recv_sem = plan[0], plan[8], plan[9], plan[10]
        return pltpu.make_async_remote_copy(
            src_ref=chunk(plan, j),
            dst_ref=buf.at[slot],
            send_sem=send_sem.at[j],
            recv_sem=recv_sem.at[slot],
            device_id={axis: member(plan, j)},
            device_id_type=MESH,
        )

    def each_peer(plan, body):
        size, pos = plan[1], plan[12]

        def step(k, carry):
            body(lax.rem(pos + k, size))
            return carry

        lax.fori_loop(1, size, step, 0)

    seconds = []
    for e, spec in enumerate(specs):
        if spec[6] > 1:
            stage, buf2, send2, recv2 = extra[4 * len(seconds) : 4 * len(seconds) + 4]
            me = plans[e][11]
            second = (spec[0], spec[6], spec[7], True, True, 0, stage, None, buf2, send2, recv2, me,
                      group_pos(me, spec[7]))
            seconds.append((e, second))
    greetings = 0
    for plan in plans + [second for _, second in seconds]:
        each_peer(
            plan,
            lambda j, plan=plan: pl.semaphore_signal(
                barrier, 1, device_id={plan[0]: member(plan, j)}, device_id_type=MESH
            ),
        )
        greetings += plan[1] - 1
    pl.semaphore_wait(barrier, greetings)
    for plan in plans:
        each_peer(plan, lambda j, plan=plan: desc(plan, j, plan[12]).start())
    for plan in plans:
        buf, pos = plan[8], plan[12]
        buf[pos] = chunk(plan, pos)[...]
    for e, second in seconds:
        plan = plans[e]

        def finish_first(j, plan=plan):
            desc(plan, j, plan[12]).wait_send()
            desc(plan, j, j).wait_recv()

        each_peer(plan, finish_first)
        second[6][...] = jnp.sum(plan[8][...].astype(jnp.float32), axis=0).astype(second[6].dtype)
    for e, plan in enumerate(plans):
        if specs[e][6] > 1:
            continue
        for k in range(1, min(plan[1], 9)):
            desc(plan, lax.rem(plan[12] + k, plan[1]), plan[12]).wait_send()
    for _, second in seconds:
        each_peer(second, lambda j, second=second: desc(second, j, second[12]).start())
        second[8][second[12]] = second[6][...]
    for e, plan in enumerate(plans):
        if specs[e][6] > 1:
            continue

        def finish(k, carry, plan=plan):
            j = lax.rem(plan[12] + k, plan[1])
            desc(plan, j, plan[12]).wait_send()
            return carry

        lax.fori_loop(min(plan[1], 9), plan[1], finish, 0)

        def arrive(j, plan=plan):
            desc(plan, j, j).wait_recv()

        each_peer(plan, arrive)
    for _, second in seconds:

        def finish_second(j, second=second):
            desc(second, j, second[12]).wait_send()
            desc(second, j, j).wait_recv()

        each_peer(second, finish_second)
    for e, plan in enumerate(plans):
        reduce, y_ref, buf = plan[4], plan[7], plan[8]
        if specs[e][6] > 1:
            buf = dict(seconds)[e][8]
        if reduce:
            y_ref[...] = jnp.sum(buf[...].astype(jnp.float32), axis=0)
        else:
            y_ref[...] = buf[...]


def exchange_many(ident, jobs):
    specs, out_shapes, scratch, extra = [], [], [], []
    for job in jobs:
        x, axis, size, stride, bcast, reduce, lanes = job[:7]
        size2, stride2 = job[7:] if len(job) > 7 else (1, ((1, 1),))
        if bcast:
            block = x.shape
        elif lanes:
            block = (x.shape[0], lanes)
        else:
            block = x.shape[1:]
        specs.append((axis, size, stride, bcast, reduce, lanes, size2, stride2))
        if size2 > 1:
            extra += [
                pltpu.VMEM(block, x.dtype),
                pltpu.VMEM((size2,) + block, x.dtype),
                pltpu.SemaphoreType.DMA((size2,)),
                pltpu.SemaphoreType.DMA((size2,)),
            ]
        out_shapes.append(
            jax.ShapeDtypeStruct(block if reduce else (size,) + block, jnp.float32 if reduce else x.dtype)
        )
        scratch += [
            pltpu.VMEM((size,) + block, x.dtype),
            pltpu.SemaphoreType.DMA((size,)),
            pltpu.SemaphoreType.DMA((size,)),
        ]
    return pl.pallas_call(
        functools.partial(exchange_kernel, tuple(specs)),
        out_shape=tuple(out_shapes),
        in_specs=[pl.BlockSpec(memory_space=pltpu.VMEM)] * len(jobs),
        out_specs=tuple(pl.BlockSpec(memory_space=pltpu.VMEM) for _ in jobs),
        scratch_shapes=scratch + extra,
        compiler_params=pltpu.CompilerParams(collective_id=ident, has_side_effects=True),
    )(*[job[0] for job in jobs])


def exchange(x, ident, axis, size, stride=None, bcast=False, reduce=False, lanes=0):
    stride = ((size, 1),) if stride is None else stride
    return exchange_many(ident, [(x, axis, size, stride, bcast, reduce, lanes)])[0]


def per_device(
    features,
    cached_embed,
    staleness,
    node_counts,
    neighbours,
    degrees,
    w_self,
    w_nbr,
    sage_bias,
    cotangent,
):
    n_dom = lax.axis_size("dom")
    n_col = lax.axis_size("col")
    col_width = features.shape[0]
    part_rows = features.shape[1]
    slot_count = neighbours.shape[0]
    hidden = w_self.shape[1]
    my_index = lax.axis_index("dom")
    fresh_flag = (staleness >= LIMIT).astype(jnp.int32)
    my_fresh = fresh_flag[my_index]
    col_inputs = jnp.concatenate([features, w_self, w_nbr, cotangent], axis=0)
    bias_block = jnp.zeros((8, 128), jnp.float32).at[0, : sage_bias.shape[0]].set(sage_bias)
    blocks = exchange(features, 0, "dom", n_dom, bcast=True)
    sources = jnp.where(
        fresh_flag[None, :, None] == 1,
        blocks.transpose(1, 0, 2),
        cached_embed.reshape(col_width, n_dom, part_rows),
    ).reshape(col_width, n_dom * part_rows)
    local_slot = jnp.arange(part_rows, dtype=jnp.int32)
    live_rows = (local_slot < node_counts[my_index]).astype(jnp.float32)
    slot_index = jnp.arange(slot_count, dtype=jnp.int32)
    used = (slot_index[:, None] < degrees[None, :]).astype(jnp.float32)
    weights = used * (live_rows / degrees.astype(jnp.float32))[None, :]
    gathered = sources[:, neighbours].astype(jnp.float32)
    aggregated = jnp.sum(weights[None, :, :] * gathered, axis=1).astype(jnp.bfloat16)
    col_blocks, bias_blocks = exchange_many(
        1,
        [
            (jnp.concatenate([aggregated, col_inputs], axis=0), "col", n_col, ((n_col, 1),), True, False, 0),
            (bias_block, "col", n_col, ((n_col, 1),), True, False, 0),
        ],
    )
    agg_full = col_blocks[:, :col_width].reshape(n_col * col_width, part_rows)
    col_blocks = col_blocks[:, col_width:]
    feat_full = col_blocks[:, :col_width].reshape(n_col * col_width, part_rows)
    w_self_full = col_blocks[:, col_width : 2 * col_width].reshape(n_col * col_width, hidden)
    w_nbr_full = col_blocks[:, 2 * col_width : 3 * col_width].reshape(n_col * col_width, hidden)
    cot_full = col_blocks[:, 3 * col_width :].reshape(hidden, part_rows)
    bias_full = bias_blocks[:, 0, : sage_bias.shape[0]].reshape(hidden)
    pre_full = (
        left_product(w_self_full, feat_full)
        + left_product(w_nbr_full, agg_full)
        + bias_full[:, None]
    )
    sig_full = 1.0 / (1.0 + jnp.exp(-pre_full))
    my_col = lax.axis_index("col")
    block_rows = hidden // n_col
    pre_act = lax.dynamic_slice_in_dim(pre_full, my_col * block_rows, block_rows, 0)
    sigmoid = lax.dynamic_slice_in_dim(sig_full, my_col * block_rows, block_rows, 0)
    activation = (live_rows[None, :] * pre_act * sigmoid).astype(jnp.bfloat16)
    grad_full = (
        live_rows[None, :]
        * cot_full.astype(jnp.float32)
        * sig_full
        * (1.0 + pre_full * (1.0 - sig_full))
    ).astype(jnp.bfloat16)
    grad_pre = lax.dynamic_slice_in_dim(grad_full, my_col * block_rows, block_rows, 0)
    self_part = right_product(features, grad_full)
    nbr_part = right_product(aggregated, grad_full)
    bias_part = jnp.sum(grad_pre.astype(jnp.float32), axis=1)
    bias_rows = jnp.zeros((8, hidden), jnp.float32).at[0, : bias_part.shape[0]].set(bias_part)
    packed = jnp.concatenate([self_part, nbr_part, bias_rows], axis=0)
    grad_agg = jnp.dot(w_nbr, grad_full, preferred_element_type=jnp.float32).astype(jnp.bfloat16)
    own_term = jnp.dot(w_self, grad_full, preferred_element_type=jnp.float32)
    spread = weights[None, :, :] * grad_agg.astype(jnp.float32)[:, None, :]
    fresh_rank = jnp.cumsum(fresh_flag) - 1
    slot_base = jnp.where(fresh_flag == 1, fresh_rank * part_rows, -part_rows)
    owner = (neighbours // part_rows)[:, :, None] == jnp.arange(n_dom, dtype=jnp.int32)
    compact = jnp.sum(jnp.where(owner, slot_base, 0), axis=2) + neighbours % part_rows
    compact = jnp.where(compact >= 0, compact, FRESH * part_rows)
    contrib = (
        jnp.zeros((col_width, FRESH * part_rows), jnp.float32)
        .at[:, compact.reshape(-1)]
        .add(spread.reshape(col_width, -1), mode="drop")
    )
    padded = jnp.concatenate(
        [contrib.astype(jnp.bfloat16), jnp.zeros((col_width, part_rows), jnp.bfloat16)], axis=1
    ).reshape(col_width, FRESH + 1, part_rows)
    block_of = jnp.where(fresh_flag == 1, fresh_rank, FRESH)
    contrib = jnp.take(padded, block_of, axis=1).reshape(col_width, n_dom * part_rows)
    ys = 8 if n_dom % 16 == 0 else 1
    first = ((2, 1), (n_dom // (2 * ys), 2 * ys))
    back, summed = exchange_many(
        5,
        [
            (contrib, "dom", n_dom, ((n_dom, 1),), False, True, part_rows),
            (packed.astype(jnp.bfloat16), "dom", n_dom // ys, first, True, True, 0, ys, ((ys, 2),)),
        ],
    )
    grad_self = summed[:col_width]
    grad_nbr = summed[col_width : 2 * col_width]
    grad_bias = summed[2 * col_width, : bias_part.shape[0]]
    grad_feat = (own_term + my_fresh.astype(jnp.float32) * back).astype(jnp.bfloat16)
    return (activation, grad_feat, grad_self, grad_nbr, grad_bias)


def solution(mesh):
    placed = (
        P("col", "dom"),
        P("col", None),
        P(),
        P(),
        P(None, "dom"),
        P("dom"),
        P("col", None),
        P("col", None),
        P("col"),
        P("col", "dom"),
    )
    return jax.shard_map(
        per_device,
        mesh=mesh,
        in_specs=placed,
        out_specs=(P("col", "dom"), P("col", "dom"), P("col", None), P("col", None), P("col")),
        check_vma=False,
    )
```

```python
import functools

import jax
import jax.numpy as jnp
from jax import lax
from jax.experimental import pallas as pl
from jax.experimental.pallas import tpu as pltpu
from jax.sharding import PartitionSpec as P

LIMIT = 8
FRESH = 16
MESH = pl.DeviceIdType.MESH


def left_product(weight, data):
    return lax.dot_general(
        weight, data, (((0,), (0,)), ((), ())), preferred_element_type=jnp.float32
    )


def right_product(data, grads):
    return lax.dot_general(
        data, grads, (((1,), (1,)), ((), ())), preferred_element_type=jnp.float32
    )


def group_pos(me, digits):
    pos, scale = 0, 1
    for radix, stride in digits:
        pos = pos + lax.rem(me // stride, radix) * scale
        scale *= radix
    return pos


def group_member(me, pos, j, digits):
    for radix, stride in digits:
        me = me + (lax.rem(j, radix) - lax.rem(pos, radix)) * stride
        j, pos = j // radix, pos // radix
    return me


def exchange_kernel(specs, *refs):
    count = len(specs)
    xs, ys = refs[:count], refs[count : 2 * count]
    scratch = refs[2 * count :]
    barrier = pltpu.get_barrier_semaphore()
    plans = []
    extra = scratch[3 * count :]
    for e, (axis, size, stride, bcast, reduce, lanes, _, _) in enumerate(specs):
        x_ref, y_ref = xs[e], ys[e]
        buf, send_sem, recv_sem = scratch[3 * e : 3 * e + 3]
        me = lax.axis_index(axis)
        pos = group_pos(me, stride)
        plans.append((axis, size, stride, bcast, reduce, lanes, x_ref, y_ref, buf, send_sem, recv_sem, me, pos))

    def member(plan, j):
        stride, me, pos = plan[2], plan[11], plan[12]
        return group_member(me, pos, j, stride)

    def chunk(plan, j):
        bcast, lanes, x_ref = plan[3], plan[5], plan[6]
        if bcast:
            return x_ref
        if lanes:
            return x_ref.at[:, pl.ds(pl.multiple_of(j * lanes, lanes), lanes)]
        return x_ref.at[j]

    def desc(plan, j, slot):
        axis, buf, send_sem, recv_sem = plan[0], plan[8], plan[9], plan[10]
        return pltpu.make_async_remote_copy(
            src_ref=chunk(plan, j),
            dst_ref=buf.at[slot],
            send_sem=send_sem.at[j],
            recv_sem=recv_sem.at[slot],
            device_id={axis: member(plan, j)},
            device_id_type=MESH,
        )

    def each_peer(plan, body):
        size, pos = plan[1], plan[12]

        def step(k, carry):
            body(lax.rem(pos + k, size))
            return carry

        lax.fori_loop(1, size, step, 0)

    seconds = []
    for e, spec in enumerate(specs):
        if spec[6] > 1:
            stage, buf2, send2, recv2 = extra[4 * len(seconds) : 4 * len(seconds) + 4]
            me = plans[e][11]
            second = (spec[0], spec[6], spec[7], True, True, 0, stage, None, buf2, send2, recv2, me,
                      group_pos(me, spec[7]))
            seconds.append((e, second))
    greetings = 0
    for plan in plans + [second for _, second in seconds]:
        each_peer(
            plan,
            lambda j, plan=plan: pl.semaphore_signal(
                barrier, 1, device_id={plan[0]: member(plan, j)}, device_id_type=MESH
            ),
        )
        greetings += plan[1] - 1
    pl.semaphore_wait(barrier, greetings)
    for plan in plans:
        each_peer(plan, lambda j, plan=plan: desc(plan, j, plan[12]).start())
    for plan in plans:
        buf, pos = plan[8], plan[12]
        buf[pos] = chunk(plan, pos)[...]
    for e, second in seconds:
        plan = plans[e]

        def finish_first(j, plan=plan):
            desc(plan, j, plan[12]).wait_send()
            desc(plan, j, j).wait_recv()

        each_peer(plan, finish_first)
        second[6][...] = jnp.sum(plan[8][...].astype(jnp.float32), axis=0).astype(second[6].dtype)
    for e, plan in enumerate(plans):
        if specs[e][6] > 1:
            continue
        for k in range(1, min(plan[1], 9)):
            desc(plan, lax.rem(plan[12] + k, plan[1]), plan[12]).wait_send()
    for _, second in seconds:
        each_peer(second, lambda j, second=second: desc(second, j, second[12]).start())
        second[8][second[12]] = second[6][...]
    for e, plan in enumerate(plans):
        if specs[e][6] > 1:
            continue

        def finish(k, carry, plan=plan):
            j = lax.rem(plan[12] + k, plan[1])
            desc(plan, j, plan[12]).wait_send()
            return carry

        lax.fori_loop(min(plan[1], 9), plan[1], finish, 0)

        def arrive(j, plan=plan):
            desc(plan, j, j).wait_recv()

        each_peer(plan, arrive)
    for _, second in seconds:

        def finish_second(j, second=second):
            desc(second, j, second[12]).wait_send()
            desc(second, j, j).wait_recv()

        each_peer(second, finish_second)
    for e, plan in enumerate(plans):
        reduce, y_ref, buf = plan[4], plan[7], plan[8]
        if specs[e][6] > 1:
            buf = dict(seconds)[e][8]
        if reduce:
            y_ref[...] = jnp.sum(buf[...].astype(jnp.float32), axis=0)
        else:
            y_ref[...] = buf[...]


def exchange_many(ident, jobs):
    specs, out_shapes, scratch, extra = [], [], [], []
    for job in jobs:
        x, axis, size, stride, bcast, reduce, lanes = job[:7]
        size2, stride2 = job[7:] if len(job) > 7 else (1, ((1, 1),))
        if bcast:
            block = x.shape
        elif lanes:
            block = (x.shape[0], lanes)
        else:
            block = x.shape[1:]
        specs.append((axis, size, stride, bcast, reduce, lanes, size2, stride2))
        if size2 > 1:
            extra += [
                pltpu.VMEM(block, x.dtype),
                pltpu.VMEM((size2,) + block, x.dtype),
                pltpu.SemaphoreType.DMA((size2,)),
                pltpu.SemaphoreType.DMA((size2,)),
            ]
        out_shapes.append(
            jax.ShapeDtypeStruct(block if reduce else (size,) + block, jnp.float32 if reduce else x.dtype)
        )
        scratch += [
            pltpu.VMEM((size,) + block, x.dtype),
            pltpu.SemaphoreType.DMA((size,)),
            pltpu.SemaphoreType.DMA((size,)),
        ]
    return pl.pallas_call(
        functools.partial(exchange_kernel, tuple(specs)),
        out_shape=tuple(out_shapes),
        in_specs=[pl.BlockSpec(memory_space=pltpu.VMEM)] * len(jobs),
        out_specs=tuple(pl.BlockSpec(memory_space=pltpu.VMEM) for _ in jobs),
        scratch_shapes=scratch + extra,
        compiler_params=pltpu.CompilerParams(collective_id=ident, has_side_effects=True),
    )(*[job[0] for job in jobs])


def exchange(x, ident, axis, size, stride=None, bcast=False, reduce=False, lanes=0):
    stride = ((size, 1),) if stride is None else stride
    return exchange_many(ident, [(x, axis, size, stride, bcast, reduce, lanes)])[0]


def per_device(
    features,
    cached_embed,
    staleness,
    node_counts,
    neighbours,
    degrees,
    w_self,
    w_nbr,
    sage_bias,
    cotangent,
):
    n_dom = lax.axis_size("dom")
    n_col = lax.axis_size("col")
    col_width = features.shape[0]
    part_rows = features.shape[1]
    slot_count = neighbours.shape[0]
    hidden = w_self.shape[1]
    my_index = lax.axis_index("dom")
    fresh_flag = (staleness >= LIMIT).astype(jnp.int32)
    my_fresh = fresh_flag[my_index]
    col_inputs = jnp.concatenate([features, w_self, w_nbr, cotangent], axis=0)
    bias_block = jnp.zeros((8, 128), jnp.float32).at[0, : sage_bias.shape[0]].set(sage_bias)
    blocks = exchange(features, 0, "dom", n_dom, bcast=True)
    sources = jnp.where(
        fresh_flag[None, :, None] == 1,
        blocks.transpose(1, 0, 2),
        cached_embed.reshape(col_width, n_dom, part_rows),
    ).reshape(col_width, n_dom * part_rows)
    local_slot = jnp.arange(part_rows, dtype=jnp.int32)
    live_rows = (local_slot < node_counts[my_index]).astype(jnp.float32)
    slot_index = jnp.arange(slot_count, dtype=jnp.int32)
    used = (slot_index[:, None] < degrees[None, :]).astype(jnp.float32)
    weights = used * (live_rows / degrees.astype(jnp.float32))[None, :]
    gathered = sources[:, neighbours].astype(jnp.float32)
    aggregated = jnp.sum(weights[None, :, :] * gathered, axis=1).astype(jnp.bfloat16)
    col_blocks, bias_blocks = exchange_many(
        1,
        [
            (jnp.concatenate([aggregated, col_inputs], axis=0), "col", n_col, ((n_col, 1),), True, False, 0),
            (bias_block, "col", n_col, ((n_col, 1),), True, False, 0),
        ],
    )
    agg_full = col_blocks[:, :col_width].reshape(n_col * col_width, part_rows)
    col_blocks = col_blocks[:, col_width:]
    feat_full = col_blocks[:, :col_width].reshape(n_col * col_width, part_rows)
    w_self_full = col_blocks[:, col_width : 2 * col_width].reshape(n_col * col_width, hidden)
    w_nbr_full = col_blocks[:, 2 * col_width : 3 * col_width].reshape(n_col * col_width, hidden)
    cot_full = col_blocks[:, 3 * col_width :].reshape(hidden, part_rows)
    bias_full = bias_blocks[:, 0, : sage_bias.shape[0]].reshape(hidden)
    pre_full = (
        left_product(w_self_full, feat_full)
        + left_product(w_nbr_full, agg_full)
        + bias_full[:, None]
    )
    sig_full = 1.0 / (1.0 + jnp.exp(-pre_full))
    my_col = lax.axis_index("col")
    block_rows = hidden // n_col
    pre_act = lax.dynamic_slice_in_dim(pre_full, my_col * block_rows, block_rows, 0)
    sigmoid = lax.dynamic_slice_in_dim(sig_full, my_col * block_rows, block_rows, 0)
    activation = (live_rows[None, :] * pre_act * sigmoid).astype(jnp.bfloat16)
    grad_full = (
        live_rows[None, :]
        * cot_full.astype(jnp.float32)
        * sig_full
        * (1.0 + pre_full * (1.0 - sig_full))
    ).astype(jnp.bfloat16)
    grad_pre = lax.dynamic_slice_in_dim(grad_full, my_col * block_rows, block_rows, 0)
    self_part = right_product(features, grad_full)
    nbr_part = right_product(aggregated, grad_full)
    bias_part = jnp.sum(grad_pre.astype(jnp.float32), axis=1)
    bias_rows = jnp.zeros((8, hidden), jnp.float32).at[0, : bias_part.shape[0]].set(bias_part)
    packed = jnp.concatenate([self_part, nbr_part, bias_rows], axis=0)
    grad_agg = jnp.dot(w_nbr, grad_full, preferred_element_type=jnp.float32).astype(jnp.bfloat16)
    own_term = jnp.dot(w_self, grad_full, preferred_element_type=jnp.float32)
    spread = weights[None, :, :] * grad_agg.astype(jnp.float32)[:, None, :]
    fresh_rank = jnp.cumsum(fresh_flag) - 1
    slot_base = jnp.where(fresh_flag == 1, fresh_rank * part_rows, -part_rows)
    owner = (neighbours // part_rows)[:, :, None] == jnp.arange(n_dom, dtype=jnp.int32)
    compact = jnp.sum(jnp.where(owner, slot_base, 0), axis=2) + neighbours % part_rows
    compact = jnp.where(compact >= 0, compact, FRESH * part_rows)
    contrib = (
        jnp.zeros((col_width, FRESH * part_rows), jnp.float32)
        .at[:, compact.reshape(-1)]
        .add(spread.reshape(col_width, -1), mode="drop")
    )
    compact_blocks = contrib.astype(jnp.bfloat16).reshape(col_width, FRESH, part_rows)
    block_of = jnp.clip(fresh_rank, 0, FRESH - 1)
    contrib = jnp.take(compact_blocks, block_of, axis=1, mode="clip").reshape(col_width, n_dom * part_rows)
    ys = 8 if n_dom % 16 == 0 else 1
    first = ((2, 1), (n_dom // (2 * ys), 2 * ys))
    back, summed = exchange_many(
        5,
        [
            (contrib, "dom", n_dom, ((n_dom, 1),), False, True, part_rows),
            (packed.astype(jnp.bfloat16), "dom", n_dom // ys, first, True, True, 0, ys, ((ys, 2),)),
        ],
    )
    grad_self = summed[:col_width]
    grad_nbr = summed[col_width : 2 * col_width]
    grad_bias = summed[2 * col_width, : bias_part.shape[0]]
    grad_feat = (own_term + my_fresh.astype(jnp.float32) * back).astype(jnp.bfloat16)
    return (activation, grad_feat, grad_self, grad_nbr, grad_bias)


def solution(mesh):
    placed = (
        P("col", "dom"),
        P("col", None),
        P(),
        P(),
        P(None, "dom"),
        P("dom"),
        P("col", None),
        P("col", None),
        P("col"),
        P("col", "dom"),
    )
    return jax.shard_map(
        per_device,
        mesh=mesh,
        in_specs=placed,
        out_specs=(P("col", "dom"), P("col", "dom"), P("col", None), P("col", None), P("col")),
        check_vma=False,
    )
```

```python
import functools

import jax
import jax.numpy as jnp
from jax import lax
from jax.experimental import pallas as pl
from jax.experimental.pallas import tpu as pltpu
from jax.sharding import PartitionSpec as P

LIMIT = 8
FRESH = 16
MESH = pl.DeviceIdType.MESH


def left_product(weight, data):
    return lax.dot_general(
        weight, data, (((0,), (0,)), ((), ())), preferred_element_type=jnp.float32
    )


def right_product(data, grads):
    return lax.dot_general(
        data, grads, (((1,), (1,)), ((), ())), preferred_element_type=jnp.float32
    )


def group_pos(me, digits):
    pos, scale = 0, 1
    for radix, stride in digits:
        pos = pos + lax.rem(me // stride, radix) * scale
        scale *= radix
    return pos


def group_member(me, pos, j, digits):
    for radix, stride in digits:
        me = me + (lax.rem(j, radix) - lax.rem(pos, radix)) * stride
        j, pos = j // radix, pos // radix
    return me


def exchange_kernel(specs, *refs):
    count = len(specs)
    xs, ys = refs[:count], refs[count : 2 * count]
    scratch = refs[2 * count :]
    barrier = pltpu.get_barrier_semaphore()
    plans = []
    extra = scratch[3 * count :]
    for e, (axis, size, stride, bcast, reduce, lanes, _, _) in enumerate(specs):
        x_ref, y_ref = xs[e], ys[e]
        buf, send_sem, recv_sem = scratch[3 * e : 3 * e + 3]
        me = lax.axis_index(axis)
        pos = group_pos(me, stride)
        plans.append((axis, size, stride, bcast, reduce, lanes, x_ref, y_ref, buf, send_sem, recv_sem, me, pos))

    def member(plan, j):
        stride, me, pos = plan[2], plan[11], plan[12]
        return group_member(me, pos, j, stride)

    def chunk(plan, j):
        bcast, lanes, x_ref = plan[3], plan[5], plan[6]
        if bcast:
            return x_ref
        if lanes:
            return x_ref.at[:, pl.ds(pl.multiple_of(j * lanes, lanes), lanes)]
        return x_ref.at[j]

    def desc(plan, j, slot):
        axis, buf, send_sem, recv_sem = plan[0], plan[8], plan[9], plan[10]
        return pltpu.make_async_remote_copy(
            src_ref=chunk(plan, j),
            dst_ref=buf.at[slot],
            send_sem=send_sem.at[j],
            recv_sem=recv_sem.at[slot],
            device_id={axis: member(plan, j)},
            device_id_type=MESH,
        )

    def each_peer(plan, body):
        size, pos = plan[1], plan[12]

        def step(k, carry):
            body(lax.rem(pos + k, size))
            return carry

        lax.fori_loop(1, size, step, 0)

    seconds = []
    for e, spec in enumerate(specs):
        if spec[6] > 1:
            stage, buf2, send2, recv2 = extra[4 * len(seconds) : 4 * len(seconds) + 4]
            me = plans[e][11]
            second = (spec[0], spec[6], spec[7], True, True, 0, stage, None, buf2, send2, recv2, me,
                      group_pos(me, spec[7]))
            seconds.append((e, second))
    greetings = 0
    for plan in plans + [second for _, second in seconds]:
        each_peer(
            plan,
            lambda j, plan=plan: pl.semaphore_signal(
                barrier, 1, device_id={plan[0]: member(plan, j)}, device_id_type=MESH
            ),
        )
        greetings += plan[1] - 1
    pl.semaphore_wait(barrier, greetings)
    for plan in plans:
        each_peer(plan, lambda j, plan=plan: desc(plan, j, plan[12]).start())
    for plan in plans:
        buf, pos = plan[8], plan[12]
        buf[pos] = chunk(plan, pos)[...]
    for e, second in seconds:
        plan = plans[e]

        def finish_first(j, plan=plan):
            desc(plan, j, plan[12]).wait_send()
            desc(plan, j, j).wait_recv()

        each_peer(plan, finish_first)
        second[6][...] = jnp.sum(plan[8][...].astype(jnp.float32), axis=0).astype(second[6].dtype)
    for e, plan in enumerate(plans):
        if specs[e][6] > 1:
            continue
        for k in range(1, min(plan[1], 9)):
            desc(plan, lax.rem(plan[12] + k, plan[1]), plan[12]).wait_send()
    for _, second in seconds:
        each_peer(second, lambda j, second=second: desc(second, j, second[12]).start())
        second[8][second[12]] = second[6][...]
    for e, plan in enumerate(plans):
        if specs[e][6] > 1:
            continue

        def finish(k, carry, plan=plan):
            j = lax.rem(plan[12] + k, plan[1])
            desc(plan, j, plan[12]).wait_send()
            return carry

        lax.fori_loop(min(plan[1], 9), plan[1], finish, 0)

        def arrive(j, plan=plan):
            desc(plan, j, j).wait_recv()

        each_peer(plan, arrive)
    for _, second in seconds:

        def finish_second(j, second=second):
            desc(second, j, second[12]).wait_send()
            desc(second, j, j).wait_recv()

        each_peer(second, finish_second)
    for e, plan in enumerate(plans):
        reduce, y_ref, buf = plan[4], plan[7], plan[8]
        if specs[e][6] > 1:
            buf = dict(seconds)[e][8]
        if reduce:
            y_ref[...] = jnp.sum(buf[...].astype(jnp.float32), axis=0)
        else:
            y_ref[...] = buf[...]


def exchange_many(ident, jobs):
    specs, out_shapes, scratch, extra = [], [], [], []
    for job in jobs:
        x, axis, size, stride, bcast, reduce, lanes = job[:7]
        size2, stride2 = job[7:] if len(job) > 7 else (1, ((1, 1),))
        if bcast:
            block = x.shape
        elif lanes:
            block = (x.shape[0], lanes)
        else:
            block = x.shape[1:]
        specs.append((axis, size, stride, bcast, reduce, lanes, size2, stride2))
        if size2 > 1:
            extra += [
                pltpu.VMEM(block, x.dtype),
                pltpu.VMEM((size2,) + block, x.dtype),
                pltpu.SemaphoreType.DMA((size2,)),
                pltpu.SemaphoreType.DMA((size2,)),
            ]
        out_shapes.append(
            jax.ShapeDtypeStruct(block if reduce else (size,) + block, jnp.float32 if reduce else x.dtype)
        )
        scratch += [
            pltpu.VMEM((size,) + block, x.dtype),
            pltpu.SemaphoreType.DMA((size,)),
            pltpu.SemaphoreType.DMA((size,)),
        ]
    return pl.pallas_call(
        functools.partial(exchange_kernel, tuple(specs)),
        out_shape=tuple(out_shapes),
        in_specs=[pl.BlockSpec(memory_space=pltpu.VMEM)] * len(jobs),
        out_specs=tuple(pl.BlockSpec(memory_space=pltpu.VMEM) for _ in jobs),
        scratch_shapes=scratch + extra,
        compiler_params=pltpu.CompilerParams(collective_id=ident, has_side_effects=True),
    )(*[job[0] for job in jobs])


def exchange(x, ident, axis, size, stride=None, bcast=False, reduce=False, lanes=0):
    stride = ((size, 1),) if stride is None else stride
    return exchange_many(ident, [(x, axis, size, stride, bcast, reduce, lanes)])[0]


def per_device(
    features,
    cached_embed,
    staleness,
    node_counts,
    neighbours,
    degrees,
    w_self,
    w_nbr,
    sage_bias,
    cotangent,
):
    n_dom = lax.axis_size("dom")
    n_col = lax.axis_size("col")
    col_width = features.shape[0]
    part_rows = features.shape[1]
    slot_count = neighbours.shape[0]
    hidden = w_self.shape[1]
    my_index = lax.axis_index("dom")
    fresh_flag = (staleness >= LIMIT).astype(jnp.int32)
    my_fresh = fresh_flag[my_index]
    col_inputs = jnp.concatenate([features, w_self, w_nbr, cotangent], axis=0)
    bias_block = sage_bias.reshape(1, -1)
    blocks = exchange(features, 0, "dom", n_dom, bcast=True)
    sources = jnp.where(
        fresh_flag[None, :, None] == 1,
        blocks.transpose(1, 0, 2),
        cached_embed.reshape(col_width, n_dom, part_rows),
    ).reshape(col_width, n_dom * part_rows)
    local_slot = jnp.arange(part_rows, dtype=jnp.int32)
    live_rows = (local_slot < node_counts[my_index]).astype(jnp.float32)
    slot_index = jnp.arange(slot_count, dtype=jnp.int32)
    used = (slot_index[:, None] < degrees[None, :]).astype(jnp.float32)
    weights = used * (live_rows / degrees.astype(jnp.float32))[None, :]
    gathered = sources[:, neighbours].astype(jnp.float32)
    aggregated = jnp.sum(weights[None, :, :] * gathered, axis=1).astype(jnp.bfloat16)
    col_blocks, bias_blocks = exchange_many(
        1,
        [
            (jnp.concatenate([aggregated, col_inputs], axis=0), "col", n_col, ((n_col, 1),), True, False, 0),
            (bias_block, "col", n_col, ((n_col, 1),), True, False, 0),
        ],
    )
    agg_full = col_blocks[:, :col_width].reshape(n_col * col_width, part_rows)
    col_blocks = col_blocks[:, col_width:]
    feat_full = col_blocks[:, :col_width].reshape(n_col * col_width, part_rows)
    w_self_full = col_blocks[:, col_width : 2 * col_width].reshape(n_col * col_width, hidden)
    w_nbr_full = col_blocks[:, 2 * col_width : 3 * col_width].reshape(n_col * col_width, hidden)
    cot_full = col_blocks[:, 3 * col_width :].reshape(hidden, part_rows)
    bias_full = bias_blocks.reshape(hidden)
    pre_full = (
        left_product(w_self_full, feat_full)
        + left_product(w_nbr_full, agg_full)
        + bias_full[:, None]
    )
    sig_full = 1.0 / (1.0 + jnp.exp(-pre_full))
    my_col = lax.axis_index("col")
    block_rows = hidden // n_col
    pre_act = lax.dynamic_slice_in_dim(pre_full, my_col * block_rows, block_rows, 0)
    sigmoid = lax.dynamic_slice_in_dim(sig_full, my_col * block_rows, block_rows, 0)
    activation = (live_rows[None, :] * pre_act * sigmoid).astype(jnp.bfloat16)
    grad_full = (
        live_rows[None, :]
        * cot_full.astype(jnp.float32)
        * sig_full
        * (1.0 + pre_full * (1.0 - sig_full))
    ).astype(jnp.bfloat16)
    grad_pre = lax.dynamic_slice_in_dim(grad_full, my_col * block_rows, block_rows, 0)
    self_part = right_product(features, grad_full)
    nbr_part = right_product(aggregated, grad_full)
    bias_part = jnp.sum(grad_pre.astype(jnp.float32), axis=1)
    bias_rows = jnp.zeros((8, hidden), jnp.float32).at[0, : bias_part.shape[0]].set(bias_part)
    packed = jnp.concatenate([self_part, nbr_part, bias_rows], axis=0)
    grad_agg = jnp.dot(w_nbr, grad_full, preferred_element_type=jnp.float32).astype(jnp.bfloat16)
    own_term = jnp.dot(w_self, grad_full, preferred_element_type=jnp.float32)
    spread = weights[None, :, :] * grad_agg.astype(jnp.float32)[:, None, :]
    fresh_rank = jnp.cumsum(fresh_flag) - 1
    slot_base = jnp.where(fresh_flag == 1, fresh_rank * part_rows, -part_rows)
    owner = (neighbours // part_rows)[:, :, None] == jnp.arange(n_dom, dtype=jnp.int32)
    compact = jnp.sum(jnp.where(owner, slot_base, 0), axis=2) + neighbours % part_rows
    compact = jnp.where(compact >= 0, compact, FRESH * part_rows)
    contrib = (
        jnp.zeros((col_width, FRESH * part_rows), jnp.float32)
        .at[:, compact.reshape(-1)]
        .add(spread.reshape(col_width, -1), mode="drop")
    )
    compact_blocks = contrib.astype(jnp.bfloat16).reshape(col_width, FRESH, part_rows)
    block_of = jnp.clip(fresh_rank, 0, FRESH - 1)
    contrib = jnp.take(compact_blocks, block_of, axis=1, mode="clip").reshape(col_width, n_dom * part_rows)
    ys = 8 if n_dom % 16 == 0 else 1
    first = ((2, 1), (n_dom // (2 * ys), 2 * ys))
    back, summed = exchange_many(
        5,
        [
            (contrib, "dom", n_dom, ((n_dom, 1),), False, True, part_rows),
            (packed.astype(jnp.bfloat16), "dom", n_dom // ys, first, True, True, 0, ys, ((ys, 2),)),
        ],
    )
    grad_self = summed[:col_width]
    grad_nbr = summed[col_width : 2 * col_width]
    grad_bias = summed[2 * col_width, : bias_part.shape[0]]
    grad_feat = (own_term + my_fresh.astype(jnp.float32) * back).astype(jnp.bfloat16)
    return (activation, grad_feat, grad_self, grad_nbr, grad_bias)


def solution(mesh):
    placed = (
        P("col", "dom"),
        P("col", None),
        P(),
        P(),
        P(None, "dom"),
        P("dom"),
        P("col", None),
        P("col", None),
        P("col"),
        P("col", "dom"),
    )
    return jax.shard_map(
        per_device,
        mesh=mesh,
        in_specs=placed,
        out_specs=(P("col", "dom"), P("col", "dom"), P("col", None), P("col", None), P("col")),
        check_vma=False,
    )
```

```python
import functools

import jax
import jax.numpy as jnp
from jax import lax
from jax.experimental import pallas as pl
from jax.experimental.pallas import tpu as pltpu
from jax.sharding import PartitionSpec as P

LIMIT = 8
FRESH = 16
MESH = pl.DeviceIdType.MESH


def left_product(weight, data):
    return lax.dot_general(
        weight, data, (((0,), (0,)), ((), ())), preferred_element_type=jnp.float32
    )


def right_product(data, grads):
    return lax.dot_general(
        data, grads, (((1,), (1,)), ((), ())), preferred_element_type=jnp.float32
    )


def group_pos(me, digits):
    pos, scale = 0, 1
    for radix, stride in digits:
        pos = pos + lax.rem(me // stride, radix) * scale
        scale *= radix
    return pos


def group_member(me, pos, j, digits):
    for radix, stride in digits:
        me = me + (lax.rem(j, radix) - lax.rem(pos, radix)) * stride
        j, pos = j // radix, pos // radix
    return me


def exchange_kernel(specs, *refs):
    count = len(specs)
    xs, ys = refs[:count], refs[count : 2 * count]
    scratch = refs[2 * count :]
    barrier = pltpu.get_barrier_semaphore()
    plans = []
    extra = scratch[3 * count :]
    for e, (axis, size, stride, bcast, reduce, lanes, _, _) in enumerate(specs):
        x_ref, y_ref = xs[e], ys[e]
        buf, send_sem, recv_sem = scratch[3 * e : 3 * e + 3]
        me = lax.axis_index(axis)
        pos = group_pos(me, stride)
        plans.append((axis, size, stride, bcast, reduce, lanes, x_ref, y_ref, buf, send_sem, recv_sem, me, pos))

    def member(plan, j):
        stride, me, pos = plan[2], plan[11], plan[12]
        return group_member(me, pos, j, stride)

    def chunk(plan, j):
        bcast, lanes, x_ref = plan[3], plan[5], plan[6]
        if bcast:
            return x_ref
        if lanes:
            return x_ref.at[:, pl.ds(pl.multiple_of(j * lanes, lanes), lanes)]
        return x_ref.at[j]

    def desc(plan, j, slot):
        axis, buf, send_sem, recv_sem = plan[0], plan[8], plan[9], plan[10]
        return pltpu.make_async_remote_copy(
            src_ref=chunk(plan, j),
            dst_ref=buf.at[slot],
            send_sem=send_sem.at[j],
            recv_sem=recv_sem.at[slot],
            device_id={axis: member(plan, j)},
            device_id_type=MESH,
        )

    def each_peer(plan, body):
        size, pos = plan[1], plan[12]

        def step(k, carry):
            body(lax.rem(pos + k, size))
            return carry

        lax.fori_loop(1, size, step, 0)

    seconds = []
    for e, spec in enumerate(specs):
        if spec[6] > 1:
            stage, buf2, send2, recv2 = extra[4 * len(seconds) : 4 * len(seconds) + 4]
            me = plans[e][11]
            second = (spec[0], spec[6], spec[7], True, True, 0, stage, None, buf2, send2, recv2, me,
                      group_pos(me, spec[7]))
            seconds.append((e, second))
    greetings = 0
    for plan in plans + [second for _, second in seconds]:
        each_peer(
            plan,
            lambda j, plan=plan: pl.semaphore_signal(
                barrier, 1, device_id={plan[0]: member(plan, j)}, device_id_type=MESH
            ),
        )
        greetings += plan[1] - 1
    pl.semaphore_wait(barrier, greetings)
    for plan in plans:
        each_peer(plan, lambda j, plan=plan: desc(plan, j, plan[12]).start())
    for plan in plans:
        buf, pos = plan[8], plan[12]
        buf[pos] = chunk(plan, pos)[...]
    for e, second in seconds:
        plan = plans[e]

        def finish_first(j, plan=plan):
            desc(plan, j, plan[12]).wait_send()
            desc(plan, j, j).wait_recv()

        each_peer(plan, finish_first)
        second[6][...] = jnp.sum(plan[8][...].astype(jnp.float32), axis=0).astype(second[6].dtype)
    for e, plan in enumerate(plans):
        if specs[e][6] > 1:
            continue
        for k in range(1, min(plan[1], 9)):
            desc(plan, lax.rem(plan[12] + k, plan[1]), plan[12]).wait_send()
    for _, second in seconds:
        each_peer(second, lambda j, second=second: desc(second, j, second[12]).start())
        second[8][second[12]] = second[6][...]
    for e, plan in enumerate(plans):
        if specs[e][6] > 1:
            continue

        def finish(k, carry, plan=plan):
            j = lax.rem(plan[12] + k, plan[1])
            desc(plan, j, plan[12]).wait_send()
            return carry

        lax.fori_loop(min(plan[1], 9), plan[1], finish, 0)

        def arrive(j, plan=plan):
            desc(plan, j, j).wait_recv()

        each_peer(plan, arrive)
    for _, second in seconds:

        def finish_second(j, second=second):
            desc(second, j, second[12]).wait_send()
            desc(second, j, j).wait_recv()

        each_peer(second, finish_second)
    for e, plan in enumerate(plans):
        reduce, y_ref, buf = plan[4], plan[7], plan[8]
        if specs[e][6] > 1:
            buf = dict(seconds)[e][8]
        if reduce:
            y_ref[...] = jnp.sum(buf[...].astype(jnp.float32), axis=0)
        else:
            y_ref[...] = buf[...]


def exchange_many(ident, jobs):
    specs, out_shapes, scratch, extra = [], [], [], []
    for job in jobs:
        x, axis, size, stride, bcast, reduce, lanes = job[:7]
        size2, stride2 = job[7:] if len(job) > 7 else (1, ((1, 1),))
        if bcast:
            block = x.shape
        elif lanes:
            block = (x.shape[0], lanes)
        else:
            block = x.shape[1:]
        specs.append((axis, size, stride, bcast, reduce, lanes, size2, stride2))
        if size2 > 1:
            extra += [
                pltpu.VMEM(block, x.dtype),
                pltpu.VMEM((size2,) + block, x.dtype),
                pltpu.SemaphoreType.DMA((size2,)),
                pltpu.SemaphoreType.DMA((size2,)),
            ]
        out_shapes.append(
            jax.ShapeDtypeStruct(block if reduce else (size,) + block, jnp.float32 if reduce else x.dtype)
        )
        scratch += [
            pltpu.VMEM((size,) + block, x.dtype),
            pltpu.SemaphoreType.DMA((size,)),
            pltpu.SemaphoreType.DMA((size,)),
        ]
    return pl.pallas_call(
        functools.partial(exchange_kernel, tuple(specs)),
        out_shape=tuple(out_shapes),
        in_specs=[pl.BlockSpec(memory_space=pltpu.VMEM)] * len(jobs),
        out_specs=tuple(pl.BlockSpec(memory_space=pltpu.VMEM) for _ in jobs),
        scratch_shapes=scratch + extra,
        compiler_params=pltpu.CompilerParams(collective_id=ident, has_side_effects=True),
    )(*[job[0] for job in jobs])


def exchange(x, ident, axis, size, stride=None, bcast=False, reduce=False, lanes=0):
    stride = ((size, 1),) if stride is None else stride
    return exchange_many(ident, [(x, axis, size, stride, bcast, reduce, lanes)])[0]


def per_device(
    features,
    cached_embed,
    staleness,
    node_counts,
    neighbours,
    degrees,
    w_self,
    w_nbr,
    sage_bias,
    cotangent,
):
    n_dom = lax.axis_size("dom")
    n_col = lax.axis_size("col")
    col_width = features.shape[0]
    part_rows = features.shape[1]
    slot_count = neighbours.shape[0]
    hidden = w_self.shape[1]
    my_index = lax.axis_index("dom")
    fresh_flag = (staleness >= LIMIT).astype(jnp.int32)
    my_fresh = fresh_flag[my_index]
    col_inputs = jnp.concatenate([features, w_self, w_nbr, cotangent], axis=0)
    bias_block = jnp.zeros((8, 128), jnp.float32).at[0, : sage_bias.shape[0]].set(sage_bias)
    blocks = exchange(features, 0, "dom", n_dom, bcast=True)
    sources = jnp.where(
        fresh_flag[None, :, None] == 1,
        blocks.transpose(1, 0, 2),
        cached_embed.reshape(col_width, n_dom, part_rows),
    ).reshape(col_width, n_dom * part_rows)
    local_slot = jnp.arange(part_rows, dtype=jnp.int32)
    live_rows = (local_slot < node_counts[my_index]).astype(jnp.float32)
    slot_index = jnp.arange(slot_count, dtype=jnp.int32)
    used = (slot_index[:, None] < degrees[None, :]).astype(jnp.float32)
    weights = used * (live_rows / degrees.astype(jnp.float32))[None, :]
    gathered = sources[:, neighbours].astype(jnp.float32)
    aggregated = jnp.sum(weights[None, :, :] * gathered, axis=1).astype(jnp.bfloat16)
    col_blocks, bias_blocks = exchange_many(
        1,
        [
            (jnp.concatenate([aggregated, col_inputs], axis=0), "col", n_col, ((n_col, 1),), True, False, 0),
            (bias_block, "col", n_col, ((n_col, 1),), True, False, 0),
        ],
    )
    agg_full = col_blocks[:, :col_width].reshape(n_col * col_width, part_rows)
    col_blocks = col_blocks[:, col_width:]
    feat_full = col_blocks[:, :col_width].reshape(n_col * col_width, part_rows)
    w_self_full = col_blocks[:, col_width : 2 * col_width].reshape(n_col * col_width, hidden)
    w_nbr_full = col_blocks[:, 2 * col_width : 3 * col_width].reshape(n_col * col_width, hidden)
    cot_full = col_blocks[:, 3 * col_width :].reshape(hidden, part_rows)
    bias_full = bias_blocks[:, 0, : sage_bias.shape[0]].reshape(hidden)
    pre_full = (
        left_product(w_self_full, feat_full)
        + left_product(w_nbr_full, agg_full)
        + bias_full[:, None]
    )
    sig_full = 1.0 / (1.0 + jnp.exp(-pre_full))
    my_col = lax.axis_index("col")
    block_rows = hidden // n_col
    pre_act = lax.dynamic_slice_in_dim(pre_full, my_col * block_rows, block_rows, 0)
    sigmoid = lax.dynamic_slice_in_dim(sig_full, my_col * block_rows, block_rows, 0)
    activation = (live_rows[None, :] * pre_act * sigmoid).astype(jnp.bfloat16)
    grad_full = (
        live_rows[None, :]
        * cot_full.astype(jnp.float32)
        * sig_full
        * (1.0 + pre_full * (1.0 - sig_full))
    ).astype(jnp.bfloat16)
    grad_pre = lax.dynamic_slice_in_dim(grad_full, my_col * block_rows, block_rows, 0)
    self_part = right_product(features, grad_full)
    nbr_part = right_product(aggregated, grad_full)
    bias_part = jnp.sum(grad_pre.astype(jnp.float32), axis=1)
    bias_rows = jnp.zeros((8, hidden), jnp.float32).at[0, : bias_part.shape[0]].set(bias_part)
    packed = jnp.concatenate([self_part, nbr_part, bias_rows], axis=0)
    grad_agg = jnp.dot(w_nbr, grad_full, preferred_element_type=jnp.float32).astype(jnp.bfloat16)
    own_term = jnp.dot(w_self, grad_full, preferred_element_type=jnp.float32)
    spread = weights[None, :, :] * grad_agg.astype(jnp.float32)[:, None, :]
    fresh_rank = jnp.cumsum(fresh_flag) - 1
    slot_base = jnp.where(fresh_flag == 1, fresh_rank * part_rows, -part_rows)
    owner = (neighbours // part_rows)[:, :, None] == jnp.arange(n_dom, dtype=jnp.int32)
    compact = jnp.sum(jnp.where(owner, slot_base, 0), axis=2) + neighbours % part_rows
    compact = jnp.where(compact >= 0, compact, FRESH * part_rows)
    contrib = (
        jnp.zeros((col_width, FRESH * part_rows), jnp.float32)
        .at[:, compact.reshape(-1)]
        .add(spread.reshape(col_width, -1), mode="drop")
    )
    compact_blocks = contrib.reshape(col_width, FRESH, part_rows)
    block_of = jnp.clip(fresh_rank, 0, FRESH - 1)
    contrib = jnp.take(compact_blocks, block_of, axis=1, mode="clip").astype(jnp.bfloat16)
    contrib = contrib.reshape(col_width, n_dom * part_rows)
    ys = 8 if n_dom % 16 == 0 else 1
    first = ((2, 1), (n_dom // (2 * ys), 2 * ys))
    back, summed = exchange_many(
        5,
        [
            (contrib, "dom", n_dom, ((n_dom, 1),), False, True, part_rows),
            (packed.astype(jnp.bfloat16), "dom", n_dom // ys, first, True, True, 0, ys, ((ys, 2),)),
        ],
    )
    grad_self = summed[:col_width]
    grad_nbr = summed[col_width : 2 * col_width]
    grad_bias = summed[2 * col_width, : bias_part.shape[0]]
    grad_feat = (own_term + my_fresh.astype(jnp.float32) * back).astype(jnp.bfloat16)
    return (activation, grad_feat, grad_self, grad_nbr, grad_bias)


def solution(mesh):
    placed = (
        P("col", "dom"),
        P("col", None),
        P(),
        P(),
        P(None, "dom"),
        P("dom"),
        P("col", None),
        P("col", None),
        P("col"),
        P("col", "dom"),
    )
    return jax.shard_map(
        per_device,
        mesh=mesh,
        in_specs=placed,
        out_specs=(P("col", "dom"), P("col", "dom"), P("col", None), P("col", None), P("col")),
        check_vma=False,
    )
```

```python
import functools

import jax
import jax.numpy as jnp
from jax import lax
from jax.experimental import pallas as pl
from jax.experimental.pallas import tpu as pltpu
from jax.sharding import PartitionSpec as P

LIMIT = 8
FRESH = 16
MESH = pl.DeviceIdType.MESH


def left_product(weight, data):
    return lax.dot_general(
        weight, data, (((0,), (0,)), ((), ())), preferred_element_type=jnp.float32
    )


def right_product(data, grads):
    return lax.dot_general(
        data, grads, (((1,), (1,)), ((), ())), preferred_element_type=jnp.float32
    )


def group_pos(me, digits):
    pos, scale = 0, 1
    for radix, stride in digits:
        pos = pos + lax.rem(me // stride, radix) * scale
        scale *= radix
    return pos


def group_member(me, pos, j, digits):
    for radix, stride in digits:
        me = me + (lax.rem(j, radix) - lax.rem(pos, radix)) * stride
        j, pos = j // radix, pos // radix
    return me


def exchange_kernel(specs, *refs):
    count = len(specs)
    xs, ys = refs[:count], refs[count : 2 * count]
    scratch = refs[2 * count :]
    barrier = pltpu.get_barrier_semaphore()
    plans = []
    extra = scratch[3 * count :]
    for e, (axis, size, stride, bcast, reduce, lanes, _, _) in enumerate(specs):
        x_ref, y_ref = xs[e], ys[e]
        buf, send_sem, recv_sem = scratch[3 * e : 3 * e + 3]
        me = lax.axis_index(axis)
        pos = group_pos(me, stride)
        plans.append((axis, size, stride, bcast, reduce, lanes, x_ref, y_ref, buf, send_sem, recv_sem, me, pos))

    def member(plan, j):
        stride, me, pos = plan[2], plan[11], plan[12]
        return group_member(me, pos, j, stride)

    def chunk(plan, j):
        bcast, lanes, x_ref = plan[3], plan[5], plan[6]
        if bcast:
            return x_ref
        if lanes:
            return x_ref.at[:, pl.ds(pl.multiple_of(j * lanes, lanes), lanes)]
        return x_ref.at[j]

    def desc(plan, j, slot):
        axis, buf, send_sem, recv_sem = plan[0], plan[8], plan[9], plan[10]
        return pltpu.make_async_remote_copy(
            src_ref=chunk(plan, j),
            dst_ref=buf.at[slot],
            send_sem=send_sem.at[j],
            recv_sem=recv_sem.at[slot],
            device_id={axis: member(plan, j)},
            device_id_type=MESH,
        )

    def each_peer(plan, body):
        size, pos = plan[1], plan[12]

        def step(k, carry):
            body(lax.rem(pos + k, size))
            return carry

        lax.fori_loop(1, size, step, 0)

    seconds = []
    for e, spec in enumerate(specs):
        if spec[6] > 1:
            stage, buf2, send2, recv2 = extra[4 * len(seconds) : 4 * len(seconds) + 4]
            me = plans[e][11]
            second = (spec[0], spec[6], spec[7], True, True, 0, stage, None, buf2, send2, recv2, me,
                      group_pos(me, spec[7]))
            seconds.append((e, second))
    greetings = 0
    for plan in plans + [second for _, second in seconds]:
        each_peer(
            plan,
            lambda j, plan=plan: pl.semaphore_signal(
                barrier, 1, device_id={plan[0]: member(plan, j)}, device_id_type=MESH
            ),
        )
        greetings += plan[1] - 1
    pl.semaphore_wait(barrier, greetings)
    for plan in plans:
        each_peer(plan, lambda j, plan=plan: desc(plan, j, plan[12]).start())
    for plan in plans:
        buf, pos = plan[8], plan[12]
        buf[pos] = chunk(plan, pos)[...]
    for e, second in seconds:
        plan = plans[e]

        def finish_first(j, plan=plan):
            desc(plan, j, plan[12]).wait_send()
            desc(plan, j, j).wait_recv()

        each_peer(plan, finish_first)
        second[6][...] = jnp.sum(plan[8][...].astype(jnp.float32), axis=0).astype(second[6].dtype)
    for e, plan in enumerate(plans):
        if specs[e][6] > 1:
            continue
        for k in range(1, min(plan[1], 9)):
            desc(plan, lax.rem(plan[12] + k, plan[1]), plan[12]).wait_send()
    for _, second in seconds:
        each_peer(second, lambda j, second=second: desc(second, j, second[12]).start())
        second[8][second[12]] = second[6][...]
    for e, plan in enumerate(plans):
        if specs[e][6] > 1:
            continue

        def finish(k, carry, plan=plan):
            j = lax.rem(plan[12] + k, plan[1])
            desc(plan, j, plan[12]).wait_send()
            return carry

        lax.fori_loop(min(plan[1], 9), plan[1], finish, 0)

        def arrive(j, plan=plan):
            desc(plan, j, j).wait_recv()

        each_peer(plan, arrive)
    for _, second in seconds:

        def finish_second(j, second=second):
            desc(second, j, second[12]).wait_send()
            desc(second, j, j).wait_recv()

        each_peer(second, finish_second)
    for e, plan in enumerate(plans):
        reduce, y_ref, buf = plan[4], plan[7], plan[8]
        if specs[e][6] > 1:
            buf = dict(seconds)[e][8]
        if reduce:
            y_ref[...] = jnp.sum(buf[...].astype(jnp.float32), axis=0)
        else:
            y_ref[...] = buf[...]


def exchange_many(ident, jobs):
    specs, out_shapes, scratch, extra = [], [], [], []
    for job in jobs:
        x, axis, size, stride, bcast, reduce, lanes = job[:7]
        size2, stride2 = job[7:] if len(job) > 7 else (1, ((1, 1),))
        if bcast:
            block = x.shape
        elif lanes:
            block = (x.shape[0], lanes)
        else:
            block = x.shape[1:]
        specs.append((axis, size, stride, bcast, reduce, lanes, size2, stride2))
        if size2 > 1:
            extra += [
                pltpu.VMEM(block, x.dtype),
                pltpu.VMEM((size2,) + block, x.dtype),
                pltpu.SemaphoreType.DMA((size2,)),
                pltpu.SemaphoreType.DMA((size2,)),
            ]
        out_shapes.append(
            jax.ShapeDtypeStruct(block if reduce else (size,) + block, jnp.float32 if reduce else x.dtype)
        )
        scratch += [
            pltpu.VMEM((size,) + block, x.dtype),
            pltpu.SemaphoreType.DMA((size,)),
            pltpu.SemaphoreType.DMA((size,)),
        ]
    return pl.pallas_call(
        functools.partial(exchange_kernel, tuple(specs)),
        out_shape=tuple(out_shapes),
        in_specs=[pl.BlockSpec(memory_space=pltpu.VMEM)] * len(jobs),
        out_specs=tuple(pl.BlockSpec(memory_space=pltpu.VMEM) for _ in jobs),
        scratch_shapes=scratch + extra,
        compiler_params=pltpu.CompilerParams(collective_id=ident, has_side_effects=True),
    )(*[job[0] for job in jobs])


def exchange(x, ident, axis, size, stride=None, bcast=False, reduce=False, lanes=0):
    stride = ((size, 1),) if stride is None else stride
    return exchange_many(ident, [(x, axis, size, stride, bcast, reduce, lanes)])[0]


def per_device(
    features,
    cached_embed,
    staleness,
    node_counts,
    neighbours,
    degrees,
    w_self,
    w_nbr,
    sage_bias,
    cotangent,
):
    n_dom = lax.axis_size("dom")
    n_col = lax.axis_size("col")
    col_width = features.shape[0]
    part_rows = features.shape[1]
    slot_count = neighbours.shape[0]
    hidden = w_self.shape[1]
    my_index = lax.axis_index("dom")
    fresh_flag = (staleness >= LIMIT).astype(jnp.int32)
    my_fresh = jnp.sum(jnp.where(jnp.arange(n_dom) == my_index, fresh_flag, 0))
    col_inputs = jnp.concatenate([features, w_self, w_nbr, cotangent], axis=0)
    bias_block = jnp.zeros((8, 128), jnp.float32).at[0, : sage_bias.shape[0]].set(sage_bias)
    blocks = exchange(features, 0, "dom", n_dom, bcast=True)
    sources = jnp.where(
        fresh_flag[None, :, None] == 1,
        blocks.transpose(1, 0, 2),
        cached_embed.reshape(col_width, n_dom, part_rows),
    ).reshape(col_width, n_dom * part_rows)
    local_slot = jnp.arange(part_rows, dtype=jnp.int32)
    live_rows = (local_slot < node_counts[my_index]).astype(jnp.float32)
    slot_index = jnp.arange(slot_count, dtype=jnp.int32)
    used = (slot_index[:, None] < degrees[None, :]).astype(jnp.float32)
    weights = used * (live_rows / degrees.astype(jnp.float32))[None, :]
    gathered = sources[:, neighbours].astype(jnp.float32)
    aggregated = jnp.sum(weights[None, :, :] * gathered, axis=1).astype(jnp.bfloat16)
    col_blocks, bias_blocks = exchange_many(
        1,
        [
            (jnp.concatenate([aggregated, col_inputs], axis=0), "col", n_col, ((n_col, 1),), True, False, 0),
            (bias_block, "col", n_col, ((n_col, 1),), True, False, 0),
        ],
    )
    agg_full = col_blocks[:, :col_width].reshape(n_col * col_width, part_rows)
    col_blocks = col_blocks[:, col_width:]
    feat_full = col_blocks[:, :col_width].reshape(n_col * col_width, part_rows)
    w_self_full = col_blocks[:, col_width : 2 * col_width].reshape(n_col * col_width, hidden)
    w_nbr_full = col_blocks[:, 2 * col_width : 3 * col_width].reshape(n_col * col_width, hidden)
    cot_full = col_blocks[:, 3 * col_width :].reshape(hidden, part_rows)
    bias_full = bias_blocks[:, 0, : sage_bias.shape[0]].reshape(hidden)
    pre_full = (
        left_product(w_self_full, feat_full)
        + left_product(w_nbr_full, agg_full)
        + bias_full[:, None]
    )
    sig_full = 1.0 / (1.0 + jnp.exp(-pre_full))
    my_col = lax.axis_index("col")
    block_rows = hidden // n_col
    pre_act = lax.dynamic_slice_in_dim(pre_full, my_col * block_rows, block_rows, 0)
    sigmoid = lax.dynamic_slice_in_dim(sig_full, my_col * block_rows, block_rows, 0)
    activation = (live_rows[None, :] * pre_act * sigmoid).astype(jnp.bfloat16)
    grad_full = (
        live_rows[None, :]
        * cot_full.astype(jnp.float32)
        * sig_full
        * (1.0 + pre_full * (1.0 - sig_full))
    ).astype(jnp.bfloat16)
    grad_pre = lax.dynamic_slice_in_dim(grad_full, my_col * block_rows, block_rows, 0)
    self_part = right_product(features, grad_full)
    nbr_part = right_product(aggregated, grad_full)
    bias_part = jnp.sum(grad_pre.astype(jnp.float32), axis=1)
    bias_rows = jnp.zeros((8, hidden), jnp.float32).at[0, : bias_part.shape[0]].set(bias_part)
    packed = jnp.concatenate([self_part, nbr_part, bias_rows], axis=0)
    grad_agg = jnp.dot(w_nbr, grad_full, preferred_element_type=jnp.float32).astype(jnp.bfloat16)
    own_term = jnp.dot(w_self, grad_full, preferred_element_type=jnp.float32)
    spread = weights[None, :, :] * grad_agg.astype(jnp.float32)[:, None, :]
    fresh_rank = jnp.cumsum(fresh_flag) - 1
    slot_base = jnp.where(fresh_flag == 1, fresh_rank * part_rows, -part_rows)
    owner = (neighbours // part_rows)[:, :, None] == jnp.arange(n_dom, dtype=jnp.int32)
    compact = jnp.sum(jnp.where(owner, slot_base, 0), axis=2) + neighbours % part_rows
    compact = jnp.where(compact >= 0, compact, FRESH * part_rows)
    contrib = (
        jnp.zeros((col_width, FRESH * part_rows), jnp.float32)
        .at[:, compact.reshape(-1)]
        .add(spread.reshape(col_width, -1), mode="drop")
    )
    compact_blocks = contrib.astype(jnp.bfloat16).reshape(col_width, FRESH, part_rows)
    block_of = jnp.clip(fresh_rank, 0, FRESH - 1)
    contrib = jnp.take(compact_blocks, block_of, axis=1, mode="clip").reshape(col_width, n_dom * part_rows)
    ys = 8 if n_dom % 16 == 0 else 1
    first = ((2, 1), (n_dom // (2 * ys), 2 * ys))
    back, summed = exchange_many(
        5,
        [
            (contrib, "dom", n_dom, ((n_dom, 1),), False, True, part_rows),
            (packed.astype(jnp.bfloat16), "dom", n_dom // ys, first, True, True, 0, ys, ((ys, 2),)),
        ],
    )
    grad_self = summed[:col_width]
    grad_nbr = summed[col_width : 2 * col_width]
    grad_bias = summed[2 * col_width, : bias_part.shape[0]]
    grad_feat = (own_term + my_fresh.astype(jnp.float32) * back).astype(jnp.bfloat16)
    return (activation, grad_feat, grad_self, grad_nbr, grad_bias)


def solution(mesh):
    placed = (
        P("col", "dom"),
        P("col", None),
        P(),
        P(),
        P(None, "dom"),
        P("dom"),
        P("col", None),
        P("col", None),
        P("col"),
        P("col", "dom"),
    )
    return jax.shard_map(
        per_device,
        mesh=mesh,
        in_specs=placed,
        out_specs=(P("col", "dom"), P("col", "dom"), P("col", None), P("col", None), P("col")),
        check_vma=False,
    )
```

```python
import functools

import jax
import jax.numpy as jnp
from jax import lax
from jax.experimental import pallas as pl
from jax.experimental.pallas import tpu as pltpu
from jax.sharding import PartitionSpec as P

LIMIT = 8
FRESH = 16
MESH = pl.DeviceIdType.MESH


def left_product(weight, data):
    return lax.dot_general(
        weight, data, (((0,), (0,)), ((), ())), preferred_element_type=jnp.float32
    )


def right_product(data, grads):
    return lax.dot_general(
        data, grads, (((1,), (1,)), ((), ())), preferred_element_type=jnp.float32
    )


def group_pos(me, digits):
    pos, scale = 0, 1
    for radix, stride in digits:
        pos = pos + lax.rem(me // stride, radix) * scale
        scale *= radix
    return pos


def group_member(me, pos, j, digits):
    for radix, stride in digits:
        me = me + (lax.rem(j, radix) - lax.rem(pos, radix)) * stride
        j, pos = j // radix, pos // radix
    return me


def exchange_kernel(specs, *refs):
    count = len(specs)
    xs, ys = refs[:count], refs[count : 2 * count]
    scratch = refs[2 * count :]
    barrier = pltpu.get_barrier_semaphore()
    plans = []
    extra = scratch[3 * count :]
    for e, (axis, size, stride, bcast, reduce, lanes, _, _) in enumerate(specs):
        x_ref, y_ref = xs[e], ys[e]
        buf, send_sem, recv_sem = scratch[3 * e : 3 * e + 3]
        me = lax.axis_index(axis)
        pos = group_pos(me, stride)
        plans.append((axis, size, stride, bcast, reduce, lanes, x_ref, y_ref, buf, send_sem, recv_sem, me, pos))

    def member(plan, j):
        stride, me, pos = plan[2], plan[11], plan[12]
        return group_member(me, pos, j, stride)

    def chunk(plan, j):
        bcast, lanes, x_ref = plan[3], plan[5], plan[6]
        if bcast:
            return x_ref
        if lanes:
            return x_ref.at[:, pl.ds(pl.multiple_of(j * lanes, lanes), lanes)]
        return x_ref.at[j]

    def desc(plan, j, slot):
        axis, buf, send_sem, recv_sem = plan[0], plan[8], plan[9], plan[10]
        return pltpu.make_async_remote_copy(
            src_ref=chunk(plan, j),
            dst_ref=buf.at[slot],
            send_sem=send_sem.at[j],
            recv_sem=recv_sem.at[slot],
            device_id={axis: member(plan, j)},
            device_id_type=MESH,
        )

    def each_peer(plan, body):
        size, pos = plan[1], plan[12]

        def step(k, carry):
            body(lax.rem(pos + k, size))
            return carry

        lax.fori_loop(1, size, step, 0)

    seconds = []
    for e, spec in enumerate(specs):
        if spec[6] > 1:
            stage, buf2, send2, recv2 = extra[4 * len(seconds) : 4 * len(seconds) + 4]
            me = plans[e][11]
            second = (spec[0], spec[6], spec[7], True, True, 0, stage, None, buf2, send2, recv2, me,
                      group_pos(me, spec[7]))
            seconds.append((e, second))
    greetings = 0
    for plan in plans + [second for _, second in seconds]:
        each_peer(
            plan,
            lambda j, plan=plan: pl.semaphore_signal(
                barrier, 1, device_id={plan[0]: member(plan, j)}, device_id_type=MESH
            ),
        )
        greetings += plan[1] - 1
    pl.semaphore_wait(barrier, greetings)
    for plan in plans:
        each_peer(plan, lambda j, plan=plan: desc(plan, j, plan[12]).start())
    for plan in plans:
        buf, pos = plan[8], plan[12]
        buf[pos] = chunk(plan, pos)[...]
    for e, second in seconds:
        plan = plans[e]

        def finish_first(j, plan=plan):
            desc(plan, j, plan[12]).wait_send()
            desc(plan, j, j).wait_recv()

        each_peer(plan, finish_first)
        second[6][...] = jnp.sum(plan[8][...].astype(jnp.float32), axis=0).astype(second[6].dtype)
    for e, plan in enumerate(plans):
        if specs[e][6] > 1:
            continue
        for k in range(1, min(plan[1], 9)):
            desc(plan, lax.rem(plan[12] + k, plan[1]), plan[12]).wait_send()
    for _, second in seconds:
        each_peer(second, lambda j, second=second: desc(second, j, second[12]).start())
        second[8][second[12]] = second[6][...]
    for e, plan in enumerate(plans):
        if specs[e][6] > 1:
            continue

        def finish(k, carry, plan=plan):
            j = lax.rem(plan[12] + k, plan[1])
            desc(plan, j, plan[12]).wait_send()
            return carry

        lax.fori_loop(min(plan[1], 9), plan[1], finish, 0)
        if plan[4]:
            def gather_sum(k, total, plan=plan):
                j = lax.rem(plan[12] + k, plan[1])
                desc(plan, j, j).wait_recv()
                return total + plan[8][j].astype(jnp.float32)

            plan[7][...] = lax.fori_loop(
                1, plan[1], gather_sum, plan[8][plan[12]].astype(jnp.float32)
            )
            continue

        def arrive(j, plan=plan):
            desc(plan, j, j).wait_recv()

        each_peer(plan, arrive)
    for _, second in seconds:

        def finish_second(j, second=second):
            desc(second, j, second[12]).wait_send()
            desc(second, j, j).wait_recv()

        each_peer(second, finish_second)
    for e, plan in enumerate(plans):
        reduce, y_ref, buf = plan[4], plan[7], plan[8]
        if specs[e][6] > 1:
            buf = dict(seconds)[e][8]
        elif reduce:
            continue
        if reduce:
            y_ref[...] = jnp.sum(buf[...].astype(jnp.float32), axis=0)
        else:
            y_ref[...] = buf[...]


def exchange_many(ident, jobs):
    specs, out_shapes, scratch, extra = [], [], [], []
    for job in jobs:
        x, axis, size, stride, bcast, reduce, lanes = job[:7]
        size2, stride2 = job[7:] if len(job) > 7 else (1, ((1, 1),))
        if bcast:
            block = x.shape
        elif lanes:
            block = (x.shape[0], lanes)
        else:
            block = x.shape[1:]
        specs.append((axis, size, stride, bcast, reduce, lanes, size2, stride2))
        if size2 > 1:
            extra += [
                pltpu.VMEM(block, x.dtype),
                pltpu.VMEM((size2,) + block, x.dtype),
                pltpu.SemaphoreType.DMA((size2,)),
                pltpu.SemaphoreType.DMA((size2,)),
            ]
        out_shapes.append(
            jax.ShapeDtypeStruct(block if reduce else (size,) + block, jnp.float32 if reduce else x.dtype)
        )
        scratch += [
            pltpu.VMEM((size,) + block, x.dtype),
            pltpu.SemaphoreType.DMA((size,)),
            pltpu.SemaphoreType.DMA((size,)),
        ]
    return pl.pallas_call(
        functools.partial(exchange_kernel, tuple(specs)),
        out_shape=tuple(out_shapes),
        in_specs=[pl.BlockSpec(memory_space=pltpu.VMEM)] * len(jobs),
        out_specs=tuple(pl.BlockSpec(memory_space=pltpu.VMEM) for _ in jobs),
        scratch_shapes=scratch + extra,
        compiler_params=pltpu.CompilerParams(collective_id=ident, has_side_effects=True),
    )(*[job[0] for job in jobs])


def exchange(x, ident, axis, size, stride=None, bcast=False, reduce=False, lanes=0):
    stride = ((size, 1),) if stride is None else stride
    return exchange_many(ident, [(x, axis, size, stride, bcast, reduce, lanes)])[0]


def per_device(
    features,
    cached_embed,
    staleness,
    node_counts,
    neighbours,
    degrees,
    w_self,
    w_nbr,
    sage_bias,
    cotangent,
):
    n_dom = lax.axis_size("dom")
    n_col = lax.axis_size("col")
    col_width = features.shape[0]
    part_rows = features.shape[1]
    slot_count = neighbours.shape[0]
    hidden = w_self.shape[1]
    my_index = lax.axis_index("dom")
    fresh_flag = (staleness >= LIMIT).astype(jnp.int32)
    my_fresh = fresh_flag[my_index]
    col_inputs = jnp.concatenate([features, w_self, w_nbr, cotangent], axis=0)
    bias_block = jnp.zeros((8, 128), jnp.float32).at[0, : sage_bias.shape[0]].set(sage_bias)
    blocks = exchange(features, 0, "dom", n_dom, bcast=True)
    sources = jnp.where(
        fresh_flag[None, :, None] == 1,
        blocks.transpose(1, 0, 2),
        cached_embed.reshape(col_width, n_dom, part_rows),
    ).reshape(col_width, n_dom * part_rows)
    local_slot = jnp.arange(part_rows, dtype=jnp.int32)
    live_rows = (local_slot < node_counts[my_index]).astype(jnp.float32)
    slot_index = jnp.arange(slot_count, dtype=jnp.int32)
    used = (slot_index[:, None] < degrees[None, :]).astype(jnp.float32)
    weights = used * (live_rows / degrees.astype(jnp.float32))[None, :]
    gathered = sources[:, neighbours].astype(jnp.float32)
    aggregated = jnp.sum(weights[None, :, :] * gathered, axis=1).astype(jnp.bfloat16)
    col_blocks, bias_blocks = exchange_many(
        1,
        [
            (jnp.concatenate([aggregated, col_inputs], axis=0), "col", n_col, ((n_col, 1),), True, False, 0),
            (bias_block, "col", n_col, ((n_col, 1),), True, False, 0),
        ],
    )
    agg_full = col_blocks[:, :col_width].reshape(n_col * col_width, part_rows)
    col_blocks = col_blocks[:, col_width:]
    feat_full = col_blocks[:, :col_width].reshape(n_col * col_width, part_rows)
    w_self_full = col_blocks[:, col_width : 2 * col_width].reshape(n_col * col_width, hidden)
    w_nbr_full = col_blocks[:, 2 * col_width : 3 * col_width].reshape(n_col * col_width, hidden)
    cot_full = col_blocks[:, 3 * col_width :].reshape(hidden, part_rows)
    bias_full = bias_blocks[:, 0, : sage_bias.shape[0]].reshape(hidden)
    pre_full = (
        left_product(w_self_full, feat_full)
        + left_product(w_nbr_full, agg_full)
        + bias_full[:, None]
    )
    sig_full = 1.0 / (1.0 + jnp.exp(-pre_full))
    my_col = lax.axis_index("col")
    block_rows = hidden // n_col
    pre_act = lax.dynamic_slice_in_dim(pre_full, my_col * block_rows, block_rows, 0)
    sigmoid = lax.dynamic_slice_in_dim(sig_full, my_col * block_rows, block_rows, 0)
    activation = (live_rows[None, :] * pre_act * sigmoid).astype(jnp.bfloat16)
    grad_full = (
        live_rows[None, :]
        * cot_full.astype(jnp.float32)
        * sig_full
        * (1.0 + pre_full * (1.0 - sig_full))
    ).astype(jnp.bfloat16)
    grad_pre = lax.dynamic_slice_in_dim(grad_full, my_col * block_rows, block_rows, 0)
    self_part = right_product(features, grad_full)
    nbr_part = right_product(aggregated, grad_full)
    bias_part = jnp.sum(grad_pre.astype(jnp.float32), axis=1)
    bias_rows = jnp.zeros((8, hidden), jnp.float32).at[0, : bias_part.shape[0]].set(bias_part)
    packed = jnp.concatenate([self_part, nbr_part, bias_rows], axis=0)
    grad_agg = jnp.dot(w_nbr, grad_full, preferred_element_type=jnp.float32).astype(jnp.bfloat16)
    own_term = jnp.dot(w_self, grad_full, preferred_element_type=jnp.float32)
    spread = weights[None, :, :] * grad_agg.astype(jnp.float32)[:, None, :]
    fresh_rank = jnp.cumsum(fresh_flag) - 1
    slot_base = jnp.where(fresh_flag == 1, fresh_rank * part_rows, -part_rows)
    owner = (neighbours // part_rows)[:, :, None] == jnp.arange(n_dom, dtype=jnp.int32)
    compact = jnp.sum(jnp.where(owner, slot_base, 0), axis=2) + neighbours % part_rows
    compact = jnp.where(compact >= 0, compact, FRESH * part_rows)
    contrib = (
        jnp.zeros((col_width, FRESH * part_rows), jnp.float32)
        .at[:, compact.reshape(-1)]
        .add(spread.reshape(col_width, -1), mode="drop")
    )
    compact_blocks = contrib.astype(jnp.bfloat16).reshape(col_width, FRESH, part_rows)
    block_of = jnp.clip(fresh_rank, 0, FRESH - 1)
    contrib = jnp.take(compact_blocks, block_of, axis=1, mode="clip").reshape(col_width, n_dom * part_rows)
    ys = 8 if n_dom % 16 == 0 else 1
    first = ((2, 1), (n_dom // (2 * ys), 2 * ys))
    back, summed = exchange_many(
        5,
        [
            (contrib, "dom", n_dom, ((n_dom, 1),), False, True, part_rows),
            (packed.astype(jnp.bfloat16), "dom", n_dom // ys, first, True, True, 0, ys, ((ys, 2),)),
        ],
    )
    grad_self = summed[:col_width]
    grad_nbr = summed[col_width : 2 * col_width]
    grad_bias = summed[2 * col_width, : bias_part.shape[0]]
    grad_feat = (own_term + my_fresh.astype(jnp.float32) * back).astype(jnp.bfloat16)
    return (activation, grad_feat, grad_self, grad_nbr, grad_bias)


def solution(mesh):
    placed = (
        P("col", "dom"),
        P("col", None),
        P(),
        P(),
        P(None, "dom"),
        P("dom"),
        P("col", None),
        P("col", None),
        P("col"),
        P("col", "dom"),
    )
    return jax.shard_map(
        per_device,
        mesh=mesh,
        in_specs=placed,
        out_specs=(P("col", "dom"), P("col", "dom"), P("col", None), P("col", None), P("col")),
        check_vma=False,
    )
```

```python
import functools

import jax
import jax.numpy as jnp
from jax import lax
from jax.experimental import pallas as pl
from jax.experimental.pallas import tpu as pltpu
from jax.sharding import PartitionSpec as P

LIMIT = 8
FRESH = 16
MESH = pl.DeviceIdType.MESH


def left_product(weight, data):
    return lax.dot_general(
        weight, data, (((0,), (0,)), ((), ())), preferred_element_type=jnp.float32
    )


def right_product(data, grads):
    return lax.dot_general(
        data, grads, (((1,), (1,)), ((), ())), preferred_element_type=jnp.float32
    )


def group_pos(me, digits):
    pos, scale = 0, 1
    for radix, stride in digits:
        pos = pos + lax.rem(me // stride, radix) * scale
        scale *= radix
    return pos


def group_member(me, pos, j, digits):
    for radix, stride in digits:
        me = me + (lax.rem(j, radix) - lax.rem(pos, radix)) * stride
        j, pos = j // radix, pos // radix
    return me


def exchange_kernel(specs, *refs):
    count = len(specs)
    xs, ys = refs[:count], refs[count : 2 * count]
    scratch = refs[2 * count :]
    barrier = pltpu.get_barrier_semaphore()
    plans = []
    extra = scratch[3 * count :]
    for e, (axis, size, stride, bcast, reduce, lanes, _, _) in enumerate(specs):
        x_ref, y_ref = xs[e], ys[e]
        buf, send_sem, recv_sem = scratch[3 * e : 3 * e + 3]
        me = lax.axis_index(axis)
        pos = group_pos(me, stride)
        plans.append((axis, size, stride, bcast, reduce, lanes, x_ref, y_ref, buf, send_sem, recv_sem, me, pos))

    def member(plan, j):
        stride, me, pos = plan[2], plan[11], plan[12]
        return group_member(me, pos, j, stride)

    def chunk(plan, j):
        bcast, lanes, x_ref = plan[3], plan[5], plan[6]
        if bcast:
            return x_ref
        if lanes:
            return x_ref.at[:, pl.ds(pl.multiple_of(j * lanes, lanes), lanes)]
        return x_ref.at[j]

    def desc(plan, j, slot):
        axis, buf, send_sem, recv_sem = plan[0], plan[8], plan[9], plan[10]
        return pltpu.make_async_remote_copy(
            src_ref=chunk(plan, j),
            dst_ref=buf.at[slot],
            send_sem=send_sem.at[j],
            recv_sem=recv_sem.at[slot],
            device_id={axis: member(plan, j)},
            device_id_type=MESH,
        )

    def each_peer(plan, body):
        size, pos = plan[1], plan[12]

        def step(k, carry):
            body(lax.rem(pos + k, size))
            return carry

        lax.fori_loop(1, size, step, 0)

    seconds = []
    for e, spec in enumerate(specs):
        if spec[6] > 1:
            stage, buf2, send2, recv2 = extra[4 * len(seconds) : 4 * len(seconds) + 4]
            me = plans[e][11]
            second = (spec[0], spec[6], spec[7], True, True, 0, stage, None, buf2, send2, recv2, me,
                      group_pos(me, spec[7]))
            seconds.append((e, second))
    greetings = 0
    for plan in plans + [second for _, second in seconds]:
        each_peer(
            plan,
            lambda j, plan=plan: pl.semaphore_signal(
                barrier, 1, device_id={plan[0]: member(plan, j)}, device_id_type=MESH
            ),
        )
        greetings += plan[1] - 1
    pl.semaphore_wait(barrier, greetings)
    for plan in plans:
        each_peer(plan, lambda j, plan=plan: desc(plan, j, plan[12]).start())
    for plan in plans:
        buf, pos = plan[8], plan[12]
        buf[pos] = chunk(plan, pos)[...]
    for e, second in seconds:
        plan = plans[e]

        def finish_first(j, plan=plan):
            desc(plan, j, plan[12]).wait_send()
            desc(plan, j, j).wait_recv()

        each_peer(plan, finish_first)
        second[6][...] = jnp.sum(plan[8][...].astype(jnp.float32), axis=0).astype(second[6].dtype)
    for e, plan in enumerate(plans):
        if specs[e][6] > 1:
            continue
        for k in range(1, min(plan[1], 9)):
            desc(plan, lax.rem(plan[12] + k, plan[1]), plan[12]).wait_send()
    for _, second in seconds:
        each_peer(second, lambda j, second=second: desc(second, j, second[12]).start())
        second[8][second[12]] = second[6][...]
    for e, plan in enumerate(plans):
        if specs[e][6] > 1:
            continue

        def finish(k, carry, plan=plan):
            j = lax.rem(plan[12] + k, plan[1])
            desc(plan, j, plan[12]).wait_send()
            return carry

        lax.fori_loop(min(plan[1], 9), plan[1], finish, 0)
        if plan[4]:
            def gather_sum(k, total, plan=plan):
                j = lax.rem(plan[12] + k, plan[1])
                desc(plan, j, j).wait_recv()
                return total + plan[8][j].astype(jnp.float32)

            plan[7][...] = lax.fori_loop(
                1, plan[1], gather_sum, plan[8][plan[12]].astype(jnp.float32)
            )
            continue

        def arrive(j, plan=plan):
            desc(plan, j, j).wait_recv()

        each_peer(plan, arrive)
    for _, second in seconds:

        def finish_second(j, second=second):
            desc(second, j, second[12]).wait_send()
            desc(second, j, j).wait_recv()

        each_peer(second, finish_second)
    for e, plan in enumerate(plans):
        reduce, y_ref, buf = plan[4], plan[7], plan[8]
        if specs[e][6] > 1:
            buf = dict(seconds)[e][8]
        elif reduce:
            continue
        if reduce:
            y_ref[...] = jnp.sum(buf[...].astype(jnp.float32), axis=0)
        else:
            y_ref[...] = buf[...]


def exchange_many(ident, jobs):
    specs, out_shapes, scratch, extra = [], [], [], []
    for job in jobs:
        x, axis, size, stride, bcast, reduce, lanes = job[:7]
        size2, stride2 = job[7:] if len(job) > 7 else (1, ((1, 1),))
        if bcast:
            block = x.shape
        elif lanes:
            block = (x.shape[0], lanes)
        else:
            block = x.shape[1:]
        specs.append((axis, size, stride, bcast, reduce, lanes, size2, stride2))
        if size2 > 1:
            extra += [
                pltpu.VMEM(block, x.dtype),
                pltpu.VMEM((size2,) + block, x.dtype),
                pltpu.SemaphoreType.DMA((size2,)),
                pltpu.SemaphoreType.DMA((size2,)),
            ]
        out_shapes.append(
            jax.ShapeDtypeStruct(block if reduce else (size,) + block, jnp.float32 if reduce else x.dtype)
        )
        scratch += [
            pltpu.VMEM((size,) + block, x.dtype),
            pltpu.SemaphoreType.DMA((size,)),
            pltpu.SemaphoreType.DMA((size,)),
        ]
    return pl.pallas_call(
        functools.partial(exchange_kernel, tuple(specs)),
        out_shape=tuple(out_shapes),
        in_specs=[pl.BlockSpec(memory_space=pltpu.VMEM)] * len(jobs),
        out_specs=tuple(pl.BlockSpec(memory_space=pltpu.VMEM) for _ in jobs),
        scratch_shapes=scratch + extra,
        compiler_params=pltpu.CompilerParams(collective_id=ident, has_side_effects=True),
    )(*[job[0] for job in jobs])


def exchange(x, ident, axis, size, stride=None, bcast=False, reduce=False, lanes=0):
    stride = ((size, 1),) if stride is None else stride
    return exchange_many(ident, [(x, axis, size, stride, bcast, reduce, lanes)])[0]


def per_device(
    features,
    cached_embed,
    staleness,
    node_counts,
    neighbours,
    degrees,
    w_self,
    w_nbr,
    sage_bias,
    cotangent,
):
    n_dom = lax.axis_size("dom")
    n_col = lax.axis_size("col")
    col_width = features.shape[0]
    part_rows = features.shape[1]
    slot_count = neighbours.shape[0]
    hidden = w_self.shape[1]
    my_index = lax.axis_index("dom")
    fresh_flag = (staleness >= LIMIT).astype(jnp.int32)
    my_fresh = fresh_flag[my_index]
    col_inputs = jnp.concatenate([features, w_self, w_nbr, cotangent], axis=0)
    bias_block = sage_bias.reshape(1, -1)
    blocks = exchange(features, 0, "dom", n_dom, bcast=True)
    sources = jnp.where(
        fresh_flag[None, :, None] == 1,
        blocks.transpose(1, 0, 2),
        cached_embed.reshape(col_width, n_dom, part_rows),
    ).reshape(col_width, n_dom * part_rows)
    local_slot = jnp.arange(part_rows, dtype=jnp.int32)
    live_rows = (local_slot < node_counts[my_index]).astype(jnp.float32)
    slot_index = jnp.arange(slot_count, dtype=jnp.int32)
    used = (slot_index[:, None] < degrees[None, :]).astype(jnp.float32)
    weights = used * (live_rows / degrees.astype(jnp.float32))[None, :]
    gathered = sources[:, neighbours].astype(jnp.float32)
    aggregated = jnp.sum(weights[None, :, :] * gathered, axis=1).astype(jnp.bfloat16)
    col_blocks, bias_blocks = exchange_many(
        1,
        [
            (jnp.concatenate([aggregated, col_inputs], axis=0), "col", n_col, ((n_col, 1),), True, False, 0),
            (bias_block, "col", n_col, ((n_col, 1),), True, False, 0),
        ],
    )
    agg_full = col_blocks[:, :col_width].reshape(n_col * col_width, part_rows)
    col_blocks = col_blocks[:, col_width:]
    feat_full = col_blocks[:, :col_width].reshape(n_col * col_width, part_rows)
    w_self_full = col_blocks[:, col_width : 2 * col_width].reshape(n_col * col_width, hidden)
    w_nbr_full = col_blocks[:, 2 * col_width : 3 * col_width].reshape(n_col * col_width, hidden)
    cot_full = col_blocks[:, 3 * col_width :].reshape(hidden, part_rows)
    bias_full = bias_blocks.reshape(hidden)
    pre_full = (
        left_product(w_self_full, feat_full)
        + left_product(w_nbr_full, agg_full)
        + bias_full[:, None]
    )
    sig_full = 1.0 / (1.0 + jnp.exp(-pre_full))
    my_col = lax.axis_index("col")
    block_rows = hidden // n_col
    pre_act = lax.dynamic_slice_in_dim(pre_full, my_col * block_rows, block_rows, 0)
    sigmoid = lax.dynamic_slice_in_dim(sig_full, my_col * block_rows, block_rows, 0)
    activation = (live_rows[None, :] * pre_act * sigmoid).astype(jnp.bfloat16)
    grad_full = (
        live_rows[None, :]
        * cot_full.astype(jnp.float32)
        * sig_full
        * (1.0 + pre_full * (1.0 - sig_full))
    ).astype(jnp.bfloat16)
    grad_pre = lax.dynamic_slice_in_dim(grad_full, my_col * block_rows, block_rows, 0)
    self_part = right_product(features, grad_full)
    nbr_part = right_product(aggregated, grad_full)
    bias_part = jnp.sum(grad_pre.astype(jnp.float32), axis=1)
    bias_rows = jnp.zeros((8, hidden), jnp.float32).at[0, : bias_part.shape[0]].set(bias_part)
    packed = jnp.concatenate([self_part, nbr_part, bias_rows], axis=0)
    grad_agg = jnp.dot(w_nbr, grad_full, preferred_element_type=jnp.float32).astype(jnp.bfloat16)
    own_term = jnp.dot(w_self, grad_full, preferred_element_type=jnp.float32)
    spread = weights[None, :, :] * grad_agg.astype(jnp.float32)[:, None, :]
    fresh_rank = jnp.cumsum(fresh_flag) - 1
    slot_base = jnp.where(fresh_flag == 1, fresh_rank * part_rows, -part_rows)
    owner = (neighbours // part_rows)[:, :, None] == jnp.arange(n_dom, dtype=jnp.int32)
    compact = jnp.sum(jnp.where(owner, slot_base, 0), axis=2) + neighbours % part_rows
    compact = jnp.where(compact >= 0, compact, FRESH * part_rows)
    contrib = (
        jnp.zeros((col_width, FRESH * part_rows), jnp.float32)
        .at[:, compact.reshape(-1)]
        .add(spread.reshape(col_width, -1), mode="drop")
    )
    compact_blocks = contrib.astype(jnp.bfloat16).reshape(col_width, FRESH, part_rows)
    block_of = jnp.clip(fresh_rank, 0, FRESH - 1)
    contrib = jnp.take(compact_blocks, block_of, axis=1, mode="clip").reshape(col_width, n_dom * part_rows)
    ys = 8 if n_dom % 16 == 0 else 1
    first = ((2, 1), (n_dom // (2 * ys), 2 * ys))
    back, summed = exchange_many(
        5,
        [
            (contrib, "dom", n_dom, ((n_dom, 1),), False, True, part_rows),
            (packed.astype(jnp.bfloat16), "dom", n_dom // ys, first, True, True, 0, ys, ((ys, 2),)),
        ],
    )
    grad_self = summed[:col_width]
    grad_nbr = summed[col_width : 2 * col_width]
    grad_bias = summed[2 * col_width, : bias_part.shape[0]]
    grad_feat = (own_term + my_fresh.astype(jnp.float32) * back).astype(jnp.bfloat16)
    return (activation, grad_feat, grad_self, grad_nbr, grad_bias)


def solution(mesh):
    placed = (
        P("col", "dom"),
        P("col", None),
        P(),
        P(),
        P(None, "dom"),
        P("dom"),
        P("col", None),
        P("col", None),
        P("col"),
        P("col", "dom"),
    )
    return jax.shard_map(
        per_device,
        mesh=mesh,
        in_specs=placed,
        out_specs=(P("col", "dom"), P("col", "dom"), P("col", None), P("col", None), P("col")),
        check_vma=False,
    )
```

```python
import functools

import jax
import jax.numpy as jnp
from jax import lax
from jax.experimental import pallas as pl
from jax.experimental.pallas import tpu as pltpu
from jax.sharding import PartitionSpec as P

LIMIT = 8
FRESH = 16
MESH = pl.DeviceIdType.MESH


def left_product(weight, data):
    return lax.dot_general(
        weight, data, (((0,), (0,)), ((), ())), preferred_element_type=jnp.float32
    )


def right_product(data, grads):
    return lax.dot_general(
        data, grads, (((1,), (1,)), ((), ())), preferred_element_type=jnp.float32
    )


def group_pos(me, digits):
    pos, scale = 0, 1
    for radix, stride in digits:
        pos = pos + lax.rem(me // stride, radix) * scale
        scale *= radix
    return pos


def group_member(me, pos, j, digits):
    for radix, stride in digits:
        me = me + (lax.rem(j, radix) - lax.rem(pos, radix)) * stride
        j, pos = j // radix, pos // radix
    return me


def exchange_kernel(specs, *refs):
    count = len(specs)
    xs, ys = refs[:count], refs[count : 2 * count]
    scratch = refs[2 * count :]
    barrier = pltpu.get_barrier_semaphore()
    plans = []
    extra = scratch[3 * count :]
    for e, (axis, size, stride, bcast, reduce, lanes, _, _) in enumerate(specs):
        x_ref, y_ref = xs[e], ys[e]
        buf, send_sem, recv_sem = scratch[3 * e : 3 * e + 3]
        me = lax.axis_index(axis)
        pos = group_pos(me, stride)
        plans.append((axis, size, stride, bcast, reduce, lanes, x_ref, y_ref, buf, send_sem, recv_sem, me, pos))

    def member(plan, j):
        stride, me, pos = plan[2], plan[11], plan[12]
        return group_member(me, pos, j, stride)

    def chunk(plan, j):
        bcast, lanes, x_ref = plan[3], plan[5], plan[6]
        if bcast:
            return x_ref
        if lanes:
            return x_ref.at[:, pl.ds(pl.multiple_of(j * lanes, lanes), lanes)]
        return x_ref.at[j]

    def desc(plan, j, slot):
        axis, buf, send_sem, recv_sem = plan[0], plan[8], plan[9], plan[10]
        return pltpu.make_async_remote_copy(
            src_ref=chunk(plan, j),
            dst_ref=buf.at[slot],
            send_sem=send_sem.at[j],
            recv_sem=recv_sem.at[slot],
            device_id={axis: member(plan, j)},
            device_id_type=MESH,
        )

    def each_peer(plan, body):
        size, pos = plan[1], plan[12]

        def step(k, carry):
            body(lax.rem(pos + k, size))
            return carry

        lax.fori_loop(1, size, step, 0)

    seconds = []
    for e, spec in enumerate(specs):
        if spec[6] > 1:
            stage, buf2, send2, recv2 = extra[4 * len(seconds) : 4 * len(seconds) + 4]
            me = plans[e][11]
            second = (spec[0], spec[6], spec[7], True, True, 0, stage, None, buf2, send2, recv2, me,
                      group_pos(me, spec[7]))
            seconds.append((e, second))
    greetings = 0
    for plan in plans + [second for _, second in seconds]:
        each_peer(
            plan,
            lambda j, plan=plan: pl.semaphore_signal(
                barrier, 1, device_id={plan[0]: member(plan, j)}, device_id_type=MESH
            ),
        )
        greetings += plan[1] - 1
    pl.semaphore_wait(barrier, greetings)
    for plan in plans:
        each_peer(plan, lambda j, plan=plan: desc(plan, j, plan[12]).start())
    for plan in plans:
        buf, pos = plan[8], plan[12]
        buf[pos] = chunk(plan, pos)[...]
    for e, second in seconds:
        plan = plans[e]

        def first_sum(k, total, plan=plan):
            j = lax.rem(plan[12] + k, plan[1])
            desc(plan, j, plan[12]).wait_send()
            desc(plan, j, j).wait_recv()
            return total + plan[8][j].astype(jnp.float32)

        total = lax.fori_loop(1, plan[1], first_sum, plan[8][plan[12]].astype(jnp.float32))
        second[6][...] = total.astype(second[6].dtype)
    for e, plan in enumerate(plans):
        if specs[e][6] > 1:
            continue
        for k in range(1, min(plan[1], 9)):
            desc(plan, lax.rem(plan[12] + k, plan[1]), plan[12]).wait_send()
    for _, second in seconds:
        each_peer(second, lambda j, second=second: desc(second, j, second[12]).start())
        second[8][second[12]] = second[6][...]
    for e, plan in enumerate(plans):
        if specs[e][6] > 1:
            continue

        def finish(k, carry, plan=plan):
            j = lax.rem(plan[12] + k, plan[1])
            desc(plan, j, plan[12]).wait_send()
            return carry

        lax.fori_loop(min(plan[1], 9), plan[1], finish, 0)
        if plan[4]:
            def gather_sum(k, total, plan=plan):
                j = lax.rem(plan[12] + k, plan[1])
                desc(plan, j, j).wait_recv()
                return total + plan[8][j].astype(jnp.float32)

            plan[7][...] = lax.fori_loop(
                1, plan[1], gather_sum, plan[8][plan[12]].astype(jnp.float32)
            )
            continue

        def arrive(j, plan=plan):
            desc(plan, j, j).wait_recv()

        each_peer(plan, arrive)
    for _, second in seconds:

        def finish_second(j, second=second):
            desc(second, j, second[12]).wait_send()
            desc(second, j, j).wait_recv()

        each_peer(second, finish_second)
    for e, plan in enumerate(plans):
        reduce, y_ref, buf = plan[4], plan[7], plan[8]
        if specs[e][6] > 1:
            buf = dict(seconds)[e][8]
        elif reduce:
            continue
        if reduce:
            y_ref[...] = jnp.sum(buf[...].astype(jnp.float32), axis=0)
        else:
            y_ref[...] = buf[...]


def exchange_many(ident, jobs):
    specs, out_shapes, scratch, extra = [], [], [], []
    for job in jobs:
        x, axis, size, stride, bcast, reduce, lanes = job[:7]
        size2, stride2 = job[7:] if len(job) > 7 else (1, ((1, 1),))
        if bcast:
            block = x.shape
        elif lanes:
            block = (x.shape[0], lanes)
        else:
            block = x.shape[1:]
        specs.append((axis, size, stride, bcast, reduce, lanes, size2, stride2))
        if size2 > 1:
            extra += [
                pltpu.VMEM(block, x.dtype),
                pltpu.VMEM((size2,) + block, x.dtype),
                pltpu.SemaphoreType.DMA((size2,)),
                pltpu.SemaphoreType.DMA((size2,)),
            ]
        out_shapes.append(
            jax.ShapeDtypeStruct(block if reduce else (size,) + block, jnp.float32 if reduce else x.dtype)
        )
        scratch += [
            pltpu.VMEM((size,) + block, x.dtype),
            pltpu.SemaphoreType.DMA((size,)),
            pltpu.SemaphoreType.DMA((size,)),
        ]
    return pl.pallas_call(
        functools.partial(exchange_kernel, tuple(specs)),
        out_shape=tuple(out_shapes),
        in_specs=[pl.BlockSpec(memory_space=pltpu.VMEM)] * len(jobs),
        out_specs=tuple(pl.BlockSpec(memory_space=pltpu.VMEM) for _ in jobs),
        scratch_shapes=scratch + extra,
        compiler_params=pltpu.CompilerParams(collective_id=ident, has_side_effects=True),
    )(*[job[0] for job in jobs])


def exchange(x, ident, axis, size, stride=None, bcast=False, reduce=False, lanes=0):
    stride = ((size, 1),) if stride is None else stride
    return exchange_many(ident, [(x, axis, size, stride, bcast, reduce, lanes)])[0]


def per_device(
    features,
    cached_embed,
    staleness,
    node_counts,
    neighbours,
    degrees,
    w_self,
    w_nbr,
    sage_bias,
    cotangent,
):
    n_dom = lax.axis_size("dom")
    n_col = lax.axis_size("col")
    col_width = features.shape[0]
    part_rows = features.shape[1]
    slot_count = neighbours.shape[0]
    hidden = w_self.shape[1]
    my_index = lax.axis_index("dom")
    fresh_flag = (staleness >= LIMIT).astype(jnp.int32)
    my_fresh = fresh_flag[my_index]
    col_inputs = jnp.concatenate([features, w_self, w_nbr, cotangent], axis=0)
    bias_block = jnp.zeros((8, 128), jnp.float32).at[0, : sage_bias.shape[0]].set(sage_bias)
    blocks = exchange(features, 0, "dom", n_dom, bcast=True)
    sources = jnp.where(
        fresh_flag[None, :, None] == 1,
        blocks.transpose(1, 0, 2),
        cached_embed.reshape(col_width, n_dom, part_rows),
    ).reshape(col_width, n_dom * part_rows)
    local_slot = jnp.arange(part_rows, dtype=jnp.int32)
    live_rows = (local_slot < node_counts[my_index]).astype(jnp.float32)
    slot_index = jnp.arange(slot_count, dtype=jnp.int32)
    used = (slot_index[:, None] < degrees[None, :]).astype(jnp.float32)
    weights = used * (live_rows / degrees.astype(jnp.float32))[None, :]
    gathered = sources[:, neighbours].astype(jnp.float32)
    aggregated = jnp.sum(weights[None, :, :] * gathered, axis=1).astype(jnp.bfloat16)
    col_blocks, bias_blocks = exchange_many(
        1,
        [
            (jnp.concatenate([aggregated, col_inputs], axis=0), "col", n_col, ((n_col, 1),), True, False, 0),
            (bias_block, "col", n_col, ((n_col, 1),), True, False, 0),
        ],
    )
    agg_full = col_blocks[:, :col_width].reshape(n_col * col_width, part_rows)
    col_blocks = col_blocks[:, col_width:]
    feat_full = col_blocks[:, :col_width].reshape(n_col * col_width, part_rows)
    w_self_full = col_blocks[:, col_width : 2 * col_width].reshape(n_col * col_width, hidden)
    w_nbr_full = col_blocks[:, 2 * col_width : 3 * col_width].reshape(n_col * col_width, hidden)
    cot_full = col_blocks[:, 3 * col_width :].reshape(hidden, part_rows)
    bias_full = bias_blocks[:, 0, : sage_bias.shape[0]].reshape(hidden)
    pre_full = (
        left_product(w_self_full, feat_full)
        + left_product(w_nbr_full, agg_full)
        + bias_full[:, None]
    )
    sig_full = 1.0 / (1.0 + jnp.exp(-pre_full))
    my_col = lax.axis_index("col")
    block_rows = hidden // n_col
    pre_act = lax.dynamic_slice_in_dim(pre_full, my_col * block_rows, block_rows, 0)
    sigmoid = lax.dynamic_slice_in_dim(sig_full, my_col * block_rows, block_rows, 0)
    activation = (live_rows[None, :] * pre_act * sigmoid).astype(jnp.bfloat16)
    grad_full = (
        live_rows[None, :]
        * cot_full.astype(jnp.float32)
        * sig_full
        * (1.0 + pre_full * (1.0 - sig_full))
    ).astype(jnp.bfloat16)
    grad_pre = lax.dynamic_slice_in_dim(grad_full, my_col * block_rows, block_rows, 0)
    self_part = right_product(features, grad_full)
    nbr_part = right_product(aggregated, grad_full)
    bias_part = jnp.sum(grad_pre.astype(jnp.float32), axis=1)
    bias_rows = jnp.zeros((8, hidden), jnp.float32).at[0, : bias_part.shape[0]].set(bias_part)
    packed = jnp.concatenate([self_part, nbr_part, bias_rows], axis=0)
    grad_agg = jnp.dot(w_nbr, grad_full, preferred_element_type=jnp.float32).astype(jnp.bfloat16)
    own_term = jnp.dot(w_self, grad_full, preferred_element_type=jnp.float32)
    spread = weights[None, :, :] * grad_agg.astype(jnp.float32)[:, None, :]
    fresh_rank = jnp.cumsum(fresh_flag) - 1
    slot_base = jnp.where(fresh_flag == 1, fresh_rank * part_rows, -part_rows)
    owner = (neighbours // part_rows)[:, :, None] == jnp.arange(n_dom, dtype=jnp.int32)
    compact = jnp.sum(jnp.where(owner, slot_base, 0), axis=2) + neighbours % part_rows
    compact = jnp.where(compact >= 0, compact, FRESH * part_rows)
    contrib = (
        jnp.zeros((col_width, FRESH * part_rows), jnp.float32)
        .at[:, compact.reshape(-1)]
        .add(spread.reshape(col_width, -1), mode="drop")
    )
    compact_blocks = contrib.astype(jnp.bfloat16).reshape(col_width, FRESH, part_rows)
    block_of = jnp.clip(fresh_rank, 0, FRESH - 1)
    contrib = jnp.take(compact_blocks, block_of, axis=1, mode="clip").reshape(col_width, n_dom * part_rows)
    ys = 8 if n_dom % 16 == 0 else 1
    first = ((2, 1), (n_dom // (2 * ys), 2 * ys))
    back, summed = exchange_many(
        5,
        [
            (contrib, "dom", n_dom, ((n_dom, 1),), False, True, part_rows),
            (packed.astype(jnp.bfloat16), "dom", n_dom // ys, first, True, True, 0, ys, ((ys, 2),)),
        ],
    )
    grad_self = summed[:col_width]
    grad_nbr = summed[col_width : 2 * col_width]
    grad_bias = summed[2 * col_width, : bias_part.shape[0]]
    grad_feat = (own_term + my_fresh.astype(jnp.float32) * back).astype(jnp.bfloat16)
    return (activation, grad_feat, grad_self, grad_nbr, grad_bias)


def solution(mesh):
    placed = (
        P("col", "dom"),
        P("col", None),
        P(),
        P(),
        P(None, "dom"),
        P("dom"),
        P("col", None),
        P("col", None),
        P("col"),
        P("col", "dom"),
    )
    return jax.shard_map(
        per_device,
        mesh=mesh,
        in_specs=placed,
        out_specs=(P("col", "dom"), P("col", "dom"), P("col", None), P("col", None), P("col")),
        check_vma=False,
    )
```
